256 devices in a mesh: layer: 16 (over z_hi, x, core), sub: 16 (over y, z_lo).
Axes of the slice: x: 4, y: 4, z: 8 (z_hi: 2, z_lo: 4; z = z_hi * 4 + z_lo), core: 2. Of those that a mesh axis runs over, the one named last changes fastest.
Arguments:
- screens: float32 [16, 7, 2048, 640], P('layer', None, None, 'sub'), may hold values from -4 to 4
- new_columns: float32 [10, 16, 2048, 8], P(None, 'layer'), may hold values from -4 to 4
- col_block: int32 [10, 16], P(None, 'layer'), may hold values from 240 to 319
- shift_x: int32 [10, 16, 6], P(None, 'layer'), may hold values from -40 to 40, as said below
- shift_y: int32 [10, 16, 6], P(None, 'layer'), may hold values from -40 to 40, as said below
- valid: int32 [80, 80], P('layer', 'sub'), may hold values 0 or 1
- recon: bfloat16 [6, 2, 80, 80, 5376], P(None, None, 'layer', 'sub'), may hold values from -0.0234375 to 0.0234375
Outputs:
- slopes: float32 [10, 6, 2, 80, 80], P(None, None, None, 'layer', 'sub')
- commands: float32 [10, 5376], replicated
The draws below stay inside these ranges and needn't reach their ends.
Inputs may be any that keep to these rules, and one draw needn't show every extreme that they name: `shift_x`: column shifts reach both -40 and 40 in every draw. `shift_y`: row shifts reach both -40 and 40 in every draw.
All inputs are finite; a program needn't handle non-finite values. No bound on the sum of `valid` on one device may be relied on, other than what follows from the above.
Results may differ from the reference program's by a relative error of at most 0.0029.
Values sent between devices are 32-bit elements; how exact they have to be, the bound alone decides.
No kernel may reach another device: no remote copies, remote signals or barrier semaphores. Data moves between devices by JAX's collectives and lax.ppermute only.
A program may use at most 64 MiB of HBM per device.

```python
import math
import jax
import jax.numpy as jnp
from jax import lax

NSUBAP = 80
FFT_LEN = 16
STARS = 6
ACTS = 5376
SCR_ROWS = 2048
TURNS = 7
STEPS = 10
HALO = 40
NEW_COLS = 8
LAYERS = 16
PUP = 640
PUP_TURN = 3
ROW0 = 704


def draw_shift_x(key, part):
    values = jax.random.randint(key, (STEPS, LAYERS, STARS), -HALO, HALO + 1)
    values = values.at[0, 0, 0].set(HALO)
    return values.at[0, 0, 1].set(-HALO)


def draw_shift_y(key, part):
    values = jax.random.randint(jax.random.fold_in(key, 7), (STEPS, LAYERS, STARS), -HALO, HALO + 1)
    values = values.at[0, 1, 2].set(HALO)
    return values.at[0, 1, 3].set(-HALO)


def plant(values, key, least, high):
    longest = values.shape.index(max(values.shape))
    spots = []
    for shift in (0, 1):
        where = [jax.random.randint(jax.random.fold_in(key, axis), (), 0, length) for axis, length in enumerate(values.shape)]
        where[longest] = (where[longest] + shift) % values.shape[longest]
        spots.append(tuple(where))
    return values.at[spots[0]].set(least).at[spots[1]].set(high)


def shard_levels(key, shape, cuts, least, high):
    def one(position, blocks):
        draws = jax.random.uniform(jax.random.fold_in(jax.random.fold_in(key, 6), position), (blocks,), jnp.float32, least / len(cuts), high / len(cuts))
        return jnp.repeat(jnp.exp(draws), shape[position] // blocks).reshape((-1,) + (1,) * (len(shape) - position - 1))

    level = one(*cuts[0])
    for cut in cuts[1:]:
        level = level * one(*cut)
    return level


def gaussian(stream_key, shape, spread, bound, shards=(), kind=jnp.bfloat16):
    gain = shard_levels(stream_key, shape, shards, -0.22, 0.18) if shards else 1.0
    values = jax.random.normal(stream_key, shape, jnp.float32) * spread * gain
    return jnp.minimum(jnp.maximum(values, -bound), bound).astype(kind)


def setup_inputs(seed: int = 0) -> dict:
    seeds = jax.random.split(jax.random.key(seed), 8)
    screens = gaussian(seeds[0], (LAYERS, TURNS, SCR_ROWS, PUP), 0.3, 4.0, ((0, 16), (3, 16)), jnp.float32)
    new_columns = gaussian(seeds[1], (STEPS, LAYERS, SCR_ROWS, NEW_COLS), 0.3, 4.0, ((1, 16),), jnp.float32)
    col_block = plant(jax.random.randint(seeds[2], (STEPS, LAYERS), PUP_TURN * PUP // NEW_COLS, (PUP_TURN + 1) * PUP // NEW_COLS), jax.random.fold_in(seeds[2], 1), PUP_TURN * PUP // NEW_COLS, ((PUP_TURN + 1) * PUP // NEW_COLS) - 1).astype(jnp.int32)
    shift_x = draw_shift_x(jax.random.fold_in(seeds[7], 71), 0)
    shift_y = draw_shift_y(jax.random.fold_in(seeds[7], 71), 0)
    valid = plant((jax.random.randint(seeds[5], (NSUBAP, NSUBAP), 0, 4) < 3).astype(jnp.int32), jax.random.fold_in(seeds[5], 1), 0, 1)
    recon = gaussian(seeds[6], (STARS, 2, NSUBAP, NSUBAP, ACTS), (2 * STARS * NSUBAP * NSUBAP) ** -0.5, 0.0234375, ((2, 16), (3, 16)))
    return {"screens": screens, "new_columns": new_columns, "col_block": col_block, "shift_x": shift_x, "shift_y": shift_y, "valid": valid, "recon": recon}


def lenslet_slopes(phase, valid, fft_len):
    stars, rows, cols = phase.shape
    subs_r, subs_c = valid.shape
    pix = rows // subs_r
    tiles = phase.reshape(stars, subs_r, pix, subs_c, pix)
    tiles = jnp.transpose(tiles, (2, 4, 0, 1, 3)).reshape(pix, pix, stars * subs_r * subs_c)
    freq = jnp.arange(fft_len).astype(jnp.float32)
    place = jnp.arange(pix).astype(jnp.float32)
    angle = (2.0 * math.pi / fft_len) * freq[:, None] * place[None, :]
    cosine = jnp.cos(angle)
    sine = -jnp.sin(angle)
    real_part = jnp.cos(tiles)
    imag_part = jnp.sin(tiles)
    highest = lax.Precision.HIGHEST

    def along_rows(mat, field):
        return jnp.einsum('kn,nms->kms', mat, field, precision=highest)

    def along_cols(field, mat):
        return jnp.einsum('kms,qm->kqs', field, mat, precision=highest)

    first_re = along_rows(cosine, real_part) - along_rows(sine, imag_part)
    first_im = along_rows(cosine, imag_part) + along_rows(sine, real_part)
    spot_re = along_cols(first_re, cosine) - along_cols(first_im, sine)
    spot_im = along_cols(first_re, sine) + along_cols(first_im, cosine)
    power = spot_re * spot_re + spot_im * spot_im
    centred = ((jnp.arange(fft_len) + fft_len // 2) % fft_len - fft_len // 2).astype(jnp.float32)
    total = jnp.sum(power, axis=(0, 1))
    along_x = jnp.sum(power * centred[None, :, None], axis=(0, 1)) / total
    along_y = jnp.sum(power * centred[:, None, None], axis=(0, 1)) / total
    result = jnp.stack([along_x, along_y]).reshape(2, stars, subs_r, subs_c)
    return jnp.transpose(result, (1, 0, 2, 3)) * valid.astype(jnp.float32)[None, None]


def write_columns(screen, fresh, block):
    column = (block * NEW_COLS).astype(jnp.int32)
    turn = (column // PUP).astype(jnp.int32)
    within = (column % PUP).astype(jnp.int32)
    return lax.dynamic_update_slice(screen, fresh[None], (turn, jnp.int32(0), within))


def footprint(screens, step_x, step_y):
    def one_layer(screen, sx, sy):
        band = screen[PUP_TURN - 1:PUP_TURN + 2, ROW0 - HALO:ROW0 + PUP + HALO, :]
        band = jnp.transpose(band, (1, 0, 2)).reshape(PUP + 2 * HALO, 3 * PUP)
        return lax.dynamic_slice(band, ((HALO + sy).astype(jnp.int32), (PUP + sx).astype(jnp.int32)), (PUP, PUP))

    return jnp.sum(jax.vmap(one_layer)(screens, step_x, step_y), axis=0)


def reference(screens, new_columns, col_block, shift_x, shift_y, valid, recon):
    matrix = recon.reshape(-1, ACTS)

    def advance(current, inputs):
        fresh, blocks, step_x, step_y = inputs
        current = jax.vmap(write_columns)(current, fresh, blocks)
        phase = jax.vmap(lambda a, b: footprint(current, a, b), in_axes=(1, 1))(step_x, step_y)
        slopes = lax.map(lambda p: lenslet_slopes(p[None], valid, FFT_LEN)[0], phase)
        flat = slopes.astype(jnp.bfloat16).reshape(-1)
        command = jnp.dot(flat, matrix, preferred_element_type=jnp.float32)
        return current, (slopes, command)

    final, (slopes, commands) = lax.scan(advance, screens, (new_columns, col_block, shift_x, shift_y))
    return slopes, commands
```

```python
import math
import jax
import jax.numpy as jnp
import numpy as np
from jax import lax
from jax.experimental import pallas as pl
from jax.experimental.pallas import tpu as pltpu
from jax.sharding import PartitionSpec as P

ACTS = 5376
HALO = 40
NEW_COLS = 8
PUP = 640
PUP_TURN = 3
ROW0 = 704
STEPS = 10
STARS = 6
PIX = 8
LANES = 128
LANE0 = 640
KEPT = 768
FIRST = ROW0 - HALO - LANE0
WINDOW = 120
UPDATES = STEPS * NEW_COLS
META = WINDOW + UPDATES
PAYLOAD = META + 8
ROLL_AT = 64
SLAB_TILES = 3
SLAB_ROWS = 32
FLAT = 300
FLAT_PAD = 384
HIGHEST = lax.Precision.HIGHEST


def toeplitz():
    d = np.arange(PIX)[:, None] - np.arange(PIX)[None, :]
    safe = np.where(d == 0, 1, d)
    return np.where(d == 0, 0.0, -4.0 * (-1.0) ** d / np.tan(np.pi * safe / 16))


def sublane_table():
    t = toeplitz()
    x = np.arange(PIX)
    rows = [t[x, (x - d) % PIX] for d in range(1, PIX)]
    rows.append((-1.0) ** x)
    return np.repeat(np.concatenate(rows)[:, None], LANES, axis=1).astype(np.float32)


def lane_table():
    t = toeplitz()
    table = np.zeros((LANES, 3 * LANES))
    for lane in range(WINDOW):
        group, y = divmod(lane, PIX)
        for z in range(PIX):
            table[group * PIX + z, lane] = t[y, z]
        table[lane, LANES + group] = (-1.0) ** y
        table[lane, 2 * LANES + group] = 1.0 / 1024
    return table.astype(np.float32)


def order_table():
    table = np.zeros((FLAT_PAD, FLAT_PAD), np.float32)
    for s in range(2):
        for k in range(2):
            for b in range(5):
                for kk in range(3):
                    for a in range(5):
                        row = (s * 10 + k * 5 + b) * 16 + kk * 5 + a
                        table[row, (((3 * k + kk) * 5 + a) * 5 + b) * 2 + s] = 1.0
    return table


def lane_index(shape):
    return lax.broadcasted_iota(jnp.int32, shape, len(shape) - 1)


def pack_kernel(low, core, high, fresh, meta, out):
    lane = lane_index((40, LANES))

    def window(ref, rows, start):
        tile, shift = divmod(start, LANES)
        first = ref[rows, tile * LANES : (tile + 1) * LANES]
        if shift == 0:
            return first
        second = ref[rows, (tile + 1) * LANES : (tile + 2) * LANES]
        first = pltpu.roll(first, LANES - shift, 1)
        second = pltpu.roll(second, LANES - shift, 1)
        return jnp.where(lane < LANES - shift, first, second)

    whole = slice(0, 40)
    for i in range(16):
        start = FIRST + i * 40
        out[i, 0:40, :] = window(low, whole, start)
        out[i, 40:80, :] = window(core, whole, start)
        out[i, 80:120, :] = window(high, whole, start)
        out[i, 120:160, :] = window(fresh, slice(0, 40), start)
        out[i, 160:200, :] = window(fresh, slice(40, 80), start)
        out[i, 200:208, :] = meta[...]


def sincos(x):
    n = jnp.floor(x * (2.0 / math.pi) + 0.5)
    r = x - n * 1.5703125
    r = r - n * 4.8351287841796875e-4
    r = r - n * 3.13855707645416259765625e-7
    r = r - n * 6.0771005065061922e-11
    q = n.astype(jnp.int32)
    z = r * r
    s = r + r * z * (-1.6666654611e-1 + z * (8.3321608736e-3 + z * -1.9515295891e-4))
    c = 1.0 - 0.5 * z + z * z * (4.166664568298827e-2 + z * (-1.388731625493765e-3 + z * 2.443315711809948e-5))
    swap = (q & 1) == 1
    sine = jnp.where(swap, c, s)
    cosine = jnp.where(swap, s, c)
    sine = jnp.where((q & 2) == 2, -sine, sine)
    cosine = jnp.where(((q + 1) & 2) == 2, -cosine, cosine)
    return sine, cosine


def main_kernel(meta, recv, sub_tab, lane_tab, order_tab, mask, recon, out, flat_out, state, phase, groups):
    lane = lane_index((40, LANES))

    def begin(l, carry):
        state[l, 0:WINDOW, :] = recv[l, 0:WINDOW, :]
        return carry

    lax.fori_loop(0, 16, begin, 0)

    def step(t, carry):
        def layer(l, acc):
            dst = pl.multiple_of(meta[l, 6, t], NEW_COLS)
            src = pl.multiple_of(WINDOW + t * NEW_COLS, NEW_COLS)
            state[l, pl.ds(dst, NEW_COLS), :] = recv[l, pl.ds(src, NEW_COLS), :]
            return tuple(
                acc[g] + pltpu.roll(state[l, pl.ds(meta[l, g, t], 40), :], meta[l, g, ROLL_AT + t], 1)
                for g in range(STARS)
            )

        zero = jnp.zeros((40, LANES), jnp.float32)
        acc = lax.fori_loop(0, 16, layer, (zero,) * STARS)
        for k in range(2):
            one, two, three = acc[3 * k : 3 * k + 3]
            joined = jnp.where(lane < 40, one, jnp.where(lane < 80, pltpu.roll(two, 40, 1), pltpu.roll(three, 80, 1)))
            for b in range(5):
                row = pl.multiple_of(((k * 5 + b) * STEPS + t) * PIX, PIX)
                phase[pl.ds(row, PIX), :] = joined[b * PIX : (b + 1) * PIX, :]
        return carry

    lax.fori_loop(0, STEPS, step, 0)

    groups[...] = jnp.zeros_like(groups)
    size = STEPS * PIX

    def spots(kb, carry):
        sine, cosine = sincos(phase[pl.ds(pl.multiple_of(kb * size, PIX), size), :])
        both = jnp.concatenate([cosine, sine], axis=0)
        along = jnp.dot(both, lane_tab[:, : 2 * LANES], precision=HIGHEST, preferred_element_type=jnp.float32)
        s3 = sine.reshape(STEPS, PIX, LANES)
        c3 = cosine.reshape(STEPS, PIX, LANES)
        acc = jnp.zeros_like(c3)
        for d in range(1, PIX):
            acc = acc + sub_tab[(d - 1) * PIX : d * PIX, :][None] * pltpu.roll(c3, d, 1)
        sign = sub_tab[7 * PIX : 8 * PIX, :][None]
        alt_c = jnp.sum(sign * c3, axis=1)
        alt_s = jnp.sum(sign * s3, axis=1)
        num_x = 4.0 * jnp.sum(s3 * acc, axis=1) - 8.0 * (alt_c * alt_c + alt_s * alt_s)
        num_y = 4.0 * jnp.sum(s3 * along[:size, :LANES].reshape(STEPS, PIX, LANES), axis=1)
        alt = along[:, LANES:]
        alt = alt * alt
        alt = jnp.sum((alt[:size] + alt[size:]).reshape(STEPS, PIX, LANES), axis=1)
        grouper = lane_tab[:, 2 * LANES :]
        got_x = jnp.dot(num_x, grouper, precision=HIGHEST, preferred_element_type=jnp.float32)
        got_y = jnp.dot(num_y, grouper, precision=HIGHEST, preferred_element_type=jnp.float32) - alt * (8.0 / 1024)
        for s, got in ((0, got_x), (1, got_y)):
            unit = s * 10 + kb
            tile = unit // 8
            groups[tile, 0:STEPS, :] = groups[tile, 0:STEPS, :] + pltpu.roll(got, (unit % 8) * 16, 1)
        return carry

    lax.fori_loop(0, 10, spots, 0)

    flat = sum(
        jnp.dot(groups[i], order_tab[i * LANES : (i + 1) * LANES, :], precision=HIGHEST, preferred_element_type=jnp.float32)
        for i in range(3)
    )
    flat = flat * mask[...]
    flat_out[...] = flat
    rounded = flat[:, :FLAT].astype(jnp.bfloat16)
    out[...] = jnp.zeros_like(out)
    for i in range(ACTS // LANES):
        part = jnp.dot(rounded, recon[:, i * LANES : (i + 1) * LANES], preferred_element_type=jnp.float32)
        owner, place = divmod(i, SLAB_TILES)
        out[owner, place * STEPS : (place + 1) * STEPS, :] = part[:STEPS]


def vmem():
    return pl.BlockSpec(memory_space=pltpu.VMEM)


def smem():
    return pl.BlockSpec(memory_space=pltpu.SMEM)


def pack(low, core, high, fresh, meta):
    return pl.pallas_call(
        pack_kernel,
        out_shape=jax.ShapeDtypeStruct((16, PAYLOAD, LANES), jnp.float32),
        in_specs=[vmem()] * 5,
        out_specs=vmem(),
        compiler_params=pltpu.CompilerParams(vmem_limit_bytes=32 << 20),
    )(low, core, high, fresh, meta)


def slopes_and_products(meta, recv, mask, recon):
    return pl.pallas_call(
        main_kernel,
        out_shape=(
            jax.ShapeDtypeStruct((16, SLAB_ROWS, LANES), jnp.float32),
            jax.ShapeDtypeStruct((16, FLAT_PAD), jnp.float32),
        ),
        in_specs=[smem()] + [vmem()] * 6,
        out_specs=(vmem(), vmem()),
        scratch_shapes=[
            pltpu.VMEM((16, LANES, LANES), jnp.float32),
            pltpu.VMEM((100 * PIX, LANES), jnp.float32),
            pltpu.VMEM((3, 16, LANES), jnp.float32),
        ],
        compiler_params=pltpu.CompilerParams(vmem_limit_bytes=40 << 20),
    )(meta, recv, jnp.asarray(sublane_table()), jnp.asarray(lane_table()), jnp.asarray(order_table()), mask, recon)


def everywhere(slab, axis):
    return lax.all_to_all(jnp.broadcast_to(slab[None], (16,) + slab.shape), axis, 0, 0, tiled=True)


def local(screens, new_columns, col_block, shift_x, shift_y, valid, recon):
    owner = lax.axis_index("sub")
    count = lax.axis_size("sub")
    strips = jnp.transpose(screens[0], (0, 2, 1))
    fresh = jnp.transpose(new_columns[:, 0], (0, 2, 1))[:, :, LANE0 : LANE0 + KEPT].reshape(UPDATES, KEPT)

    def strip(turn):
        return lax.dynamic_slice(strips, (turn, 0, LANE0), (1, 40, KEPT))[0]

    core = strip(PUP_TURN)
    forward = [(i, (i + 1) % count) for i in range(count)]
    backward = [(target, source) for source, target in forward]
    low = lax.ppermute(strip(jnp.where(owner == count - 1, PUP_TURN - 1, PUP_TURN)), "sub", forward)
    high = lax.ppermute(strip(jnp.where(owner == 0, PUP_TURN + 1, PUP_TURN)), "sub", backward)

    start = jnp.transpose(shift_x[:, 0]) + HALO
    turn = (LANES - HALO - jnp.transpose(shift_y[:, 0])) % LANES
    block = jnp.transpose(col_block) - (PUP_TURN * PUP // NEW_COLS) - (owner * 5 - 5)
    block = jnp.where((block >= 0) & (block < WINDOW // NEW_COLS), block, WINDOW // NEW_COLS) * NEW_COLS
    meta = (
        jnp.pad(start, ((0, 2), (0, LANES - STEPS)))
        + jnp.pad(turn, ((0, 2), (ROLL_AT, LANES - ROLL_AT - STEPS)))
        + jnp.pad(block, ((6, 1), (0, LANES - STEPS)))
    ).astype(jnp.float32)

    payload = pack(low, core, high, fresh, meta)
    recv = lax.all_to_all(payload, "layer", 0, 0, tiled=True)
    numbers = recv[:, META:, :].astype(jnp.int32)

    matrix = jnp.transpose(recon, (0, 2, 3, 1, 4)).reshape(FLAT, ACTS)
    mask = jnp.broadcast_to(valid.astype(jnp.float32)[None, :, :, None], (STARS, 5, 5, 2)).reshape(1, FLAT)
    mask = jnp.pad(mask, ((0, 0), (0, FLAT_PAD - FLAT)))
    products, flat = slopes_and_products(numbers, recv, mask, matrix)

    part = jnp.sum(lax.all_to_all(products, "sub", 0, 0, tiled=True), axis=0)
    total = jnp.sum(everywhere(part, "layer"), axis=0)
    slabs = everywhere(total, "sub")[: ACTS // LANES // SLAB_TILES, : SLAB_TILES * STEPS]
    commands = jnp.transpose(slabs.reshape(ACTS // LANES, STEPS, LANES), (1, 0, 2)).reshape(STEPS, ACTS)
    slopes = jnp.transpose(flat[:STEPS, :FLAT].reshape(STEPS, STARS, 5, 5, 2), (0, 1, 4, 2, 3))
    return (slopes, commands)


def solution(mesh):
    return jax.shard_map(
        local,
        mesh=mesh,
        in_specs=(
            P("layer", None, None, "sub"),
            P(None, "layer", None, None),
            P(None, "layer"),
            P(None, "layer", None),
            P(None, "layer", None),
            P("layer", "sub"),
            P(None, None, "layer", "sub", None),
        ),
        out_specs=(P(None, None, None, "layer", "sub"), P()),
        check_vma=False,
    )
```

```python
import math
import jax
import jax.numpy as jnp
import numpy as np
from jax import lax
from jax.experimental import pallas as pl
from jax.experimental.pallas import tpu as pltpu
from jax.sharding import PartitionSpec as P

ACTS = 5376
HALO = 40
NEW_COLS = 8
PUP = 640
PUP_TURN = 3
ROW0 = 704
STEPS = 10
STARS = 6
PIX = 8
LANES = 128
LANE0 = 640
KEPT = 768
FIRST = ROW0 - HALO - LANE0
WINDOW = 120
UPDATES = STEPS * NEW_COLS
COLS = WINDOW + UPDATES
REST = 56
META = COLS + REST
PAYLOAD = META + 8
CHIPS = 8
CHIP_ROWS = 80
REST_LANES = 32
ROLL_AT = 64
HALF_TILES = 21
SLABS = 16
SLAB_USED = 14
SLAB_ROWS = 16
FLAT = 300
FLAT_PAD = 384
HIGHEST = lax.Precision.HIGHEST


def toeplitz():
    d = np.arange(PIX)[:, None] - np.arange(PIX)[None, :]
    safe = np.where(d == 0, 1, d)
    return np.where(d == 0, 0.0, -4.0 * (-1.0) ** d / np.tan(np.pi * safe / 16))


def sublane_table():
    t = toeplitz()
    x = np.arange(PIX)
    rows = [t[x, (x - d) % PIX] for d in range(1, PIX)]
    rows.append((-1.0) ** x)
    return np.repeat(np.concatenate(rows)[:, None], LANES, axis=1).astype(np.float32)


def lane_table():
    t = toeplitz()
    table = np.zeros((LANES, 3 * LANES))
    for lane in range(WINDOW):
        group, y = divmod(lane, PIX)
        for z in range(PIX):
            table[group * PIX + z, lane] = t[y, z]
        table[lane, LANES + group] = (-1.0) ** y
        table[lane, 2 * LANES + group] = 1.0 / 1024
    return table.astype(np.float32)


def order_table():
    table = np.zeros((FLAT_PAD, FLAT_PAD), np.float32)
    for s in range(2):
        for k in range(2):
            for b in range(5):
                for kk in range(3):
                    for a in range(5):
                        row = (s * 10 + k * 5 + b) * 16 + kk * 5 + a
                        table[row, (((3 * k + kk) * 5 + a) * 5 + b) * 2 + s] = 1.0
    return table


def lane_index(shape):
    return lax.broadcasted_iota(jnp.int32, shape, len(shape) - 1)


def pack_kernel(low, core, high, fresh, meta, out):
    def window(ref, first, count, start):
        tile, shift = divmod(start, LANES)
        rows = slice(first, first + count)
        left = ref[rows, tile * LANES : (tile + 1) * LANES]
        if shift == 0:
            return left
        left = pltpu.roll(left, LANES - shift, 1)
        if (tile + 2) * LANES > KEPT:
            return left
        right = pltpu.roll(ref[rows, (tile + 1) * LANES : (tile + 2) * LANES], LANES - shift, 1)
        return jnp.where(lane_index(left.shape) < LANES - shift, left, right)

    parts = ((low, 0), (core, 40), (high, 80), (fresh, 120))

    def columns(first, start):
        ref, base = [part for part in parts if part[1] <= first][-1]
        return window(ref, first - base, PIX, start)

    lane = lane_index((PIX, LANES))
    for m in range(CHIPS):
        start = FIRST + m * CHIP_ROWS
        for ref, base in parts:
            count = UPDATES if base == WINDOW else 40
            out[m, base : base + count, :] = window(ref, 0, count, start)
        for r in range(REST // PIX):
            joined = None
            for q in range(4):
                first = q * REST + r * PIX
                if first >= COLS:
                    continue
                piece = columns(first, start + LANES - q * REST_LANES)
                joined = piece if joined is None else jnp.where(lane < q * REST_LANES, joined, piece)
            out[m, COLS + r * PIX : COLS + (r + 1) * PIX, :] = joined
        out[m, META:PAYLOAD, :] = meta[...]


def sincos(x):
    n = jnp.floor(x * (2.0 / math.pi) + 0.5)
    r = x - n * 1.5703125
    r = r - n * 4.8351287841796875e-4
    r = r - n * 3.13855707645416259765625e-7
    r = r - n * 6.0771005065061922e-11
    q = n.astype(jnp.int32)
    z = r * r
    s = r + r * z * (-1.6666654611e-1 + z * (8.3321608736e-3 + z * -1.9515295891e-4))
    c = 1.0 - 0.5 * z + z * z * (4.166664568298827e-2 + z * (-1.388731625493765e-3 + z * 2.443315711809948e-5))
    swap = (q & 1) == 1
    sine = jnp.where(swap, c, s)
    cosine = jnp.where(swap, s, c)
    sine = jnp.where((q & 2) == 2, -sine, sine)
    cosine = jnp.where(((q + 1) & 2) == 2, -cosine, cosine)
    return sine, cosine


def main_kernel(
    core, mine, other, sub_tab, lane_tab, order_tab, mask, recon,
    keep, send, flat_out,
    state, phase, groups, numbers, meta, arrived,
):
    lane = lane_index((40, LANES))
    side = core[0]
    for p in range(CHIPS):
        numbers[p] = mine[p, META:, :].astype(jnp.int32)
        numbers[CHIPS + p] = other[p, META:, :].astype(jnp.int32)
    copy = pltpu.make_async_copy(numbers, meta, arrived)
    copy.start()

    cut = LANES - 40 * side
    turn = lax.rem(cut, LANES)

    def begin(p, carry):
        for base, ref in ((0, mine), (CHIPS, other)):
            for q in range(4):
                first = q * REST
                count = min(REST, COLS - first)
                left = pltpu.roll(ref[p, first : first + count, :], turn, 1)
                right = pltpu.roll(ref[p, COLS : COLS + count, :], (88 - REST_LANES * q) % LANES, 1)
                state[base + p, first : first + count, :] = jnp.where(lane_index(left.shape) < cut, left, right)
        return carry

    lax.fori_loop(0, CHIPS, begin, 0)
    copy.wait()

    def step(t, carry):
        def layer(l, acc):
            dst = pl.multiple_of(meta[l, 6, t], NEW_COLS)
            src = pl.multiple_of(WINDOW + t * NEW_COLS, NEW_COLS)
            state[l, pl.ds(dst, NEW_COLS), :] = state[l, pl.ds(src, NEW_COLS), :]
            return tuple(
                acc[g] + pltpu.roll(state[l, pl.ds(meta[l, g, t], 40), :], meta[l, g, ROLL_AT + t], 1)
                for g in range(STARS)
            )

        zero = jnp.zeros((40, LANES), jnp.float32)
        acc = lax.fori_loop(0, 2 * CHIPS, layer, (zero,) * STARS, unroll=8)
        for k in range(2):
            one, two, three = acc[3 * k : 3 * k + 3]
            joined = jnp.where(lane < 40, one, jnp.where(lane < 80, pltpu.roll(two, 40, 1), pltpu.roll(three, 80, 1)))
            for b in range(5):
                row = pl.multiple_of(((k * 5 + b) * STEPS + t) * PIX, PIX)
                phase[pl.ds(row, PIX), :] = joined[b * PIX : (b + 1) * PIX, :]
        return carry

    lax.fori_loop(0, STEPS, step, 0)

    groups[...] = jnp.zeros_like(groups)
    size = STEPS * PIX

    def spots(kb, carry):
        sine, cosine = sincos(phase[pl.ds(pl.multiple_of(kb * size, PIX), size), :])
        both = jnp.concatenate([cosine, sine], axis=0)
        along = jnp.dot(both, lane_tab[:, : 2 * LANES], precision=HIGHEST, preferred_element_type=jnp.float32)
        s3 = sine.reshape(STEPS, PIX, LANES)
        c3 = cosine.reshape(STEPS, PIX, LANES)
        acc = jnp.zeros_like(c3)
        for d in range(1, PIX):
            acc = acc + sub_tab[(d - 1) * PIX : d * PIX, :][None] * pltpu.roll(c3, d, 1)
        sign = sub_tab[7 * PIX : 8 * PIX, :][None]
        alt_c = jnp.sum(sign * c3, axis=1)
        alt_s = jnp.sum(sign * s3, axis=1)
        num_x = 4.0 * jnp.sum(s3 * acc, axis=1) - 8.0 * (alt_c * alt_c + alt_s * alt_s)
        num_y = 4.0 * jnp.sum(s3 * along[:size, :LANES].reshape(STEPS, PIX, LANES), axis=1)
        alt = along[:, LANES:]
        alt = alt * alt
        alt = jnp.sum((alt[:size] + alt[size:]).reshape(STEPS, PIX, LANES), axis=1)
        grouper = lane_tab[:, 2 * LANES :]
        got_x = jnp.dot(num_x, grouper, precision=HIGHEST, preferred_element_type=jnp.float32)
        got_y = jnp.dot(num_y, grouper, precision=HIGHEST, preferred_element_type=jnp.float32) - alt * (8.0 / 1024)
        for s, got in ((0, got_x), (1, got_y)):
            unit = s * 10 + kb
            tile = unit // 8
            groups[tile, 0:STEPS, :] = groups[tile, 0:STEPS, :] + pltpu.roll(got, (unit % 8) * 16, 1)
        return carry

    lax.fori_loop(0, 10, spots, 0)

    flat = sum(
        jnp.dot(groups[i], order_tab[i * LANES : (i + 1) * LANES, :], precision=HIGHEST, preferred_element_type=jnp.float32)
        for i in range(3)
    )
    flat = flat * mask[...]
    flat_out[...] = flat
    rounded = flat[:, :FLAT].astype(jnp.bfloat16)
    for out, half in ((keep, side), (send, 1 - side)):
        out[...] = jnp.zeros_like(out)
        for i in range(HALF_TILES):
            column = pl.multiple_of((half * HALF_TILES + i) * LANES, LANES)
            part = jnp.dot(rounded, recon[:, pl.ds(column, LANES)], preferred_element_type=jnp.float32)
            for slab, row, first, count in pieces(i):
                out[slab, row : row + count, :] = part[first : first + count]


def pieces(i):
    found = []
    first = 0
    while first < STEPS:
        slab, row = divmod(i * STEPS + first, SLAB_USED)
        count = min(STEPS - first, SLAB_USED - row)
        found.append((slab, row, first, count))
        first += count
    return found


def finish_kernel(core, mine, other, out):
    for ref, half in ((mine, core[0]), (other, 1 - core[0])):
        for i in range(HALF_TILES):
            column = pl.multiple_of((half * HALF_TILES + i) * LANES, LANES)
            for slab, row, first, count in pieces(i):
                out[first : first + count, pl.ds(column, LANES)] = ref[slab, row : row + count, :]


def vmem():
    return pl.BlockSpec(memory_space=pltpu.VMEM)


def smem():
    return pl.BlockSpec(memory_space=pltpu.SMEM)


def pack(low, core, high, fresh, meta):
    return pl.pallas_call(
        pack_kernel,
        out_shape=jax.ShapeDtypeStruct((CHIPS, PAYLOAD, LANES), jnp.float32),
        in_specs=[vmem()] * 5,
        out_specs=vmem(),
        compiler_params=pltpu.CompilerParams(vmem_limit_bytes=32 << 20),
    )(low, core, high, fresh, meta)


def slopes_and_products(core, mine, other, mask, recon):
    slab = jax.ShapeDtypeStruct((SLABS, SLAB_ROWS, LANES), jnp.float32)
    return pl.pallas_call(
        main_kernel,
        out_shape=(slab, slab, jax.ShapeDtypeStruct((16, FLAT_PAD), jnp.float32)),
        in_specs=[smem()] + [vmem()] * 7,
        out_specs=(vmem(),) * 3,
        scratch_shapes=[
            pltpu.VMEM((2 * CHIPS, COLS + NEW_COLS, LANES), jnp.float32),
            pltpu.VMEM((100 * PIX, LANES), jnp.float32),
            pltpu.VMEM((3, 16, LANES), jnp.float32),
            pltpu.VMEM((2 * CHIPS, 8, LANES), jnp.int32),
            pltpu.SMEM((2 * CHIPS, 8, LANES), jnp.int32),
            pltpu.SemaphoreType.DMA(()),
        ],
        compiler_params=pltpu.CompilerParams(vmem_limit_bytes=40 << 20),
    )(core, mine, other, jnp.asarray(sublane_table()), jnp.asarray(lane_table()), jnp.asarray(order_table()), mask, recon)


def finish(core, mine, other):
    return pl.pallas_call(
        finish_kernel,
        out_shape=jax.ShapeDtypeStruct((STEPS, ACTS), jnp.float32),
        in_specs=[smem(), vmem(), vmem()],
        out_specs=vmem(),
    )(core, mine, other)


def groups_by(key):
    found = {}
    for device in range(256):
        layer, sub = divmod(device, 16)
        found.setdefault(key(layer // 8, layer // 2 % 4, layer % 2, sub // 4, sub % 4), []).append(device)
    return [found[name] for name in sorted(found)]


def exchange(blocks, groups):
    return lax.all_to_all(blocks, ("layer", "sub"), 0, 0, tiled=True, axis_index_groups=groups)


def to_all(block, groups):
    return exchange(jnp.broadcast_to(block[None], (len(groups[0]),) + block.shape), groups)


def to_other_core(block):
    return lax.ppermute(block, "layer", [(i, i ^ 1) for i in range(16)])


def local(screens, new_columns, col_block, shift_x, shift_y, valid, recon):
    owner = lax.axis_index("sub")
    count = lax.axis_size("sub")
    strips = jnp.transpose(screens[0], (0, 2, 1))
    fresh = jnp.transpose(new_columns[:, 0], (0, 2, 1))[:, :, LANE0 : LANE0 + KEPT].reshape(UPDATES, KEPT)

    def strip(turn):
        return lax.dynamic_slice(strips, (turn, 0, LANE0), (1, 40, KEPT))[0]

    core = strip(PUP_TURN)
    forward = [(i, (i + 1) % count) for i in range(count)]
    backward = [(target, source) for source, target in forward]
    low = lax.ppermute(strip(jnp.where(owner == count - 1, PUP_TURN - 1, PUP_TURN)), "sub", forward)
    high = lax.ppermute(strip(jnp.where(owner == 0, PUP_TURN + 1, PUP_TURN)), "sub", backward)

    start = jnp.transpose(shift_x[:, 0]) + HALO
    turn = (LANES - HALO - jnp.transpose(shift_y[:, 0])) % LANES
    block = jnp.transpose(col_block) - (PUP_TURN * PUP // NEW_COLS) - (owner * 5 - 5)
    block = jnp.where((block >= 0) & (block < WINDOW // NEW_COLS), block, COLS // NEW_COLS) * NEW_COLS
    meta = (
        jnp.pad(start, ((0, 2), (0, LANES - STEPS)))
        + jnp.pad(turn, ((0, 2), (ROLL_AT, LANES - ROLL_AT - STEPS)))
        + jnp.pad(block, ((6, 1), (0, LANES - STEPS)))
    ).astype(jnp.float32)

    side = (lax.axis_index("layer") % 2).astype(jnp.int32).reshape(1)
    mine = exchange(pack(low, core, high, fresh, meta), groups_by(lambda zh, x, c, y, zl: (c, y, zl)))
    other = to_other_core(mine)

    matrix = jnp.transpose(recon, (0, 2, 3, 1, 4)).reshape(FLAT, ACTS)
    mask = jnp.broadcast_to(valid.astype(jnp.float32)[None, :, :, None], (STARS, 5, 5, 2)).reshape(1, FLAT)
    mask = jnp.pad(mask, ((0, 0), (0, FLAT_PAD - FLAT)))
    keep, send, flat = slopes_and_products(side, mine, other, mask, matrix)

    plane = groups_by(lambda zh, x, c, y, zl: (c, zh, zl))
    column = groups_by(lambda zh, x, c, y, zl: (c, x, y))
    part = jnp.sum(exchange(keep + to_other_core(send), plane), axis=0)
    total = to_all(jnp.sum(to_all(part, column), axis=0), plane)
    commands = finish(side, total, to_other_core(total))
    slopes = jnp.transpose(flat[:STEPS, :FLAT].reshape(STEPS, STARS, 5, 5, 2), (0, 1, 4, 2, 3))
    return (slopes, commands)


def solution(mesh):
    return jax.shard_map(
        local,
        mesh=mesh,
        in_specs=(
            P("layer", None, None, "sub"),
            P(None, "layer", None, None),
            P(None, "layer"),
            P(None, "layer", None),
            P(None, "layer", None),
            P("layer", "sub"),
            P(None, None, "layer", "sub", None),
        ),
        out_specs=(P(None, None, None, "layer", "sub"), P()),
        check_vma=False,
    )
```

```python
import math
import jax
import jax.numpy as jnp
import numpy as np
from jax import lax
from jax.experimental import pallas as pl
from jax.experimental.pallas import tpu as pltpu
from jax.sharding import PartitionSpec as P

ACTS = 5376
HALO = 40
NEW_COLS = 8
PUP = 640
PUP_TURN = 3
ROW0 = 704
STEPS = 10
STARS = 6
PIX = 8
LANES = 128
LANE0 = 640
KEPT = 768
FIRST = ROW0 - HALO - LANE0
WINDOW = 120
UPDATES = STEPS * NEW_COLS
COLS = WINDOW + UPDATES
REST = 56
META = COLS + REST
PAYLOAD = META + 8
CHIPS = 8
CHIP_ROWS = 80
REST_LANES = 32
ROLL_AT = 64
HALF_TILES = 21
SLABS = 16
SLAB_USED = 14
SLAB_ROWS = 16
FLAT = 300
FLAT_PAD = 384


def toeplitz():
    d = np.arange(PIX)[:, None] - np.arange(PIX)[None, :]
    safe = np.where(d == 0, 1, d)
    return np.where(d == 0, 0.0, -4.0 * (-1.0) ** d / np.tan(np.pi * safe / 16))


def parts(value, count):
    found = []
    rest = value
    for _ in range(count):
        found.append(rest.astype(jnp.bfloat16))
        rest = rest - found[-1].astype(jnp.float32)
    return found


def sublane_table():
    t = toeplitz()
    x = np.arange(PIX)
    rows = [(2.0 if d == 4 else 4.0) * t[x, (x - d) % PIX] for d in range(1, 5)]
    return np.repeat(np.concatenate(rows)[:, None], LANES, axis=1).astype(np.float32)


def lane_table():
    t = toeplitz()
    table = np.zeros((2 * LANES, 2 * LANES))
    y = np.arange(PIX)
    sign = (-1.0) ** (y[:, None] - y[None, :])
    for group in range(WINDOW // PIX):
        rows = slice(group * PIX, (group + 1) * PIX)
        after = slice(LANES + group * PIX, LANES + (group + 1) * PIX)
        table[rows, rows] = 4.0 * t.T
        table[after, rows] = -8.0 * sign
        table[rows, after] = -8.0 * sign
    first = table.astype(jnp.bfloat16)
    second = (table - first.astype(np.float64)).astype(jnp.bfloat16)
    return np.concatenate([first, second])


def group_table():
    table = np.zeros((LANES, LANES))
    lane = np.arange(WINDOW)
    table[lane, lane // PIX] = 1.0 / 1024
    return table.astype(jnp.bfloat16)


def order_table():
    table = np.zeros((FLAT_PAD, FLAT_PAD))
    for s in range(2):
        for k in range(2):
            for b in range(5):
                for kk in range(3):
                    for a in range(5):
                        row = (s * 10 + k * 5 + b) * 16 + kk * 5 + a
                        table[row, (((3 * k + kk) * 5 + a) * 5 + b) * 2 + s] = 1.0
    return table.astype(jnp.bfloat16)


def lane_index(shape):
    return lax.broadcasted_iota(jnp.int32, shape, len(shape) - 1)


def pack_kernel(low, core, high, fresh, meta, out):
    def window(ref, first, count, start):
        tile, shift = divmod(start, LANES)
        rows = slice(first, first + count)
        left = ref[rows, tile * LANES : (tile + 1) * LANES]
        if shift == 0:
            return left
        left = pltpu.roll(left, LANES - shift, 1)
        if (tile + 2) * LANES > KEPT:
            return left
        right = pltpu.roll(ref[rows, (tile + 1) * LANES : (tile + 2) * LANES], LANES - shift, 1)
        return jnp.where(lane_index(left.shape) < LANES - shift, left, right)

    sources = ((low, 0), (core, 40), (high, 80), (fresh, 120))

    def columns(first, start):
        ref, base = [source for source in sources if source[1] <= first][-1]
        return window(ref, first - base, PIX, start)

    lane = lane_index((PIX, LANES))
    for m in range(CHIPS):
        start = FIRST + m * CHIP_ROWS
        for ref, base in sources:
            count = UPDATES if base == WINDOW else 40
            out[m, base : base + count, :] = window(ref, 0, count, start)
        for r in range(REST // PIX):
            joined = None
            for q in range(4):
                first = q * REST + r * PIX
                if first >= COLS:
                    continue
                piece = columns(first, start + LANES - q * REST_LANES)
                joined = piece if joined is None else jnp.where(lane < q * REST_LANES, joined, piece)
            out[m, COLS + r * PIX : COLS + (r + 1) * PIX, :] = joined
        out[m, META:PAYLOAD, :] = meta[...]


def sincos(x):
    n = jnp.floor(x * (2.0 / math.pi) + 0.5)
    r = x - n * 1.5703125
    r = r - n * 4.8351287841796875e-4
    r = r - n * 3.13855707645416259765625e-7
    r = r - n * 6.0771005065061922e-11
    q = n.astype(jnp.int32)
    z = r * r
    s = r + r * z * (-1.6666654611e-1 + z * (8.3321608736e-3 + z * -1.9515295891e-4))
    c = 1.0 - 0.5 * z + z * z * (4.166664568298827e-2 + z * (-1.388731625493765e-3 + z * 2.443315711809948e-5))
    swap = (q & 1) == 1
    sine = jnp.where(swap, c, s)
    cosine = jnp.where(swap, s, c)
    sine = jnp.where((q & 2) == 2, -sine, sine)
    cosine = jnp.where(((q + 1) & 2) == 2, -cosine, cosine)
    return sine, cosine


def main_kernel(
    core, mine, other, sub_hbm, lane_hbm, group_hbm, order_hbm, mask, recon,
    keep, send, flat_out,
    state, phase, sums, numbers, sub_tab, lane_tab, group_tab, order_tab, meta, arrived,
):
    lane = lane_index((40, LANES))
    side = core[0]
    for p in range(CHIPS):
        numbers[p] = mine[p, META:, :].astype(jnp.int32)
        numbers[CHIPS + p] = other[p, META:, :].astype(jnp.int32)
    copy = pltpu.make_async_copy(numbers, meta, arrived.at[0])
    copy.start()
    tables = ((sub_hbm, sub_tab), (lane_hbm, lane_tab), (group_hbm, group_tab), (order_hbm, order_tab))
    fetches = [pltpu.make_async_copy(source, target, arrived.at[1 + i]) for i, (source, target) in enumerate(tables)]
    for fetch in fetches:
        fetch.start()
    sums[...] = jnp.zeros_like(sums)

    cut = LANES - 40 * side
    turn = lax.rem(cut, LANES)

    def begin(p, carry):
        for base, ref in ((0, mine), (CHIPS, other)):
            for q in range(4):
                first = q * REST
                count = min(REST, COLS - first)
                left = pltpu.roll(ref[p, first : first + count, :], turn, 1)
                right = pltpu.roll(ref[p, COLS : COLS + count, :], (88 - REST_LANES * q) % LANES, 1)
                state[base + p, first : first + count, :] = jnp.where(lane_index(left.shape) < cut, left, right)
        return carry

    lax.fori_loop(0, CHIPS, begin, 0)
    copy.wait()

    def cut_and_add(t):
        def layer(l, acc):
            dst = pl.multiple_of(meta[l, 6, t], NEW_COLS)
            src = pl.multiple_of(WINDOW + t * NEW_COLS, NEW_COLS)
            state[l, pl.ds(dst, NEW_COLS), :] = state[l, pl.ds(src, NEW_COLS), :]
            return tuple(
                acc[g] + pltpu.roll(state[l, pl.ds(meta[l, g, t], 40), :], meta[l, g, ROLL_AT + t], 1)
                for g in range(STARS)
            )

        acc = (jnp.zeros((40, LANES), jnp.float32),) * STARS
        for l in range(2 * CHIPS):
            acc = layer(l, acc)
        for k in range(2):
            one, two, three = acc[3 * k : 3 * k + 3]
            joined = jnp.where(lane < 40, one, jnp.where(lane < 80, pltpu.roll(two, 40, 1), pltpu.roll(three, 80, 1)))
            phase[lax.rem(t, 2), k * 40 : (k + 1) * 40, :] = joined

    def spots(t):
        sine, cosine = sincos(phase[lax.rem(t, 2)])
        c1, c2 = parts(cosine, 2)
        s1, s2 = parts(sine, 2)
        head = jnp.concatenate([c1, s1], axis=1)
        tail = jnp.concatenate([c2, s2], axis=1)
        first = jnp.dot(jnp.concatenate([head, tail]), lane_tab[: 2 * LANES], preferred_element_type=jnp.float32)
        second = jnp.dot(head, lane_tab[2 * LANES :], preferred_element_type=jnp.float32)
        along = first[:80] + first[80:] + second
        z_y = sine * along[:, :LANES] + cosine * along[:, LANES:]

        c3 = cosine.reshape(10, PIX, LANES)
        s3 = sine.reshape(10, PIX, LANES)
        by_sine = -8.0 * s3
        by_cosine = -8.0 * c3
        for d in range(1, 5):
            weight = sub_tab[(d - 1) * PIX : d * PIX, :][None]
            even = -8.0 if d == 4 else 16.0 * (-1.0) ** (d + 1)
            c_d = pltpu.roll(c3, d, 1)
            s_d = pltpu.roll(s3, d, 1)
            by_sine = by_sine + (weight * c_d + even * s_d)
            by_cosine = by_cosine + (even * c_d - weight * s_d)
        z_x = jnp.sum(s3 * by_sine + c3 * by_cosine, axis=1)
        z_y = jnp.sum(z_y.reshape(10, PIX, LANES), axis=1)
        for unit in range(10):
            sums[unit, pl.ds(t, 1), :] = z_x[unit : unit + 1]
            sums[10 + unit, pl.ds(t, 1), :] = z_y[unit : unit + 1]

    cut_and_add(0)
    for fetch in fetches:
        fetch.wait()

    def step(t, carry):
        cut_and_add(t)
        spots(t - 1)
        return carry

    lax.fori_loop(1, STEPS, step, 0)
    spots(STEPS - 1)

    units = 20
    stacked = jnp.concatenate(parts(sums[...].reshape(units * 16, LANES), 3))
    got = jnp.dot(stacked, group_tab[...], preferred_element_type=jnp.float32)
    size = units * 16
    got = (got[:size] + got[size : 2 * size]) + got[2 * size :]
    tiles = [jnp.zeros((16, LANES), jnp.float32) for _ in range(3)]
    for unit in range(units):
        tiles[unit // 8] = tiles[unit // 8] + pltpu.roll(got[unit * 16 : (unit + 1) * 16], (unit % 8) * 16, 1)
    flat = jnp.zeros((16, FLAT_PAD), jnp.float32)
    for i in range(3):
        moved = jnp.dot(
            jnp.concatenate(parts(tiles[i], 3)), order_tab[i * LANES : (i + 1) * LANES, :], preferred_element_type=jnp.float32
        )
        flat = flat + ((moved[:16] + moved[16:32]) + moved[32:])
    flat = flat * mask[...]
    flat_out[...] = flat
    rounded = flat[:, :FLAT].astype(jnp.bfloat16)
    for out, half in ((keep, side), (send, 1 - side)):
        out[...] = jnp.zeros_like(out)
        for i in range(HALF_TILES):
            column = pl.multiple_of((half * HALF_TILES + i) * LANES, LANES)
            part = jnp.dot(rounded, recon[:, pl.ds(column, LANES)], preferred_element_type=jnp.float32)
            for slab, row, first, count in pieces(i):
                out[slab, row : row + count, :] = part[first : first + count]


def pieces(i):
    found = []
    first = 0
    while first < STEPS:
        slab, row = divmod(i * STEPS + first, SLAB_USED)
        count = min(STEPS - first, SLAB_USED - row)
        found.append((slab, row, first, count))
        first += count
    return found


def finish_kernel(core, mine, other, out):
    for ref, half in ((mine, core[0]), (other, 1 - core[0])):
        for i in range(HALF_TILES):
            column = pl.multiple_of((half * HALF_TILES + i) * LANES, LANES)
            for slab, row, first, count in pieces(i):
                out[first : first + count, pl.ds(column, LANES)] = ref[slab, row : row + count, :]


def vmem():
    return pl.BlockSpec(memory_space=pltpu.VMEM)


def smem():
    return pl.BlockSpec(memory_space=pltpu.SMEM)


def pack(low, core, high, fresh, meta):
    return pl.pallas_call(
        pack_kernel,
        out_shape=jax.ShapeDtypeStruct((CHIPS, PAYLOAD, LANES), jnp.float32),
        in_specs=[vmem()] * 5,
        out_specs=vmem(),
        compiler_params=pltpu.CompilerParams(vmem_limit_bytes=32 << 20),
    )(low, core, high, fresh, meta)


def slopes_and_products(core, mine, other, mask, recon):
    slab = jax.ShapeDtypeStruct((SLABS, SLAB_ROWS, LANES), jnp.float32)
    return pl.pallas_call(
        main_kernel,
        out_shape=(slab, slab, jax.ShapeDtypeStruct((16, FLAT_PAD), jnp.float32)),
        in_specs=[smem()] + [vmem()] * 2 + [pl.BlockSpec(memory_space=pltpu.HBM)] * 4 + [vmem()] * 2,
        out_specs=(vmem(),) * 3,
        scratch_shapes=[
            pltpu.VMEM((2 * CHIPS, COLS + NEW_COLS, LANES), jnp.float32),
            pltpu.VMEM((2, 10 * PIX, LANES), jnp.float32),
            pltpu.VMEM((20, 16, LANES), jnp.float32),
            pltpu.VMEM((2 * CHIPS, 8, LANES), jnp.int32),
            pltpu.VMEM((4 * PIX, LANES), jnp.float32),
            pltpu.VMEM((4 * LANES, 2 * LANES), jnp.bfloat16),
            pltpu.VMEM((LANES, LANES), jnp.bfloat16),
            pltpu.VMEM((FLAT_PAD, FLAT_PAD), jnp.bfloat16),
            pltpu.SMEM((2 * CHIPS, 8, LANES), jnp.int32),
            pltpu.SemaphoreType.DMA((5,)),
        ],
        compiler_params=pltpu.CompilerParams(vmem_limit_bytes=40 << 20),
    )(
        core, mine, other, jnp.asarray(sublane_table()), jnp.asarray(lane_table()), jnp.asarray(group_table()),
        jnp.asarray(order_table()), mask, recon,
    )


def finish(core, mine, other):
    return pl.pallas_call(
        finish_kernel,
        out_shape=jax.ShapeDtypeStruct((STEPS, ACTS), jnp.float32),
        in_specs=[smem(), vmem(), vmem()],
        out_specs=vmem(),
    )(core, mine, other)


def groups_by(key):
    found = {}
    for device in range(256):
        layer, sub = divmod(device, 16)
        found.setdefault(key(layer // 8, layer // 2 % 4, layer % 2, sub // 4, sub % 4), []).append(device)
    return [found[name] for name in sorted(found)]


def exchange(blocks, groups):
    return lax.all_to_all(blocks, ("layer", "sub"), 0, 0, tiled=True, axis_index_groups=groups)


def to_all(block, groups):
    return exchange(jnp.broadcast_to(block[None], (len(groups[0]),) + block.shape), groups)


def to_other_core(block):
    return lax.ppermute(block, "layer", [(i, i ^ 1) for i in range(16)])


def local(screens, new_columns, col_block, shift_x, shift_y, valid, recon):
    owner = lax.axis_index("sub")
    count = lax.axis_size("sub")
    strips = jnp.transpose(screens[0], (0, 2, 1))
    fresh = jnp.transpose(new_columns[:, 0], (0, 2, 1))[:, :, LANE0 : LANE0 + KEPT].reshape(UPDATES, KEPT)

    def strip(turn):
        return lax.dynamic_slice(strips, (turn, 0, LANE0), (1, 40, KEPT))[0]

    core = strip(PUP_TURN)
    forward = [(i, (i + 1) % count) for i in range(count)]
    backward = [(target, source) for source, target in forward]
    low = lax.ppermute(strip(jnp.where(owner == count - 1, PUP_TURN - 1, PUP_TURN)), "sub", forward)
    high = lax.ppermute(strip(jnp.where(owner == 0, PUP_TURN + 1, PUP_TURN)), "sub", backward)

    start = jnp.transpose(shift_x[:, 0]) + HALO
    turn = (LANES - HALO - jnp.transpose(shift_y[:, 0])) % LANES
    block = jnp.transpose(col_block) - (PUP_TURN * PUP // NEW_COLS) - (owner * 5 - 5)
    block = jnp.where((block >= 0) & (block < WINDOW // NEW_COLS), block, COLS // NEW_COLS) * NEW_COLS
    meta = (
        jnp.pad(start, ((0, 2), (0, LANES - STEPS)))
        + jnp.pad(turn, ((0, 2), (ROLL_AT, LANES - ROLL_AT - STEPS)))
        + jnp.pad(block, ((6, 1), (0, LANES - STEPS)))
    ).astype(jnp.float32)

    side = (lax.axis_index("layer") % 2).astype(jnp.int32).reshape(1)
    mine = exchange(pack(low, core, high, fresh, meta), groups_by(lambda zh, x, c, y, zl: (c, y, zl)))
    matrix = jnp.transpose(recon, (0, 2, 3, 1, 4)).reshape(FLAT, ACTS)
    mine, matrix = lax.optimization_barrier((mine, matrix))
    other = to_other_core(mine)

    mask = jnp.broadcast_to(valid.astype(jnp.float32)[None, :, :, None], (STARS, 5, 5, 2)).reshape(1, FLAT)
    mask = jnp.pad(mask, ((0, 0), (0, FLAT_PAD - FLAT)))
    keep, send, flat = slopes_and_products(side, mine, other, mask, matrix)

    plane = groups_by(lambda zh, x, c, y, zl: (c, zh, zl))
    column = groups_by(lambda zh, x, c, y, zl: (c, x, y))
    part = jnp.sum(exchange(keep + to_other_core(send), plane), axis=0)
    total = to_all(jnp.sum(to_all(part, column), axis=0), plane)
    commands = finish(side, total, to_other_core(total))
    slopes = jnp.transpose(flat[:STEPS, :FLAT].reshape(STEPS, STARS, 5, 5, 2), (0, 1, 4, 2, 3))
    return (slopes, commands)


def solution(mesh):
    return jax.shard_map(
        local,
        mesh=mesh,
        in_specs=(
            P("layer", None, None, "sub"),
            P(None, "layer", None, None),
            P(None, "layer"),
            P(None, "layer", None),
            P(None, "layer", None),
            P("layer", "sub"),
            P(None, None, "layer", "sub", None),
        ),
        out_specs=(P(None, None, None, "layer", "sub"), P()),
        check_vma=False,
    )
```

```python
import math
import jax
import jax.numpy as jnp
import numpy as np
from jax import lax
from jax.experimental import pallas as pl
from jax.experimental.pallas import tpu as pltpu
from jax.sharding import PartitionSpec as P

ACTS = 5376
HALO = 40
NEW_COLS = 8
PUP = 640
PUP_TURN = 3
ROW0 = 704
STEPS = 10
STARS = 6
PIX = 8
LANES = 128
LANE0 = 640
KEPT = 768
FIRST = ROW0 - HALO - LANE0
WINDOW = 120
UPDATES = STEPS * NEW_COLS
COLS = WINDOW + UPDATES
REST = 56
META = COLS + REST
PAYLOAD = META + 8
CHIPS = 8
CHIP_ROWS = 80
REST_LANES = 32
ROLL_AT = 64
HALF_TILES = 21
SLABS = 16
SLAB_USED = 14
SLAB_ROWS = 16
FLAT = 300
FLAT_PAD = 384


def toeplitz():
    d = np.arange(PIX)[:, None] - np.arange(PIX)[None, :]
    safe = np.where(d == 0, 1, d)
    return np.where(d == 0, 0.0, -4.0 * (-1.0) ** d / np.tan(np.pi * safe / 16))


def parts(value, count):
    found = []
    rest = value
    for _ in range(count):
        found.append(rest.astype(jnp.bfloat16))
        rest = rest - found[-1].astype(jnp.float32)
    return found


def ahead(d):
    t = toeplitz()
    x = lax.broadcasted_iota(jnp.int32, (PIX, LANES), 0)
    weight = jnp.zeros((PIX, LANES), jnp.float32)
    for i in range(PIX):
        weight = jnp.where(x == i, jnp.float32((2.0 if d == 4 else 4.0) * t[i, (i - d) % PIX]), weight)
    return weight


def lane_table():
    t = toeplitz()
    table = np.zeros((2 * LANES, 2 * LANES))
    y = np.arange(PIX)
    sign = (-1.0) ** (y[:, None] - y[None, :])
    for group in range(WINDOW // PIX):
        rows = slice(group * PIX, (group + 1) * PIX)
        after = slice(LANES + group * PIX, LANES + (group + 1) * PIX)
        table[rows, rows] = 4.0 * t.T
        table[after, rows] = -8.0 * sign
        table[rows, after] = -8.0 * sign
    first = table.astype(jnp.bfloat16)
    second = (table - first.astype(np.float64)).astype(jnp.bfloat16)
    return np.concatenate([first, second])


def group_table():
    lane = lax.broadcasted_iota(jnp.int32, (LANES, LANES), 0)
    group = lax.broadcasted_iota(jnp.int32, (LANES, LANES), 1)
    first = group * PIX
    return jnp.where((lane >= first) & (lane < first + PIX) & (lane < WINDOW), 1.0 / 1024, 0.0).astype(jnp.bfloat16)


def multiple(value, step, count):
    found = jnp.zeros_like(value)
    for i in range(1, count + 1):
        found = found + (value >= step * i).astype(jnp.int32)
    return found


def order_table(tile):
    row = lax.broadcasted_iota(jnp.int32, (LANES, LANES), 0) + tile * LANES
    column = lax.broadcasted_iota(jnp.int32, (LANES, LANES), 1)
    unit = lax.shift_right_logical(row, 4)
    place = row & 15
    s = multiple(unit, 10, 1)
    k = multiple(unit - 10 * s, 5, 1)
    b = unit - 10 * s - 5 * k
    kk = multiple(place, 5, 2)
    target = (((3 * k + kk) * 5 + place - 5 * kk) * 5 + b) * 2 + s
    target = jnp.where((place < 15) & (unit < 20), target, -1)
    blocks = [(target == column + i * LANES).astype(jnp.float32).astype(jnp.bfloat16) for i in range(FLAT_PAD // LANES)]
    return jnp.concatenate(blocks, axis=1)


def lit(flags):
    place = lax.shift_right_logical(lax.broadcasted_iota(jnp.int32, (8, FLAT_PAD), 1), 1)
    place = place - 25 * multiple(place, 25, 7)
    found = jnp.zeros((8, FLAT_PAD), jnp.float32)
    for a in range(5):
        for b in range(5):
            found = jnp.where(place == a * 5 + b, flags[1 + a * 5 + b].astype(jnp.float32), found)
    return found


def lane_index(shape):
    return lax.broadcasted_iota(jnp.int32, shape, len(shape) - 1)


def pack_kernel(low, core, high, fresh, meta, out):
    def window(ref, first, count, start):
        tile, shift = divmod(start, LANES)
        rows = slice(first, first + count)
        left = ref[rows, tile * LANES : (tile + 1) * LANES]
        if shift == 0:
            return left
        left = pltpu.roll(left, LANES - shift, 1)
        if (tile + 2) * LANES > KEPT:
            return left
        right = pltpu.roll(ref[rows, (tile + 1) * LANES : (tile + 2) * LANES], LANES - shift, 1)
        return jnp.where(lane_index(left.shape) < LANES - shift, left, right)

    sources = ((low, 0), (core, 40), (high, 80), (fresh, 120))

    def columns(first, start):
        ref, base = [source for source in sources if source[1] <= first][-1]
        return window(ref, first - base, PIX, start)

    lane = lane_index((PIX, LANES))
    for m in range(CHIPS):
        start = FIRST + m * CHIP_ROWS
        for ref, base in sources:
            count = UPDATES if base == WINDOW else 40
            out[m, base : base + count, :] = window(ref, 0, count, start)
        for r in range(REST // PIX):
            joined = None
            for q in range(4):
                first = q * REST + r * PIX
                if first >= COLS:
                    continue
                piece = columns(first, start + LANES - q * REST_LANES)
                joined = piece if joined is None else jnp.where(lane < q * REST_LANES, joined, piece)
            out[m, COLS + r * PIX : COLS + (r + 1) * PIX, :] = joined
        out[m, META:PAYLOAD, :] = meta[...]


def sincos(x):
    n = jnp.floor(x * (2.0 / math.pi) + 0.5)
    r = x - n * 1.5703125
    r = r - n * 4.8351287841796875e-4
    r = r - n * 3.13855707645416259765625e-7
    r = r - n * 6.0771005065061922e-11
    q = n.astype(jnp.int32)
    z = r * r
    s = r + r * z * (-1.6666654611e-1 + z * (8.3321608736e-3 + z * -1.9515295891e-4))
    c = 1.0 - 0.5 * z + z * z * (4.166664568298827e-2 + z * (-1.388731625493765e-3 + z * 2.443315711809948e-5))
    swap = (q & 1) == 1
    sine = jnp.where(swap, c, s)
    cosine = jnp.where(swap, s, c)
    sine = jnp.where((q & 2) == 2, -sine, sine)
    cosine = jnp.where(((q + 1) & 2) == 2, -cosine, cosine)
    return sine, cosine


def main_kernel(
    flags, mine, other, lane_tab, recon,
    keep, send, flat_out,
    state, phase, sums, numbers, meta, arrived,
):
    lane = lane_index((40, LANES))
    side = flags[0]
    for p in range(CHIPS):
        numbers[p] = mine[p, META:, :].astype(jnp.int32)
        numbers[CHIPS + p] = other[p, META:, :].astype(jnp.int32)
    copy = pltpu.make_async_copy(numbers, meta, arrived)
    copy.start()
    sums[...] = jnp.zeros_like(sums)

    cut = LANES - 40 * side
    turn = lax.rem(cut, LANES)

    def begin(p, carry):
        for base, ref in ((0, mine), (CHIPS, other)):
            for q in range(4):
                first = q * REST
                count = min(REST, COLS - first)
                left = pltpu.roll(ref[p, first : first + count, :], turn, 1)
                right = pltpu.roll(ref[p, COLS : COLS + count, :], (88 - REST_LANES * q) % LANES, 1)
                state[base + p, first : first + count, :] = jnp.where(lane_index(left.shape) < cut, left, right)
        return carry

    lax.fori_loop(0, CHIPS, begin, 0)
    copy.wait()

    def cut_and_add(t):
        for l in range(2 * CHIPS):
            dst = pl.multiple_of(meta[l, 6, t], NEW_COLS)
            src = pl.multiple_of(WINDOW + t * NEW_COLS, NEW_COLS)
            state[l, pl.ds(dst, NEW_COLS), :] = state[l, pl.ds(src, NEW_COLS), :]
        acc = []
        for g in range(STARS):
            total = jnp.zeros((40, LANES), jnp.float32)
            for l in range(2 * CHIPS):
                total = total + pltpu.roll(state[l, pl.ds(meta[l, g, t], 40), :], meta[l, g, ROLL_AT + t], 1)
            acc.append(total)
        for k in range(2):
            one, two, three = acc[3 * k : 3 * k + 3]
            joined = jnp.where(lane < 40, one, jnp.where(lane < 80, pltpu.roll(two, 40, 1), pltpu.roll(three, 80, 1)))
            phase[lax.rem(t, 2), k * 40 : (k + 1) * 40, :] = joined

    def spots(t):
        sine, cosine = sincos(phase[lax.rem(t, 2)])
        c1, c2 = parts(cosine, 2)
        s1, s2 = parts(sine, 2)
        head = jnp.concatenate([c1, s1], axis=1)
        tail = jnp.concatenate([c2, s2], axis=1)
        first = jnp.dot(jnp.concatenate([head, tail]), lane_tab[: 2 * LANES], preferred_element_type=jnp.float32)
        second = jnp.dot(head, lane_tab[2 * LANES :], preferred_element_type=jnp.float32)
        along = first[:80] + first[80:] + second
        z_y = sine * along[:, :LANES] + cosine * along[:, LANES:]

        c3 = cosine.reshape(10, PIX, LANES)
        s3 = sine.reshape(10, PIX, LANES)
        by_sine = -8.0 * s3
        by_cosine = -8.0 * c3
        for d in range(1, 5):
            weight = weights[d - 1][None]
            even = -8.0 if d == 4 else 16.0 * (-1.0) ** (d + 1)
            c_d = pltpu.roll(c3, d, 1)
            s_d = pltpu.roll(s3, d, 1)
            by_sine = by_sine + (weight * c_d + even * s_d)
            by_cosine = by_cosine + (even * c_d - weight * s_d)
        z_x = jnp.sum(s3 * by_sine + c3 * by_cosine, axis=1)
        z_y = jnp.sum(z_y.reshape(10, PIX, LANES), axis=1)
        for unit in range(10):
            sums[unit, pl.ds(t, 1), :] = z_x[unit : unit + 1]
            sums[10 + unit, pl.ds(t, 1), :] = z_y[unit : unit + 1]

    weights = [ahead(d) for d in range(1, 5)]
    cut_and_add(0)

    def step(t, carry):
        cut_and_add(t)
        spots(t - 1)
        return carry

    lax.fori_loop(1, STEPS, step, 0)
    spots(STEPS - 1)

    units = 20
    stacked = jnp.concatenate(parts(sums[...].reshape(units * 16, LANES), 3))
    got = jnp.dot(stacked, group_table(), preferred_element_type=jnp.float32)
    size = units * 16
    got = (got[:size] + got[size : 2 * size]) + got[2 * size :]
    tiles = [jnp.zeros((16, LANES), jnp.float32) for _ in range(3)]
    for unit in range(units):
        tiles[unit // 8] = tiles[unit // 8] + pltpu.roll(got[unit * 16 : (unit + 1) * 16], (unit % 8) * 16, 1)
    flat = jnp.zeros((16, FLAT_PAD), jnp.float32)
    for i in range(3):
        moved = jnp.dot(
            jnp.concatenate(parts(tiles[i], 3)), order_table(i), preferred_element_type=jnp.float32
        )
        flat = flat + ((moved[:16] + moved[16:32]) + moved[32:])
    shown = lit(flags)
    flat = flat * jnp.concatenate([shown, shown])
    flat_out[...] = flat
    rounded = flat[:, :FLAT].astype(jnp.bfloat16)
    for out, half in ((keep, side), (send, 1 - side)):
        out[...] = jnp.zeros_like(out)
        for i in range(HALF_TILES):
            column = pl.multiple_of((half * HALF_TILES + i) * LANES, LANES)
            part = jnp.dot(rounded, recon[:, pl.ds(column, LANES)], preferred_element_type=jnp.float32)
            for slab, row, first, count in pieces(i):
                out[slab, row : row + count, :] = part[first : first + count]


def pieces(i):
    found = []
    first = 0
    while first < STEPS:
        slab, row = divmod(i * STEPS + first, SLAB_USED)
        count = min(STEPS - first, SLAB_USED - row)
        found.append((slab, row, first, count))
        first += count
    return found


def finish_kernel(core, mine, other, out):
    for ref, half in ((mine, core[0]), (other, 1 - core[0])):
        for i in range(HALF_TILES):
            column = pl.multiple_of((half * HALF_TILES + i) * LANES, LANES)
            for slab, row, first, count in pieces(i):
                out[first : first + count, pl.ds(column, LANES)] = ref[slab, row : row + count, :]


def vmem():
    return pl.BlockSpec(memory_space=pltpu.VMEM)


def smem():
    return pl.BlockSpec(memory_space=pltpu.SMEM)


def pack(low, core, high, fresh, meta):
    return pl.pallas_call(
        pack_kernel,
        out_shape=jax.ShapeDtypeStruct((CHIPS, PAYLOAD, LANES), jnp.float32),
        in_specs=[vmem()] * 5,
        out_specs=vmem(),
        compiler_params=pltpu.CompilerParams(vmem_limit_bytes=16 << 20),
    )(low, core, high, fresh, meta)


def slopes_and_products(flags, mine, other, recon):
    slab = jax.ShapeDtypeStruct((SLABS, SLAB_ROWS, LANES), jnp.float32)
    return pl.pallas_call(
        main_kernel,
        out_shape=(slab, slab, jax.ShapeDtypeStruct((16, FLAT_PAD), jnp.float32)),
        in_specs=[smem()] + [vmem()] * 4,
        out_specs=(vmem(),) * 3,
        scratch_shapes=[
            pltpu.VMEM((2 * CHIPS, COLS + NEW_COLS, LANES), jnp.float32),
            pltpu.VMEM((2, 10 * PIX, LANES), jnp.float32),
            pltpu.VMEM((20, 16, LANES), jnp.float32),
            pltpu.VMEM((2 * CHIPS, 8, LANES), jnp.int32),
            pltpu.SMEM((2 * CHIPS, 8, LANES), jnp.int32),
            pltpu.SemaphoreType.DMA(()),
        ],
        compiler_params=pltpu.CompilerParams(vmem_limit_bytes=20 << 20),
    )(flags, mine, other, jnp.asarray(lane_table()), recon)


def finish(core, mine, other):
    return pl.pallas_call(
        finish_kernel,
        out_shape=jax.ShapeDtypeStruct((STEPS, ACTS), jnp.float32),
        in_specs=[smem(), vmem(), vmem()],
        out_specs=vmem(),
        compiler_params=pltpu.CompilerParams(vmem_limit_bytes=8 << 20),
    )(core, mine, other)


def groups_by(key):
    found = {}
    for device in range(256):
        layer, sub = divmod(device, 16)
        found.setdefault(key(layer // 8, layer // 2 % 4, layer % 2, sub // 4, sub % 4), []).append(device)
    return [found[name] for name in sorted(found)]


def exchange(blocks, groups):
    return lax.all_to_all(blocks, ("layer", "sub"), 0, 0, tiled=True, axis_index_groups=groups)


def to_all(block, groups):
    return exchange(jnp.broadcast_to(block[None], (len(groups[0]),) + block.shape), groups)


def to_other_core(block):
    return lax.ppermute(block, "layer", [(i, i ^ 1) for i in range(16)])


def local(screens, new_columns, col_block, shift_x, shift_y, valid, recon):
    owner = lax.axis_index("sub")
    count = lax.axis_size("sub")
    strips = jnp.transpose(screens[0], (0, 2, 1))
    fresh = jnp.transpose(new_columns[:, 0], (0, 2, 1))[:, :, LANE0 : LANE0 + KEPT].reshape(UPDATES, KEPT)

    def strip(turn):
        return lax.dynamic_slice(strips, (turn, 0, LANE0), (1, 40, KEPT))[0]

    core = strip(PUP_TURN)
    forward = [(i, (i + 1) % count) for i in range(count)]
    backward = [(target, source) for source, target in forward]
    low = lax.ppermute(strip(jnp.where(owner == count - 1, PUP_TURN - 1, PUP_TURN)), "sub", forward)
    high = lax.ppermute(strip(jnp.where(owner == 0, PUP_TURN + 1, PUP_TURN)), "sub", backward)

    start = jnp.transpose(shift_x[:, 0]) + HALO
    turn = (LANES - HALO - jnp.transpose(shift_y[:, 0])) % LANES
    block = jnp.transpose(col_block) - (PUP_TURN * PUP // NEW_COLS) - (owner * 5 - 5)
    block = jnp.where((block >= 0) & (block < WINDOW // NEW_COLS), block, COLS // NEW_COLS) * NEW_COLS
    meta = (
        jnp.pad(start, ((0, 2), (0, LANES - STEPS)))
        + jnp.pad(turn, ((0, 2), (ROLL_AT, LANES - ROLL_AT - STEPS)))
        + jnp.pad(block, ((6, 1), (0, LANES - STEPS)))
    ).astype(jnp.float32)

    side = (lax.axis_index("layer") % 2).astype(jnp.int32).reshape(1)
    mine = exchange(pack(low, core, high, fresh, meta), groups_by(lambda zh, x, c, y, zl: (c, y, zl)))
    matrix = jnp.transpose(recon, (0, 2, 3, 1, 4)).reshape(FLAT, ACTS)
    flags = jnp.concatenate([side, valid.reshape(-1)])
    mine, matrix, flags = lax.optimization_barrier((mine, matrix, flags))
    other = to_other_core(mine)

    keep, send, flat = slopes_and_products(flags, mine, other, matrix)

    plane = groups_by(lambda zh, x, c, y, zl: (c, zh, zl))
    column = groups_by(lambda zh, x, c, y, zl: (c, x, y))
    part = jnp.sum(exchange(keep + to_other_core(send), plane), axis=0)
    total = to_all(jnp.sum(to_all(part, column), axis=0), plane)
    commands = finish(side, total, to_other_core(total))
    slopes = jnp.transpose(flat[:STEPS, :FLAT].reshape(STEPS, STARS, 5, 5, 2), (0, 1, 4, 2, 3))
    return (slopes, commands)


def solution(mesh):
    return jax.shard_map(
        local,
        mesh=mesh,
        in_specs=(
            P("layer", None, None, "sub"),
            P(None, "layer", None, None),
            P(None, "layer"),
            P(None, "layer", None),
            P(None, "layer", None),
            P("layer", "sub"),
            P(None, None, "layer", "sub", None),
        ),
        out_specs=(P(None, None, None, "layer", "sub"), P()),
        check_vma=False,
    )
```

```python
import math
import jax
import jax.numpy as jnp
import numpy as np
from jax import lax
from jax.experimental import pallas as pl
from jax.experimental.pallas import tpu as pltpu
from jax.sharding import PartitionSpec as P

ACTS = 5376
HALO = 40
NEW_COLS = 8
PUP = 640
PUP_TURN = 3
ROW0 = 704
STEPS = 10
STARS = 6
PIX = 8
LANES = 128
LANE0 = 640
KEPT = 768
FIRST = ROW0 - HALO - LANE0
WINDOW = 120
UPDATES = STEPS * NEW_COLS
COLS = WINDOW + UPDATES
REST = 56
META = COLS + 32
PAYLOAD = COLS + REST
TILE = COLS + NEW_COLS
META_LANE = 96
TURN_LANE = 106
BEHIND = 32
CHIPS = 8
CHIP_ROWS = 80
REST_LANES = 32
HALF_TILES = 21
SLABS = 16
SLAB_USED = 14
SLAB_ROWS = 16
FLAT = 300
FLAT_PAD = 384


def toeplitz():
    d = np.arange(PIX)[:, None] - np.arange(PIX)[None, :]
    safe = np.where(d == 0, 1, d)
    return np.where(d == 0, 0.0, -4.0 * (-1.0) ** d / np.tan(np.pi * safe / 16))


def parts(value, count):
    found = []
    rest = value
    for _ in range(count):
        found.append(rest.astype(jnp.bfloat16))
        rest = rest - found[-1].astype(jnp.float32)
    return found


def ahead(d):
    t = toeplitz()
    x = lax.broadcasted_iota(jnp.int32, (PIX, LANES), 0)
    weight = jnp.zeros((PIX, LANES), jnp.float32)
    for i in range(PIX):
        weight = jnp.where(x == i, jnp.float32((2.0 if d == 4 else 4.0) * t[i, (i - d) % PIX]), weight)
    return weight


def lane_table():
    t = toeplitz()
    table = np.zeros((2 * LANES, 2 * LANES))
    y = np.arange(PIX)
    sign = (-1.0) ** (y[:, None] - y[None, :])
    for group in range(WINDOW // PIX):
        rows = slice(group * PIX, (group + 1) * PIX)
        after = slice(LANES + group * PIX, LANES + (group + 1) * PIX)
        table[rows, rows] = 4.0 * t.T
        table[after, rows] = -8.0 * sign
        table[rows, after] = -8.0 * sign
    first = table.astype(jnp.bfloat16)
    second = (table - first.astype(np.float64)).astype(jnp.bfloat16)
    return np.concatenate([first, second])


def group_table():
    lane = lax.broadcasted_iota(jnp.int32, (LANES, LANES), 0)
    group = lax.broadcasted_iota(jnp.int32, (LANES, LANES), 1)
    first = group * PIX
    return jnp.where((lane >= first) & (lane < first + PIX) & (lane < WINDOW), 1.0 / 1024, 0.0).astype(jnp.bfloat16)


def multiple(value, step, count):
    found = jnp.zeros_like(value)
    for i in range(1, count + 1):
        found = found + (value >= step * i).astype(jnp.int32)
    return found


def order_table(tile):
    row = lax.broadcasted_iota(jnp.int32, (LANES, LANES), 0) + tile * LANES
    column = lax.broadcasted_iota(jnp.int32, (LANES, LANES), 1)
    unit = lax.shift_right_logical(row, 4)
    place = row & 15
    s = multiple(unit, 10, 1)
    k = multiple(unit - 10 * s, 5, 1)
    b = unit - 10 * s - 5 * k
    kk = multiple(place, 5, 2)
    target = (((3 * k + kk) * 5 + place - 5 * kk) * 5 + b) * 2 + s
    target = jnp.where((place < 15) & (unit < 20), target, -1)
    blocks = [(target == column + i * LANES).astype(jnp.float32).astype(jnp.bfloat16) for i in range(FLAT_PAD // LANES)]
    return jnp.concatenate(blocks, axis=1)


def lit(flags):
    place = lax.shift_right_logical(lax.broadcasted_iota(jnp.int32, (8, FLAT_PAD), 1), 1)
    place = place - 25 * multiple(place, 25, 7)
    found = jnp.zeros((8, FLAT_PAD), jnp.float32)
    for a in range(5):
        for b in range(5):
            found = jnp.where(place == a * 5 + b, flags[1 + a * 5 + b].astype(jnp.float32), found)
    return found


def lane_index(shape):
    return lax.broadcasted_iota(jnp.int32, shape, len(shape) - 1)


def pack_kernel(low, core, high, fresh, meta, out):
    def window(ref, first, count, start):
        tile, shift = divmod(start, LANES)
        rows = slice(first, first + count)
        left = ref[rows, tile * LANES : (tile + 1) * LANES]
        if shift == 0:
            return left
        left = pltpu.roll(left, LANES - shift, 1)
        if (tile + 2) * LANES > KEPT:
            return left
        right = pltpu.roll(ref[rows, (tile + 1) * LANES : (tile + 2) * LANES], LANES - shift, 1)
        return jnp.where(lane_index(left.shape) < LANES - shift, left, right)

    sources = ((low, 0), (core, 40), (high, 80), (fresh, 120))

    def columns(first, start):
        ref, base = [source for source in sources if source[1] <= first][-1]
        return window(ref, first - base, PIX, start)

    lane = lane_index((PIX, LANES))
    for m in range(CHIPS):
        start = FIRST + m * CHIP_ROWS
        for ref, base in sources:
            count = UPDATES if base == WINDOW else 40
            out[m, base : base + count, :] = window(ref, 0, count, start)
        for r in range(REST // PIX):
            joined = None
            for q in range(4):
                first = q * REST + r * PIX
                if first >= COLS:
                    continue
                piece = columns(first, start + LANES - q * REST_LANES)
                joined = piece if joined is None else jnp.where(lane < q * REST_LANES, joined, piece)
            if COLS + r * PIX == META:
                joined = jnp.where(lane < META_LANE, joined, meta[...])
            out[m, COLS + r * PIX : COLS + (r + 1) * PIX, :] = joined


def sincos(x):
    n = jnp.floor(x * (2.0 / math.pi) + 0.5)
    r = x - n * 1.5703125
    r = r - n * 4.8351287841796875e-4
    r = r - n * 3.13855707645416259765625e-7
    r = r - n * 6.0771005065061922e-11
    q = n.astype(jnp.int32)
    z = r * r
    s = r + r * z * (-1.6666654611e-1 + z * (8.3321608736e-3 + z * -1.9515295891e-4))
    c = 1.0 - 0.5 * z + z * z * (4.166664568298827e-2 + z * (-1.388731625493765e-3 + z * 2.443315711809948e-5))
    swap = (q & 1) == 1
    sine = jnp.where(swap, c, s)
    cosine = jnp.where(swap, s, c)
    sine = jnp.where((q & 2) == 2, -sine, sine)
    cosine = jnp.where(((q + 1) & 2) == 2, -cosine, cosine)
    return sine, cosine


def sum_kernel(core, mine, keep, send, state, numbers, meta, arrived):
    lane = lane_index((40, LANES))
    side = core[0]
    for p in range(CHIPS):
        numbers[p] = mine[p, META : META + PIX, :].astype(jnp.int32)
    copy = pltpu.make_async_copy(numbers, meta, arrived)
    copy.start()

    def begin(p, carry):
        for q in range(4):
            first = q * REST
            count = min(REST, COLS - first)
            near = mine[p, first : first + count, :]
            left = pltpu.roll(near, LANES - BEHIND, 1)
            right = pltpu.roll(mine[p, COLS : COLS + count, :], (LANES - BEHIND - REST_LANES * q) % LANES, 1)
            state[p, first : first + count, :] = near
            state[p, TILE + first : TILE + first + count, :] = jnp.where(
                lane_index(left.shape) < LANES - BEHIND, left, right
            )
        return carry

    lax.fori_loop(0, CHIPS, begin, 0)
    copy.wait()

    def step(t, carry):
        for l in range(CHIPS):
            dst = pl.multiple_of(meta[l, 6, META_LANE + t], NEW_COLS)
            src = pl.multiple_of(WINDOW + t * NEW_COLS, NEW_COLS)
            for base in (0, TILE):
                state[l, pl.ds(base + dst, NEW_COLS), :] = state[l, pl.ds(base + src, NEW_COLS), :]
        acc = []
        for g in range(STARS):
            total = jnp.zeros((40, LANES), jnp.float32)
            for l in range(CHIPS):
                window = state[l, pl.ds(meta[l, g, META_LANE + t], 40), :]
                total = total + pltpu.roll(window, meta[l, g, TURN_LANE + t], 1)
            acc.append(total)
        for out, block in ((keep, side), (send, 1 - side)):
            for k in range(2):
                placed = [
                    pltpu.roll(acc[3 * k + j], lax.rem(LANES + 40 * j - 40 * block, LANES), 1) for j in range(3)
                ]
                joined = jnp.where(lane < 40, placed[0], jnp.where(lane < 80, placed[1], placed[2]))
                out[t, k * 40 : (k + 1) * 40, :] = joined
        return carry

    lax.fori_loop(0, STEPS, step, 0)


def spot_kernel(flags, here, there, lane_tab, recon, keep, send, flat_out, sums):
    side = flags[0]
    sums[...] = jnp.zeros_like(sums)
    weights = [ahead(d) for d in range(1, 5)]

    def spots(t):
        sine, cosine = sincos(here[t] + there[t])
        c1, c2 = parts(cosine, 2)
        s1, s2 = parts(sine, 2)
        head = jnp.concatenate([c1, s1], axis=1)
        tail = jnp.concatenate([c2, s2], axis=1)
        first = jnp.dot(jnp.concatenate([head, tail]), lane_tab[: 2 * LANES], preferred_element_type=jnp.float32)
        second = jnp.dot(head, lane_tab[2 * LANES :], preferred_element_type=jnp.float32)
        along = first[:80] + first[80:] + second
        z_y = sine * along[:, :LANES] + cosine * along[:, LANES:]

        c3 = cosine.reshape(10, PIX, LANES)
        s3 = sine.reshape(10, PIX, LANES)
        by_sine = -8.0 * s3
        by_cosine = -8.0 * c3
        for d in range(1, 5):
            weight = weights[d - 1][None]
            even = -8.0 if d == 4 else 16.0 * (-1.0) ** (d + 1)
            c_d = pltpu.roll(c3, d, 1)
            s_d = pltpu.roll(s3, d, 1)
            by_sine = by_sine + (weight * c_d + even * s_d)
            by_cosine = by_cosine + (even * c_d - weight * s_d)
        z_x = jnp.sum(s3 * by_sine + c3 * by_cosine, axis=1)
        z_y = jnp.sum(z_y.reshape(10, PIX, LANES), axis=1)
        for unit in range(10):
            sums[unit, pl.ds(t, 1), :] = z_x[unit : unit + 1]
            sums[10 + unit, pl.ds(t, 1), :] = z_y[unit : unit + 1]

    def step(t, carry):
        spots(t)
        return carry

    lax.fori_loop(0, STEPS, step, 0, unroll=2)

    units = 20
    stacked = jnp.concatenate(parts(sums[...].reshape(units * 16, LANES), 3))
    got = jnp.dot(stacked, group_table(), preferred_element_type=jnp.float32)
    size = units * 16
    got = (got[:size] + got[size : 2 * size]) + got[2 * size :]
    tiles = [jnp.zeros((16, LANES), jnp.float32) for _ in range(3)]
    for unit in range(units):
        tiles[unit // 8] = tiles[unit // 8] + pltpu.roll(got[unit * 16 : (unit + 1) * 16], (unit % 8) * 16, 1)
    flat = jnp.zeros((16, FLAT_PAD), jnp.float32)
    for i in range(3):
        moved = jnp.dot(
            jnp.concatenate(parts(tiles[i], 3)), order_table(i), preferred_element_type=jnp.float32
        )
        flat = flat + ((moved[:16] + moved[16:32]) + moved[32:])
    shown = lit(flags)
    flat = flat * jnp.concatenate([shown, shown])
    flat_out[...] = flat
    rounded = flat[:, :FLAT].astype(jnp.bfloat16)
    for out, half in ((keep, side), (send, 1 - side)):
        out[...] = jnp.zeros_like(out)
        for i in range(HALF_TILES):
            column = pl.multiple_of((half * HALF_TILES + i) * LANES, LANES)
            part = jnp.dot(rounded, recon[:, pl.ds(column, LANES)], preferred_element_type=jnp.float32)
            for slab, row, first, count in pieces(i):
                out[slab, row : row + count, :] = part[first : first + count]


def pieces(i):
    found = []
    first = 0
    while first < STEPS:
        slab, row = divmod(i * STEPS + first, SLAB_USED)
        count = min(STEPS - first, SLAB_USED - row)
        found.append((slab, row, first, count))
        first += count
    return found


def finish_kernel(core, mine, other, out):
    for ref, half in ((mine, core[0]), (other, 1 - core[0])):
        for i in range(HALF_TILES):
            column = pl.multiple_of((half * HALF_TILES + i) * LANES, LANES)
            for slab, row, first, count in pieces(i):
                out[first : first + count, pl.ds(column, LANES)] = ref[slab, row : row + count, :]


def vmem():
    return pl.BlockSpec(memory_space=pltpu.VMEM)


def smem():
    return pl.BlockSpec(memory_space=pltpu.SMEM)


def pack(low, core, high, fresh, meta):
    return pl.pallas_call(
        pack_kernel,
        out_shape=jax.ShapeDtypeStruct((CHIPS, PAYLOAD, LANES), jnp.float32),
        in_specs=[vmem()] * 5,
        out_specs=vmem(),
        compiler_params=pltpu.CompilerParams(vmem_limit_bytes=16 << 20),
    )(low, core, high, fresh, meta)


def partial_phases(core, mine):
    half = jax.ShapeDtypeStruct((STEPS, 10 * PIX, LANES), jnp.float32)
    return pl.pallas_call(
        sum_kernel,
        out_shape=(half, half),
        in_specs=[smem(), vmem()],
        out_specs=(vmem(), vmem()),
        scratch_shapes=[
            pltpu.VMEM((CHIPS, 2 * TILE, LANES), jnp.float32),
            pltpu.VMEM((CHIPS, PIX, LANES), jnp.int32),
            pltpu.SMEM((CHIPS, PIX, LANES), jnp.int32),
            pltpu.SemaphoreType.DMA(()),
        ],
        compiler_params=pltpu.CompilerParams(vmem_limit_bytes=16 << 20),
    )(core, mine)


def slopes_and_products(flags, here, there, recon):
    slab = jax.ShapeDtypeStruct((SLABS, SLAB_ROWS, LANES), jnp.float32)
    return pl.pallas_call(
        spot_kernel,
        out_shape=(slab, slab, jax.ShapeDtypeStruct((16, FLAT_PAD), jnp.float32)),
        in_specs=[smem()] + [vmem()] * 4,
        out_specs=(vmem(),) * 3,
        scratch_shapes=[pltpu.VMEM((20, 16, LANES), jnp.float32)],
        compiler_params=pltpu.CompilerParams(vmem_limit_bytes=16 << 20),
    )(flags, here, there, jnp.asarray(lane_table()), recon)


def finish(core, mine, other):
    return pl.pallas_call(
        finish_kernel,
        out_shape=jax.ShapeDtypeStruct((STEPS, ACTS), jnp.float32),
        in_specs=[smem(), vmem(), vmem()],
        out_specs=vmem(),
        compiler_params=pltpu.CompilerParams(vmem_limit_bytes=8 << 20),
    )(core, mine, other)


def groups_by(key):
    found = {}
    for device in range(256):
        layer, sub = divmod(device, 16)
        found.setdefault(key(layer // 8, layer // 2 % 4, layer % 2, sub // 4, sub % 4), []).append(device)
    return [found[name] for name in sorted(found)]


def exchange(blocks, groups):
    return lax.all_to_all(blocks, ("layer", "sub"), 0, 0, tiled=True, axis_index_groups=groups)


def to_all(block, groups):
    return exchange(jnp.broadcast_to(block[None], (len(groups[0]),) + block.shape), groups)


def to_other_core(block):
    return lax.ppermute(block, "layer", [(i, i ^ 1) for i in range(16)])


def local(screens, new_columns, col_block, shift_x, shift_y, valid, recon):
    owner = lax.axis_index("sub")
    count = lax.axis_size("sub")
    strips = jnp.transpose(screens[0], (0, 2, 1))
    fresh = jnp.transpose(new_columns[:, 0], (0, 2, 1))[:, :, LANE0 : LANE0 + KEPT].reshape(UPDATES, KEPT)

    def strip(turn):
        return lax.dynamic_slice(strips, (turn, 0, LANE0), (1, 40, KEPT))[0]

    core = strip(PUP_TURN)
    forward = [(i, (i + 1) % count) for i in range(count)]
    backward = [(target, source) for source, target in forward]
    low = lax.ppermute(strip(jnp.where(owner == count - 1, PUP_TURN - 1, PUP_TURN)), "sub", forward)
    high = lax.ppermute(strip(jnp.where(owner == 0, PUP_TURN + 1, PUP_TURN)), "sub", backward)

    offset = jnp.transpose(shift_y[:, 0]) + HALO
    behind = (offset > LANES - CHIP_ROWS).astype(jnp.int32)
    start = jnp.transpose(shift_x[:, 0]) + HALO + behind * TILE
    turn = (LANES - offset + behind * BEHIND) % LANES
    block = jnp.transpose(col_block) - (PUP_TURN * PUP // NEW_COLS) - (owner * 5 - 5)
    block = jnp.where((block >= 0) & (block < WINDOW // NEW_COLS), block, COLS // NEW_COLS) * NEW_COLS
    meta = (
        jnp.pad(start, ((0, 2), (META_LANE, LANES - META_LANE - STEPS)))
        + jnp.pad(turn, ((0, 2), (TURN_LANE, LANES - TURN_LANE - STEPS)))
        + jnp.pad(block, ((6, 1), (META_LANE, LANES - META_LANE - STEPS)))
    ).astype(jnp.float32)

    side = (lax.axis_index("layer") % 2).astype(jnp.int32).reshape(1)
    mine = exchange(pack(low, core, high, fresh, meta), groups_by(lambda zh, x, c, y, zl: (c, y, zl)))
    matrix = jnp.transpose(recon, (0, 2, 3, 1, 4)).reshape(FLAT, ACTS)
    flags = jnp.concatenate([side, valid.reshape(-1)])
    mine, matrix, flags = lax.optimization_barrier((mine, matrix, flags))
    here, there = partial_phases(side, mine)
    keep, send, flat = slopes_and_products(flags, here, to_other_core(there), matrix)

    plane = groups_by(lambda zh, x, c, y, zl: (c, zh, zl))
    column = groups_by(lambda zh, x, c, y, zl: (c, x, y))
    part = jnp.sum(exchange(keep + to_other_core(send), plane), axis=0)
    total = to_all(jnp.sum(to_all(part, column), axis=0), plane)
    commands = finish(side, total, to_other_core(total))
    slopes = jnp.transpose(flat[:STEPS, :FLAT].reshape(STEPS, STARS, 5, 5, 2), (0, 1, 4, 2, 3))
    return (slopes, commands)


def solution(mesh):
    return jax.shard_map(
        local,
        mesh=mesh,
        in_specs=(
            P("layer", None, None, "sub"),
            P(None, "layer", None, None),
            P(None, "layer"),
            P(None, "layer", None),
            P(None, "layer", None),
            P("layer", "sub"),
            P(None, None, "layer", "sub", None),
        ),
        out_specs=(P(None, None, None, "layer", "sub"), P()),
        check_vma=False,
    )
```

```python
import math
import jax
import jax.numpy as jnp
import numpy as np
from jax import lax
from jax.experimental import pallas as pl
from jax.experimental.pallas import tpu as pltpu
from jax.sharding import PartitionSpec as P

ACTS = 5376
HALO = 40
NEW_COLS = 8
PUP = 640
PUP_TURN = 3
ROW0 = 704
STEPS = 10
STARS = 6
PIX = 8
LANES = 128
LANE0 = 640
KEPT = 768
FIRST = ROW0 - HALO - LANE0
WINDOW = 120
UPDATES = STEPS * NEW_COLS
COLS = WINDOW + UPDATES
REST = 32
META = WINDOW + 24
PAYLOAD = WINDOW + REST
NEW_REST = 24
NEW_PAYLOAD = UPDATES + NEW_REST
HALF_LANES = 512
TILE = COLS + NEW_COLS
META_LANE = 96
TURN_LANE = 106
BEHIND = 32
CHIPS = 8
CHIP_ROWS = 80
REST_LANES = 32
HALF_TILES = 21
SLABS = 16
SLAB_USED = 14
SLAB_ROWS = 16
FLAT = 300
FLAT_PAD = 384


def toeplitz():
    d = np.arange(PIX)[:, None] - np.arange(PIX)[None, :]
    safe = np.where(d == 0, 1, d)
    return np.where(d == 0, 0.0, -4.0 * (-1.0) ** d / np.tan(np.pi * safe / 16))


def parts(value, count):
    found = []
    rest = value
    for _ in range(count):
        found.append(rest.astype(jnp.bfloat16))
        rest = rest - found[-1].astype(jnp.float32)
    return found


def ahead(d):
    t = toeplitz()
    x = lax.broadcasted_iota(jnp.int32, (PIX, LANES), 0)
    weight = jnp.zeros((PIX, LANES), jnp.float32)
    for i in range(PIX):
        weight = jnp.where(x == i, jnp.float32((2.0 if d == 4 else 4.0) * t[i, (i - d) % PIX]), weight)
    return weight


def lane_table():
    t = toeplitz()
    table = np.zeros((2 * LANES, 2 * LANES))
    y = np.arange(PIX)
    sign = (-1.0) ** (y[:, None] - y[None, :])
    for group in range(WINDOW // PIX):
        rows = slice(group * PIX, (group + 1) * PIX)
        after = slice(LANES + group * PIX, LANES + (group + 1) * PIX)
        table[rows, rows] = 4.0 * t.T
        table[after, rows] = -8.0 * sign
        table[rows, after] = -8.0 * sign
    first = table.astype(jnp.bfloat16)
    second = (table - first.astype(np.float64)).astype(jnp.bfloat16)
    return np.concatenate([first, second])


def group_table():
    lane = lax.broadcasted_iota(jnp.int32, (LANES, LANES), 0)
    group = lax.broadcasted_iota(jnp.int32, (LANES, LANES), 1)
    first = group * PIX
    return jnp.where((lane >= first) & (lane < first + PIX) & (lane < WINDOW), 1.0 / 1024, 0.0).astype(jnp.bfloat16)


def multiple(value, step, count):
    found = jnp.zeros_like(value)
    for i in range(1, count + 1):
        found = found + (value >= step * i).astype(jnp.int32)
    return found


def order_table(tile):
    row = lax.broadcasted_iota(jnp.int32, (LANES, LANES), 0) + tile * LANES
    column = lax.broadcasted_iota(jnp.int32, (LANES, LANES), 1)
    unit = lax.shift_right_logical(row, 4)
    place = row & 15
    s = multiple(unit, 10, 1)
    k = multiple(unit - 10 * s, 5, 1)
    b = unit - 10 * s - 5 * k
    kk = multiple(place, 5, 2)
    target = (((3 * k + kk) * 5 + place - 5 * kk) * 5 + b) * 2 + s
    target = jnp.where((place < 15) & (unit < 20), target, -1)
    blocks = [(target == column + i * LANES).astype(jnp.float32).astype(jnp.bfloat16) for i in range(FLAT_PAD // LANES)]
    return jnp.concatenate(blocks, axis=1)


def lit(flags):
    place = lax.shift_right_logical(lax.broadcasted_iota(jnp.int32, (8, FLAT_PAD), 1), 1)
    place = place - 25 * multiple(place, 25, 7)
    found = jnp.zeros((8, FLAT_PAD), jnp.float32)
    for a in range(5):
        for b in range(5):
            found = jnp.where(place == a * 5 + b, flags[1 + a * 5 + b].astype(jnp.float32), found)
    return found


def lane_index(shape):
    return lax.broadcasted_iota(jnp.int32, shape, len(shape) - 1)


def pack_kernel(low, core, high, meta, out):
    def window(ref, first, count, start):
        tile, shift = divmod(start, LANES)
        rows = slice(first, first + count)
        left = ref[rows, tile * LANES : (tile + 1) * LANES]
        if shift == 0:
            return left
        left = pltpu.roll(left, LANES - shift, 1)
        if (tile + 2) * LANES > KEPT:
            return left
        right = pltpu.roll(ref[rows, (tile + 1) * LANES : (tile + 2) * LANES], LANES - shift, 1)
        return jnp.where(lane_index(left.shape) < LANES - shift, left, right)

    sources = ((low, 0), (core, 40), (high, 80))

    def columns(first, start):
        ref, base = [source for source in sources if source[1] <= first][-1]
        return window(ref, first - base, PIX, start)

    lane = lane_index((PIX, LANES))
    for m in range(CHIPS):
        start = FIRST + m * CHIP_ROWS
        for ref, base in sources:
            out[m, base : base + 40, :] = window(ref, 0, 40, start)
        for r in range(REST // PIX):
            joined = None
            for q in range(4):
                first = q * REST + r * PIX
                if first >= WINDOW:
                    continue
                piece = columns(first, start + LANES - q * REST_LANES)
                joined = piece if joined is None else jnp.where(lane < q * REST_LANES, joined, piece)
            if WINDOW + r * PIX == META:
                joined = jnp.where(lane < META_LANE, joined, meta[...])
            out[m, WINDOW + r * PIX : WINDOW + (r + 1) * PIX, :] = joined


def hand_kernel(place, own, partner, *outs):
    lane = lane_index((PIX, LANES))

    def window(ref, first, count, start):
        tile = lax.shift_right_logical(start, 7)
        cut = LANES - (start & (LANES - 1))
        turn = cut & (LANES - 1)
        rows = slice(first, first + count)
        after = jnp.minimum(tile + 1, HALF_LANES // LANES - 1)
        left = pltpu.roll(ref[rows, pl.ds(pl.multiple_of(tile * LANES, LANES), LANES)], turn, 1)
        right = pltpu.roll(ref[rows, pl.ds(pl.multiple_of(after * LANES, LANES), LANES)], turn, 1)
        return jnp.where(lane_index(left.shape) < cut, left, right)

    for d, out in enumerate(outs):
        start = FIRST + 64 * place[2] + CHIP_ROWS * ((place[1] + d) & 3)
        for w, ref in enumerate((own, partner)):
            base = w * NEW_PAYLOAD
            out[base : base + UPDATES, :] = window(ref, 0, UPDATES, start)
            for r in range(NEW_REST // PIX):
                joined = None
                for q in range(4):
                    first = q * NEW_REST + r * PIX
                    if first >= UPDATES:
                        continue
                    piece = window(ref, first, PIX, start + LANES - q * REST_LANES)
                    joined = piece if joined is None else jnp.where(lane < q * REST_LANES, joined, piece)
                out[base + UPDATES + r * PIX : base + UPDATES + (r + 1) * PIX, :] = joined


def sincos(x):
    n = jnp.floor(x * (2.0 / math.pi) + 0.5)
    r = x - n * 1.5703125
    r = r - n * 4.8351287841796875e-4
    r = r - n * 3.13855707645416259765625e-7
    r = r - n * 6.0771005065061922e-11
    q = n.astype(jnp.int32)
    z = r * r
    s = r + r * z * (-1.6666654611e-1 + z * (8.3321608736e-3 + z * -1.9515295891e-4))
    c = 1.0 - 0.5 * z + z * z * (4.166664568298827e-2 + z * (-1.388731625493765e-3 + z * 2.443315711809948e-5))
    swap = (q & 1) == 1
    sine = jnp.where(swap, c, s)
    cosine = jnp.where(swap, s, c)
    sine = jnp.where((q & 2) == 2, -sine, sine)
    cosine = jnp.where(((q + 1) & 2) == 2, -cosine, cosine)
    return sine, cosine


def sum_kernel(place, mine, new_0, new_1, new_2, new_3, keep, send, state, numbers, meta, arrived):
    lane = lane_index((40, LANES))
    side = place[0]
    for p in range(CHIPS):
        numbers[p] = mine[p, META : META + PIX, :].astype(jnp.int32)
    copy = pltpu.make_async_copy(numbers, meta, arrived)
    copy.start()

    def unpack(p, target, near, rest, q):
        count = near.shape[0]
        left = pltpu.roll(near, LANES - BEHIND, 1)
        right = pltpu.roll(rest, (LANES - BEHIND - REST_LANES * q) % LANES, 1)
        state[p, target : target + count, :] = near
        state[p, TILE + target : TILE + target + count, :] = jnp.where(
            lane_index(left.shape) < LANES - BEHIND, left, right
        )

    def begin(p, carry):
        for q in range(4):
            first = q * REST
            count = min(REST, WINDOW - first)
            unpack(p, first, mine[p, first : first + count, :], mine[p, WINDOW : WINDOW + count, :], q)
        return carry

    lax.fori_loop(0, CHIPS, begin, 0)
    for d, ref in enumerate((new_0, new_1, new_2, new_3)):
        for w in range(2):
            half = place[2] if w == 0 else 1 - place[2]
            p = half * 4 + ((place[1] + 4 - d) & 3)
            base = w * NEW_PAYLOAD
            for q in range(4):
                first = q * NEW_REST
                count = min(NEW_REST, UPDATES - first)
                near = ref[base + first : base + first + count, :]
                unpack(p, WINDOW + first, near, ref[base + UPDATES : base + UPDATES + count, :], q)
    copy.wait()

    def step(t, carry):
        for l in range(CHIPS):
            dst = pl.multiple_of(meta[l, 6, META_LANE + t], NEW_COLS)
            src = pl.multiple_of(WINDOW + t * NEW_COLS, NEW_COLS)
            for base in (0, TILE):
                state[l, pl.ds(base + dst, NEW_COLS), :] = state[l, pl.ds(base + src, NEW_COLS), :]
        acc = []
        for g in range(STARS):
            total = jnp.zeros((40, LANES), jnp.float32)
            for l in range(CHIPS):
                window = state[l, pl.ds(meta[l, g, META_LANE + t], 40), :]
                total = total + pltpu.roll(window, meta[l, g, TURN_LANE + t], 1)
            acc.append(total)
        for out, block in ((keep, side), (send, 1 - side)):
            for k in range(2):
                placed = [
                    pltpu.roll(acc[3 * k + j], lax.rem(LANES + 40 * j - 40 * block, LANES), 1) for j in range(3)
                ]
                joined = jnp.where(lane < 40, placed[0], jnp.where(lane < 80, placed[1], placed[2]))
                out[t, k * 40 : (k + 1) * 40, :] = joined
        return carry

    lax.fori_loop(0, STEPS, step, 0)


def spot_kernel(flags, here, there, lane_tab, recon, keep, send, flat_out, sums):
    side = flags[0]
    sums[...] = jnp.zeros_like(sums)
    weights = [ahead(d) for d in range(1, 5)]

    def spots(t):
        sine, cosine = sincos(here[t] + there[t])
        c1, c2 = parts(cosine, 2)
        s1, s2 = parts(sine, 2)
        head = jnp.concatenate([c1, s1], axis=1)
        tail = jnp.concatenate([c2, s2], axis=1)
        first = jnp.dot(jnp.concatenate([head, tail]), lane_tab[: 2 * LANES], preferred_element_type=jnp.float32)
        second = jnp.dot(head, lane_tab[2 * LANES :], preferred_element_type=jnp.float32)
        along = first[:80] + first[80:] + second
        z_y = sine * along[:, :LANES] + cosine * along[:, LANES:]

        c3 = cosine.reshape(10, PIX, LANES)
        s3 = sine.reshape(10, PIX, LANES)
        by_sine = -8.0 * s3
        by_cosine = -8.0 * c3
        for d in range(1, 5):
            weight = weights[d - 1][None]
            even = -8.0 if d == 4 else 16.0 * (-1.0) ** (d + 1)
            c_d = pltpu.roll(c3, d, 1)
            s_d = pltpu.roll(s3, d, 1)
            by_sine = by_sine + (weight * c_d + even * s_d)
            by_cosine = by_cosine + (even * c_d - weight * s_d)
        z_x = jnp.sum(s3 * by_sine + c3 * by_cosine, axis=1)
        z_y = jnp.sum(z_y.reshape(10, PIX, LANES), axis=1)
        for unit in range(10):
            sums[unit, pl.ds(t, 1), :] = z_x[unit : unit + 1]
            sums[10 + unit, pl.ds(t, 1), :] = z_y[unit : unit + 1]

    def step(t, carry):
        spots(t)
        return carry

    lax.fori_loop(0, STEPS, step, 0, unroll=2)

    units = 20
    stacked = jnp.concatenate(parts(sums[...].reshape(units * 16, LANES), 3))
    got = jnp.dot(stacked, group_table(), preferred_element_type=jnp.float32)
    size = units * 16
    got = (got[:size] + got[size : 2 * size]) + got[2 * size :]
    tiles = [jnp.zeros((16, LANES), jnp.float32) for _ in range(3)]
    for unit in range(units):
        tiles[unit // 8] = tiles[unit // 8] + pltpu.roll(got[unit * 16 : (unit + 1) * 16], (unit % 8) * 16, 1)
    flat = jnp.zeros((16, FLAT_PAD), jnp.float32)
    for i in range(3):
        moved = jnp.dot(
            jnp.concatenate(parts(tiles[i], 3)), order_table(i), preferred_element_type=jnp.float32
        )
        flat = flat + ((moved[:16] + moved[16:32]) + moved[32:])
    shown = lit(flags)
    flat = flat * jnp.concatenate([shown, shown])
    flat_out[...] = flat
    rounded = flat[:, :FLAT].astype(jnp.bfloat16)
    for out, half in ((keep, side), (send, 1 - side)):
        out[...] = jnp.zeros_like(out)
        for i in range(HALF_TILES):
            column = pl.multiple_of((half * HALF_TILES + i) * LANES, LANES)
            part = jnp.dot(rounded, recon[:, pl.ds(column, LANES)], preferred_element_type=jnp.float32)
            for slab, row, first, count in pieces(i):
                out[slab, row : row + count, :] = part[first : first + count]


def pieces(i):
    found = []
    first = 0
    while first < STEPS:
        slab, row = divmod(i * STEPS + first, SLAB_USED)
        count = min(STEPS - first, SLAB_USED - row)
        found.append((slab, row, first, count))
        first += count
    return found


def finish_kernel(core, mine, other, out):
    for ref, half in ((mine, core[0]), (other, 1 - core[0])):
        for i in range(HALF_TILES):
            column = pl.multiple_of((half * HALF_TILES + i) * LANES, LANES)
            for slab, row, first, count in pieces(i):
                out[first : first + count, pl.ds(column, LANES)] = ref[slab, row : row + count, :]


def vmem():
    return pl.BlockSpec(memory_space=pltpu.VMEM)


def smem():
    return pl.BlockSpec(memory_space=pltpu.SMEM)


def pack(low, core, high, meta):
    return pl.pallas_call(
        pack_kernel,
        out_shape=jax.ShapeDtypeStruct((CHIPS, PAYLOAD, LANES), jnp.float32),
        in_specs=[vmem()] * 4,
        out_specs=vmem(),
        compiler_params=pltpu.CompilerParams(vmem_limit_bytes=16 << 20),
    )(low, core, high, meta)


def hand(place, own, partner):
    return pl.pallas_call(
        hand_kernel,
        out_shape=(jax.ShapeDtypeStruct((2 * NEW_PAYLOAD, LANES), jnp.float32),) * 4,
        in_specs=[smem(), vmem(), vmem()],
        out_specs=(vmem(),) * 4,
        compiler_params=pltpu.CompilerParams(vmem_limit_bytes=8 << 20),
    )(place, own, partner)


def partial_phases(place, mine, news):
    half = jax.ShapeDtypeStruct((STEPS, 10 * PIX, LANES), jnp.float32)
    return pl.pallas_call(
        sum_kernel,
        out_shape=(half, half),
        in_specs=[smem()] + [vmem()] * 5,
        out_specs=(vmem(), vmem()),
        scratch_shapes=[
            pltpu.VMEM((CHIPS, 2 * TILE, LANES), jnp.float32),
            pltpu.VMEM((CHIPS, PIX, LANES), jnp.int32),
            pltpu.SMEM((CHIPS, PIX, LANES), jnp.int32),
            pltpu.SemaphoreType.DMA(()),
        ],
        compiler_params=pltpu.CompilerParams(vmem_limit_bytes=16 << 20),
    )(place, mine, *news)


def slopes_and_products(flags, here, there, recon):
    slab = jax.ShapeDtypeStruct((SLABS, SLAB_ROWS, LANES), jnp.float32)
    return pl.pallas_call(
        spot_kernel,
        out_shape=(slab, slab, jax.ShapeDtypeStruct((16, FLAT_PAD), jnp.float32)),
        in_specs=[smem()] + [vmem()] * 4,
        out_specs=(vmem(),) * 3,
        scratch_shapes=[pltpu.VMEM((20, 16, LANES), jnp.float32)],
        compiler_params=pltpu.CompilerParams(vmem_limit_bytes=16 << 20),
    )(flags, here, there, jnp.asarray(lane_table()), recon)


def finish(core, mine, other):
    return pl.pallas_call(
        finish_kernel,
        out_shape=jax.ShapeDtypeStruct((STEPS, ACTS), jnp.float32),
        in_specs=[smem(), vmem(), vmem()],
        out_specs=vmem(),
        compiler_params=pltpu.CompilerParams(vmem_limit_bytes=8 << 20),
    )(core, mine, other)


def groups_by(key):
    found = {}
    for device in range(256):
        layer, sub = divmod(device, 16)
        found.setdefault(key(layer // 8, layer // 2 % 4, layer % 2, sub // 4, sub % 4), []).append(device)
    return [found[name] for name in sorted(found)]


def exchange(blocks, groups):
    return lax.all_to_all(blocks, ("layer", "sub"), 0, 0, tiled=True, axis_index_groups=groups)


def to_all(block, groups):
    return exchange(jnp.broadcast_to(block[None], (len(groups[0]),) + block.shape), groups)


def to_other_core(block):
    return lax.ppermute(block, "layer", [(i, i ^ 1) for i in range(16)])


def local(screens, new_columns, col_block, shift_x, shift_y, valid, recon):
    owner = lax.axis_index("sub")
    count = lax.axis_size("sub")
    strips = jnp.transpose(screens[0], (0, 2, 1))
    fresh = jnp.transpose(new_columns[:, 0], (0, 2, 1))
    layer = lax.axis_index("layer").astype(jnp.int32)
    half = layer // 8

    def new_rows(part):
        at = LANE0 + part * (KEPT - HALF_LANES)
        return lax.dynamic_slice(fresh, (0, 0, at), (STEPS, NEW_COLS, HALF_LANES)).reshape(UPDATES, HALF_LANES)

    def strip(turn):
        return lax.dynamic_slice(strips, (turn, 0, LANE0), (1, 40, KEPT))[0]

    core = strip(PUP_TURN)
    forward = [(i, (i + 1) % count) for i in range(count)]
    backward = [(target, source) for source, target in forward]
    low = lax.ppermute(strip(jnp.where(owner == count - 1, PUP_TURN - 1, PUP_TURN)), "sub", forward)
    high = lax.ppermute(strip(jnp.where(owner == 0, PUP_TURN + 1, PUP_TURN)), "sub", backward)

    partner = lax.ppermute(new_rows(1 - half), "layer", [(i, i ^ 8) for i in range(16)])

    offset = jnp.transpose(shift_y[:, 0]) + HALO
    behind = (offset > LANES - CHIP_ROWS).astype(jnp.int32)
    start = jnp.transpose(shift_x[:, 0]) + HALO + behind * TILE
    turn = (LANES - offset + behind * BEHIND) % LANES
    block = jnp.transpose(col_block) - (PUP_TURN * PUP // NEW_COLS) - (owner * 5 - 5)
    block = jnp.where((block >= 0) & (block < WINDOW // NEW_COLS), block, COLS // NEW_COLS) * NEW_COLS
    meta = (
        jnp.pad(start, ((0, 2), (META_LANE, LANES - META_LANE - STEPS)))
        + jnp.pad(turn, ((0, 2), (TURN_LANE, LANES - TURN_LANE - STEPS)))
        + jnp.pad(block, ((6, 1), (META_LANE, LANES - META_LANE - STEPS)))
    ).astype(jnp.float32)

    side = (layer % 2).reshape(1)
    place = jnp.stack([layer % 2, layer // 2 % 4, half])
    payload, partner = lax.optimization_barrier((pack(low, core, high, meta), partner))
    mine = exchange(payload, groups_by(lambda zh, x, c, y, zl: (c, y, zl)))
    *news, recon = lax.optimization_barrier((*hand(place, new_rows(half), partner), recon))
    for d in range(1, 4):
        along = [(i, i // 8 * 8 + (i % 8 + 2 * d) % 8) for i in range(16)]
        news[d] = lax.ppermute(news[d], "layer", along)
    matrix = jnp.transpose(recon, (0, 2, 3, 1, 4)).reshape(FLAT, ACTS)
    flags = jnp.concatenate([side, valid.reshape(-1)])
    mine, matrix, flags = lax.optimization_barrier((mine, matrix, flags))
    here, there = partial_phases(place, mine, news)
    keep, send, flat = slopes_and_products(flags, here, to_other_core(there), matrix)

    plane = groups_by(lambda zh, x, c, y, zl: (c, zh, zl))
    column = groups_by(lambda zh, x, c, y, zl: (c, x, y))
    part = jnp.sum(exchange(keep + to_other_core(send), plane), axis=0)
    total = to_all(jnp.sum(to_all(part, column), axis=0), plane)
    commands = finish(side, total, to_other_core(total))
    slopes = jnp.transpose(flat[:STEPS, :FLAT].reshape(STEPS, STARS, 5, 5, 2), (0, 1, 4, 2, 3))
    return (slopes, commands)


def solution(mesh):
    return jax.shard_map(
        local,
        mesh=mesh,
        in_specs=(
            P("layer", None, None, "sub"),
            P(None, "layer", None, None),
            P(None, "layer"),
            P(None, "layer", None),
            P(None, "layer", None),
            P("layer", "sub"),
            P(None, None, "layer", "sub", None),
        ),
        out_specs=(P(None, None, None, "layer", "sub"), P()),
        check_vma=False,
    )
```

```python
import math
import jax
import jax.numpy as jnp
import numpy as np
from jax import lax
from jax.experimental import pallas as pl
from jax.experimental.pallas import tpu as pltpu
from jax.sharding import PartitionSpec as P

ACTS = 5376
HALO = 40
NEW_COLS = 8
PUP = 640
PUP_TURN = 3
ROW0 = 704
STEPS = 10
STARS = 6
PIX = 8
LANES = 128
LANE0 = 640
KEPT = 768
FIRST = ROW0 - HALO - LANE0
WINDOW = 120
UPDATES = STEPS * NEW_COLS
COLS = WINDOW + UPDATES
REST = 32
META = WINDOW + 24
PAYLOAD = WINDOW + REST
NEW_REST = 24
NEW_PAYLOAD = UPDATES + NEW_REST
HALF_LANES = 512
TILE = COLS + NEW_COLS
META_LANE = 96
TURN_LANE = 106
BEHIND = 32
CHIPS = 8
CHIP_ROWS = 80
REST_LANES = 32
HALF_TILES = 21
SLABS = 16
SLAB_USED = 14
SLAB_ROWS = 16
FLAT = 300
FLAT_PAD = 384


def toeplitz():
    d = np.arange(PIX)[:, None] - np.arange(PIX)[None, :]
    safe = np.where(d == 0, 1, d)
    return np.where(d == 0, 0.0, -4.0 * (-1.0) ** d / np.tan(np.pi * safe / 16))


def parts(value, count):
    found = []
    rest = value
    for _ in range(count):
        found.append(rest.astype(jnp.bfloat16))
        rest = rest - found[-1].astype(jnp.float32)
    return found


def ahead(d):
    t = toeplitz()
    x = lax.broadcasted_iota(jnp.int32, (PIX, LANES), 0)
    weight = jnp.zeros((PIX, LANES), jnp.float32)
    for i in range(PIX):
        weight = jnp.where(x == i, jnp.float32((2.0 if d == 4 else 4.0) * t[i, (i - d) % PIX]), weight)
    return weight


def lane_table():
    t = toeplitz()
    row = lax.broadcasted_iota(jnp.int32, (LANES, LANES), 0)
    column = lax.broadcasted_iota(jnp.int32, (LANES, LANES), 1)
    same = (lax.shift_right_logical(row, 3) == lax.shift_right_logical(column, 3)) & (row < WINDOW)
    ahead_by = jnp.where(same, column - row, LANES)
    value = jnp.zeros((LANES, LANES), jnp.float32)
    for d in range(1, PIX):
        for step in (d, -d):
            value = jnp.where(ahead_by == step, jnp.float32(4.0 * t[max(step, 0), max(-step, 0)]), value)
    sign = jnp.where(same, jnp.where((ahead_by & 1) == 0, -8.0, 8.0), 0.0).astype(jnp.bfloat16)
    main, rest = parts(value, 2)
    left = jnp.concatenate([main, sign], axis=0)
    right = jnp.concatenate([sign, jnp.zeros_like(sign)], axis=0)
    return jnp.concatenate([left, right], axis=1), rest


def group_table():
    lane = lax.broadcasted_iota(jnp.int32, (LANES, LANES), 0)
    group = lax.broadcasted_iota(jnp.int32, (LANES, LANES), 1)
    first = group * PIX
    return jnp.where((lane >= first) & (lane < first + PIX) & (lane < WINDOW), 1.0 / 1024, 0.0).astype(jnp.bfloat16)


def multiple(value, step, count):
    found = jnp.zeros_like(value)
    for i in range(1, count + 1):
        found = found + (value >= step * i).astype(jnp.int32)
    return found


def order_table(tile):
    row = lax.broadcasted_iota(jnp.int32, (LANES, LANES), 0) + tile * LANES
    column = lax.broadcasted_iota(jnp.int32, (LANES, LANES), 1)
    unit = lax.shift_right_logical(row, 4)
    place = row & 15
    s = multiple(unit, 10, 1)
    k = multiple(unit - 10 * s, 5, 1)
    b = unit - 10 * s - 5 * k
    kk = multiple(place, 5, 2)
    target = (((3 * k + kk) * 5 + place - 5 * kk) * 5 + b) * 2 + s
    target = jnp.where((place < 15) & (unit < 20), target, -1)
    blocks = [(target == column + i * LANES).astype(jnp.float32).astype(jnp.bfloat16) for i in range(FLAT_PAD // LANES)]
    return jnp.concatenate(blocks, axis=1)


def lit(flags):
    place = lax.shift_right_logical(lax.broadcasted_iota(jnp.int32, (8, FLAT_PAD), 1), 1)
    place = place - 25 * multiple(place, 25, 7)
    found = jnp.zeros((8, FLAT_PAD), jnp.float32)
    for a in range(5):
        for b in range(5):
            found = jnp.where(place == a * 5 + b, flags[1 + a * 5 + b].astype(jnp.float32), found)
    return found


def lane_index(shape):
    return lax.broadcasted_iota(jnp.int32, shape, len(shape) - 1)


def pack_kernel(low, core, high, meta, out):
    def window(ref, first, count, start):
        tile, shift = divmod(start, LANES)
        rows = slice(first, first + count)
        left = ref[rows, tile * LANES : (tile + 1) * LANES]
        if shift == 0:
            return left
        left = pltpu.roll(left, LANES - shift, 1)
        if (tile + 2) * LANES > KEPT:
            return left
        right = pltpu.roll(ref[rows, (tile + 1) * LANES : (tile + 2) * LANES], LANES - shift, 1)
        return jnp.where(lane_index(left.shape) < LANES - shift, left, right)

    sources = ((low, 0), (core, 40), (high, 80))

    def columns(first, start):
        ref, base = [source for source in sources if source[1] <= first][-1]
        return window(ref, first - base, PIX, start)

    lane = lane_index((PIX, LANES))
    for m in range(CHIPS):
        start = FIRST + m * CHIP_ROWS
        for ref, base in sources:
            out[m, base : base + 40, :] = window(ref, 0, 40, start)
        for r in range(REST // PIX):
            joined = None
            for q in range(4):
                first = q * REST + r * PIX
                if first >= WINDOW:
                    continue
                piece = columns(first, start + LANES - q * REST_LANES)
                joined = piece if joined is None else jnp.where(lane < q * REST_LANES, joined, piece)
            if WINDOW + r * PIX == META:
                joined = jnp.where(lane < META_LANE, joined, meta[...])
            out[m, WINDOW + r * PIX : WINDOW + (r + 1) * PIX, :] = joined


def hand_kernel(place, own, partner, *outs):
    lane = lane_index((PIX, LANES))

    def window(ref, first, count, start):
        tile = lax.shift_right_logical(start, 7)
        cut = LANES - (start & (LANES - 1))
        turn = cut & (LANES - 1)
        rows = slice(first, first + count)
        after = jnp.minimum(tile + 1, HALF_LANES // LANES - 1)
        left = pltpu.roll(ref[rows, pl.ds(pl.multiple_of(tile * LANES, LANES), LANES)], turn, 1)
        right = pltpu.roll(ref[rows, pl.ds(pl.multiple_of(after * LANES, LANES), LANES)], turn, 1)
        return jnp.where(lane_index(left.shape) < cut, left, right)

    for d, out in enumerate(outs):
        start = FIRST + 64 * place[2] + CHIP_ROWS * ((place[1] + d) & 3)
        for w, ref in enumerate((own, partner)):
            base = w * NEW_PAYLOAD
            out[base : base + UPDATES, :] = window(ref, 0, UPDATES, start)
            for r in range(NEW_REST // PIX):
                joined = None
                for q in range(4):
                    first = q * NEW_REST + r * PIX
                    if first >= UPDATES:
                        continue
                    piece = window(ref, first, PIX, start + LANES - q * REST_LANES)
                    joined = piece if joined is None else jnp.where(lane < q * REST_LANES, joined, piece)
                out[base + UPDATES + r * PIX : base + UPDATES + (r + 1) * PIX, :] = joined


def sincos(x):
    n = jnp.floor(x * (2.0 / math.pi) + 0.5)
    r = x - n * 1.5703125
    r = r - n * 4.8351287841796875e-4
    r = r - n * 3.13855707645416259765625e-7
    r = r - n * 6.0771005065061922e-11
    q = n.astype(jnp.int32)
    z = r * r
    s = r + r * z * (-1.6666654611e-1 + z * (8.3321608736e-3 + z * -1.9515295891e-4))
    c = 1.0 - 0.5 * z + z * z * (4.166664568298827e-2 + z * (-1.388731625493765e-3 + z * 2.443315711809948e-5))
    swap = (q & 1) == 1
    sine = jnp.where(swap, c, s)
    cosine = jnp.where(swap, s, c)
    sine = jnp.where((q & 2) == 2, -sine, sine)
    cosine = jnp.where(((q + 1) & 2) == 2, -cosine, cosine)
    return sine, cosine


def sum_kernel(place, mine, new_0, new_1, new_2, new_3, keep, send, state, numbers, meta, arrived):
    lane = lane_index((40, LANES))
    side = place[0]
    for p in range(CHIPS):
        numbers[p] = mine[p, META : META + PIX, :].astype(jnp.int32)
    copy = pltpu.make_async_copy(numbers, meta, arrived)
    copy.start()

    def unpack(p, target, near, rest, q):
        count = near.shape[0]
        left = pltpu.roll(near, LANES - BEHIND, 1)
        right = pltpu.roll(rest, (LANES - BEHIND - REST_LANES * q) % LANES, 1)
        state[p, target : target + count, :] = near
        state[p, TILE + target : TILE + target + count, :] = jnp.where(
            lane_index(left.shape) < LANES - BEHIND, left, right
        )

    def begin(p, carry):
        for q in range(4):
            first = q * REST
            count = min(REST, WINDOW - first)
            unpack(p, first, mine[p, first : first + count, :], mine[p, WINDOW : WINDOW + count, :], q)
        return carry

    lax.fori_loop(0, CHIPS, begin, 0)
    for d, ref in enumerate((new_0, new_1, new_2, new_3)):
        for w in range(2):
            half = place[2] if w == 0 else 1 - place[2]
            p = half * 4 + ((place[1] + 4 - d) & 3)
            base = w * NEW_PAYLOAD
            for q in range(4):
                first = q * NEW_REST
                count = min(NEW_REST, UPDATES - first)
                near = ref[base + first : base + first + count, :]
                unpack(p, WINDOW + first, near, ref[base + UPDATES : base + UPDATES + count, :], q)
    copy.wait()

    def step(t, carry):
        for l in range(CHIPS):
            dst = pl.multiple_of(meta[l, 6, META_LANE + t], NEW_COLS)
            src = pl.multiple_of(WINDOW + t * NEW_COLS, NEW_COLS)
            for base in (0, TILE):
                state[l, pl.ds(base + dst, NEW_COLS), :] = state[l, pl.ds(base + src, NEW_COLS), :]
        acc = []
        for g in range(STARS):
            total = jnp.zeros((40, LANES), jnp.float32)
            for l in range(CHIPS):
                window = state[l, pl.ds(meta[l, g, META_LANE + t], 40), :]
                total = total + pltpu.roll(window, meta[l, g, TURN_LANE + t], 1)
            acc.append(total)
        for out, block in ((keep, side), (send, 1 - side)):
            for k in range(2):
                placed = [
                    pltpu.roll(acc[3 * k + j], lax.rem(LANES + 40 * j - 40 * block, LANES), 1) for j in range(3)
                ]
                joined = jnp.where(lane < 40, placed[0], jnp.where(lane < 80, placed[1], placed[2]))
                out[t, k * 40 : (k + 1) * 40, :] = joined
        return carry

    lax.fori_loop(0, STEPS, step, 0)


def spot_kernel(flags, here, there, recon, keep, send, flat_out, sums, lane_tab, lane_rest):
    side = flags[0]
    sums[...] = jnp.zeros_like(sums)
    weights = [ahead(d) for d in range(1, 5)]
    lane_tab[...], lane_rest[...] = lane_table()

    def spots(t):
        sine, cosine = sincos(here[t] + there[t])
        c1, c2 = parts(cosine, 2)
        s1, s2 = parts(sine, 2)
        head = jnp.concatenate([c1, s1], axis=1)
        tail = jnp.concatenate([c2, s2], axis=1)
        first = jnp.dot(jnp.concatenate([head, tail]), lane_tab[...], preferred_element_type=jnp.float32)
        second = jnp.dot(c1, lane_rest[...], preferred_element_type=jnp.float32)
        along = first[:80] + first[80:]
        z_y = sine * (along[:, :LANES] + second) + cosine * along[:, LANES:]

        c3 = cosine.reshape(10, PIX, LANES)
        s3 = sine.reshape(10, PIX, LANES)
        by_sine = -8.0 * s3
        by_cosine = -8.0 * c3
        for d in range(1, 5):
            weight = weights[d - 1][None]
            even = -8.0 if d == 4 else 16.0 * (-1.0) ** (d + 1)
            c_d = pltpu.roll(c3, d, 1)
            s_d = pltpu.roll(s3, d, 1)
            by_sine = by_sine + (weight * c_d + even * s_d)
            by_cosine = by_cosine + (even * c_d - weight * s_d)
        z_x = jnp.sum(s3 * by_sine + c3 * by_cosine, axis=1)
        z_y = jnp.sum(z_y.reshape(10, PIX, LANES), axis=1)
        for unit in range(10):
            sums[unit, pl.ds(t, 1), :] = z_x[unit : unit + 1]
            sums[10 + unit, pl.ds(t, 1), :] = z_y[unit : unit + 1]

    def step(t, carry):
        spots(t)
        return carry

    lax.fori_loop(0, STEPS, step, 0, unroll=2)

    units = 20
    stacked = jnp.concatenate(parts(sums[...].reshape(units * 16, LANES), 3))
    got = jnp.dot(stacked, group_table(), preferred_element_type=jnp.float32)
    size = units * 16
    got = (got[:size] + got[size : 2 * size]) + got[2 * size :]
    tiles = [jnp.zeros((16, LANES), jnp.float32) for _ in range(3)]
    for unit in range(units):
        tiles[unit // 8] = tiles[unit // 8] + pltpu.roll(got[unit * 16 : (unit + 1) * 16], (unit % 8) * 16, 1)
    flat = jnp.zeros((16, FLAT_PAD), jnp.float32)
    for i in range(3):
        moved = jnp.dot(
            jnp.concatenate(parts(tiles[i], 3)), order_table(i), preferred_element_type=jnp.float32
        )
        flat = flat + ((moved[:16] + moved[16:32]) + moved[32:])
    shown = lit(flags)
    flat = flat * jnp.concatenate([shown, shown])
    flat_out[...] = flat
    rounded = flat[:, :FLAT].astype(jnp.bfloat16)
    for out, half in ((keep, side), (send, 1 - side)):
        out[...] = jnp.zeros_like(out)
        for i in range(HALF_TILES):
            column = pl.multiple_of((half * HALF_TILES + i) * LANES, LANES)
            part = jnp.dot(rounded, recon[:, pl.ds(column, LANES)], preferred_element_type=jnp.float32)
            for slab, row, first, count in pieces(i):
                out[slab, row : row + count, :] = part[first : first + count]


def pieces(i):
    found = []
    first = 0
    while first < STEPS:
        slab, row = divmod(i * STEPS + first, SLAB_USED)
        count = min(STEPS - first, SLAB_USED - row)
        found.append((slab, row, first, count))
        first += count
    return found


def finish_kernel(core, mine, other, out):
    for ref, half in ((mine, core[0]), (other, 1 - core[0])):
        for i in range(HALF_TILES):
            column = pl.multiple_of((half * HALF_TILES + i) * LANES, LANES)
            for slab, row, first, count in pieces(i):
                out[first : first + count, pl.ds(column, LANES)] = ref[slab, row : row + count, :]


def vmem():
    return pl.BlockSpec(memory_space=pltpu.VMEM)


def smem():
    return pl.BlockSpec(memory_space=pltpu.SMEM)


def pack(low, core, high, meta):
    return pl.pallas_call(
        pack_kernel,
        out_shape=jax.ShapeDtypeStruct((CHIPS, PAYLOAD, LANES), jnp.float32),
        in_specs=[vmem()] * 4,
        out_specs=vmem(),
        compiler_params=pltpu.CompilerParams(vmem_limit_bytes=16 << 20),
    )(low, core, high, meta)


def hand(place, own, partner):
    return pl.pallas_call(
        hand_kernel,
        out_shape=(jax.ShapeDtypeStruct((2 * NEW_PAYLOAD, LANES), jnp.float32),) * 4,
        in_specs=[smem(), vmem(), vmem()],
        out_specs=(vmem(),) * 4,
        compiler_params=pltpu.CompilerParams(vmem_limit_bytes=8 << 20),
    )(place, own, partner)


def partial_phases(place, mine, news):
    half = jax.ShapeDtypeStruct((STEPS, 10 * PIX, LANES), jnp.float32)
    return pl.pallas_call(
        sum_kernel,
        out_shape=(half, half),
        in_specs=[smem()] + [vmem()] * 5,
        out_specs=(vmem(), vmem()),
        scratch_shapes=[
            pltpu.VMEM((CHIPS, 2 * TILE, LANES), jnp.float32),
            pltpu.VMEM((CHIPS, PIX, LANES), jnp.int32),
            pltpu.SMEM((CHIPS, PIX, LANES), jnp.int32),
            pltpu.SemaphoreType.DMA(()),
        ],
        compiler_params=pltpu.CompilerParams(vmem_limit_bytes=16 << 20),
    )(place, mine, *news)


def slopes_and_products(flags, here, there, recon):
    slab = jax.ShapeDtypeStruct((SLABS, SLAB_ROWS, LANES), jnp.float32)
    return pl.pallas_call(
        spot_kernel,
        out_shape=(slab, slab, jax.ShapeDtypeStruct((16, FLAT_PAD), jnp.float32)),
        in_specs=[smem()] + [vmem()] * 3,
        out_specs=(vmem(),) * 3,
        scratch_shapes=[
            pltpu.VMEM((20, 16, LANES), jnp.float32),
            pltpu.VMEM((2 * LANES, 2 * LANES), jnp.bfloat16),
            pltpu.VMEM((LANES, LANES), jnp.bfloat16),
        ],
        compiler_params=pltpu.CompilerParams(vmem_limit_bytes=16 << 20),
    )(flags, here, there, recon)


def finish(core, mine, other):
    return pl.pallas_call(
        finish_kernel,
        out_shape=jax.ShapeDtypeStruct((STEPS, ACTS), jnp.float32),
        in_specs=[smem(), vmem(), vmem()],
        out_specs=vmem(),
        compiler_params=pltpu.CompilerParams(vmem_limit_bytes=8 << 20),
    )(core, mine, other)


def groups_by(key):
    found = {}
    for device in range(256):
        layer, sub = divmod(device, 16)
        found.setdefault(key(layer // 8, layer // 2 % 4, layer % 2, sub // 4, sub % 4), []).append(device)
    return [found[name] for name in sorted(found)]


def exchange(blocks, groups):
    return lax.all_to_all(blocks, ("layer", "sub"), 0, 0, tiled=True, axis_index_groups=groups)


def to_all(block, groups):
    return exchange(jnp.broadcast_to(block[None], (len(groups[0]),) + block.shape), groups)


def to_other_core(block):
    return lax.ppermute(block, "layer", [(i, i ^ 1) for i in range(16)])


def local(screens, new_columns, col_block, shift_x, shift_y, valid, recon):
    owner = lax.axis_index("sub")
    count = lax.axis_size("sub")
    strips = jnp.transpose(screens[0], (0, 2, 1))
    fresh = jnp.transpose(new_columns[:, 0], (0, 2, 1))
    layer = lax.axis_index("layer").astype(jnp.int32)
    half = layer // 8

    def new_rows(part):
        at = LANE0 + part * (KEPT - HALF_LANES)
        return lax.dynamic_slice(fresh, (0, 0, at), (STEPS, NEW_COLS, HALF_LANES)).reshape(UPDATES, HALF_LANES)

    def strip(turn):
        return lax.dynamic_slice(strips, (turn, 0, LANE0), (1, 40, KEPT))[0]

    core = strip(PUP_TURN)
    forward = [(i, (i + 1) % count) for i in range(count)]
    backward = [(target, source) for source, target in forward]
    low = lax.ppermute(strip(jnp.where(owner == count - 1, PUP_TURN - 1, PUP_TURN)), "sub", forward)
    high = lax.ppermute(strip(jnp.where(owner == 0, PUP_TURN + 1, PUP_TURN)), "sub", backward)

    partner = lax.ppermute(new_rows(1 - half), "layer", [(i, i ^ 8) for i in range(16)])

    offset = jnp.transpose(shift_y[:, 0]) + HALO
    behind = (offset > LANES - CHIP_ROWS).astype(jnp.int32)
    start = jnp.transpose(shift_x[:, 0]) + HALO + behind * TILE
    turn = (LANES - offset + behind * BEHIND) % LANES
    block = jnp.transpose(col_block) - (PUP_TURN * PUP // NEW_COLS) - (owner * 5 - 5)
    block = jnp.where((block >= 0) & (block < WINDOW // NEW_COLS), block, COLS // NEW_COLS) * NEW_COLS
    meta = (
        jnp.pad(start, ((0, 2), (META_LANE, LANES - META_LANE - STEPS)))
        + jnp.pad(turn, ((0, 2), (TURN_LANE, LANES - TURN_LANE - STEPS)))
        + jnp.pad(block, ((6, 1), (META_LANE, LANES - META_LANE - STEPS)))
    ).astype(jnp.float32)

    side = (layer % 2).reshape(1)
    place = jnp.stack([layer % 2, layer // 2 % 4, half])
    payload = pack(low, core, high, meta)
    _, later = lax.optimization_barrier((payload, place))
    mine = exchange(payload, groups_by(lambda zh, x, c, y, zl: (c, y, zl)))
    news = list(hand(later, new_rows(half), partner))
    for d in range(1, 4):
        along = [(i, i // 8 * 8 + (i % 8 + 2 * d) % 8) for i in range(16)]
        news[d] = lax.ppermute(news[d], "layer", along)
    matrix = jnp.transpose(recon, (0, 2, 3, 1, 4)).reshape(FLAT, ACTS)
    flags = jnp.concatenate([side, valid.reshape(-1)])
    mine, matrix, flags = lax.optimization_barrier((mine, matrix, flags))
    here, there = partial_phases(place, mine, news)
    keep, send, flat = slopes_and_products(flags, here, to_other_core(there), matrix)

    plane = groups_by(lambda zh, x, c, y, zl: (c, zh, zl))
    column = groups_by(lambda zh, x, c, y, zl: (c, x, y))
    part = jnp.sum(exchange(keep + to_other_core(send), plane), axis=0)
    total = to_all(jnp.sum(to_all(part, column), axis=0), plane)
    commands = finish(side, total, to_other_core(total))
    slopes = jnp.transpose(flat[:STEPS, :FLAT].reshape(STEPS, STARS, 5, 5, 2), (0, 1, 4, 2, 3))
    return (slopes, commands)


def solution(mesh):
    return jax.shard_map(
        local,
        mesh=mesh,
        in_specs=(
            P("layer", None, None, "sub"),
            P(None, "layer", None, None),
            P(None, "layer"),
            P(None, "layer", None),
            P(None, "layer", None),
            P("layer", "sub"),
            P(None, None, "layer", "sub", None),
        ),
        out_specs=(P(None, None, None, "layer", "sub"), P()),
        check_vma=False,
    )
```

```python
import math
import jax
import jax.numpy as jnp
import numpy as np
from jax import lax
from jax.experimental import pallas as pl
from jax.experimental.pallas import tpu as pltpu
from jax.sharding import PartitionSpec as P

ACTS = 5376
HALO = 40
NEW_COLS = 8
PUP = 640
PUP_TURN = 3
ROW0 = 704
STEPS = 10
STARS = 6
PIX = 8
LANES = 128
LANE0 = 640
KEPT = 768
FIRST = ROW0 - HALO - LANE0
WINDOW = 120
UPDATES = STEPS * NEW_COLS
COLS = WINDOW + UPDATES
REST = 32
META = WINDOW + 24
PAYLOAD = WINDOW + REST
NEW_REST = 24
NEW_PAYLOAD = UPDATES + NEW_REST
HALF_LANES = 512
TILE = COLS + NEW_COLS
META_LANE = 96
TURN_LANE = 106
BEHIND = 32
CHIPS = 8
CHIP_ROWS = 80
REST_LANES = 32
HALF_TILES = 21
SLABS = 16
SLAB_USED = 14
SLAB_ROWS = 16
FLAT = 300
FLAT_PAD = 384


def toeplitz():
    d = np.arange(PIX)[:, None] - np.arange(PIX)[None, :]
    safe = np.where(d == 0, 1, d)
    return np.where(d == 0, 0.0, -4.0 * (-1.0) ** d / np.tan(np.pi * safe / 16))


def parts(value, count):
    found = []
    rest = value
    for _ in range(count):
        found.append(rest.astype(jnp.bfloat16))
        rest = rest - found[-1].astype(jnp.float32)
    return found


def ahead(d):
    t = toeplitz()
    x = lax.broadcasted_iota(jnp.int32, (PIX, LANES), 0)
    weight = jnp.zeros((PIX, LANES), jnp.float32)
    for i in range(PIX):
        weight = jnp.where(x == i, jnp.float32((2.0 if d == 4 else 4.0) * t[i, (i - d) % PIX]), weight)
    return weight


def lane_table():
    t = toeplitz()
    row = lax.broadcasted_iota(jnp.int32, (LANES, LANES), 0)
    column = lax.broadcasted_iota(jnp.int32, (LANES, LANES), 1)
    same = (lax.shift_right_logical(row, 3) == lax.shift_right_logical(column, 3)) & (row < WINDOW)
    ahead_by = jnp.where(same, column - row, LANES)
    value = jnp.zeros((LANES, LANES), jnp.float32)
    for d in range(1, PIX):
        for step in (d, -d):
            value = jnp.where(ahead_by == step, jnp.float32(4.0 * t[max(step, 0), max(-step, 0)]), value)
    sign = jnp.where(same, jnp.where((ahead_by & 1) == 0, -8.0, 8.0), 0.0).astype(jnp.bfloat16)
    main, rest = parts(value, 2)
    left = jnp.concatenate([main, sign], axis=0)
    right = jnp.concatenate([sign, jnp.zeros_like(sign)], axis=0)
    return jnp.concatenate([left, right], axis=1), rest


def group_table():
    lane = lax.broadcasted_iota(jnp.int32, (LANES, LANES), 0)
    group = lax.broadcasted_iota(jnp.int32, (LANES, LANES), 1)
    first = group * PIX
    return jnp.where((lane >= first) & (lane < first + PIX) & (lane < WINDOW), 1.0 / 1024, 0.0).astype(jnp.bfloat16)


def multiple(value, step, count):
    found = jnp.zeros_like(value)
    for i in range(1, count + 1):
        found = found + (value >= step * i).astype(jnp.int32)
    return found


def order_table(tile):
    row = lax.broadcasted_iota(jnp.int32, (LANES, LANES), 0) + tile * LANES
    column = lax.broadcasted_iota(jnp.int32, (LANES, LANES), 1)
    unit = lax.shift_right_logical(row, 4)
    place = row & 15
    s = multiple(unit, 10, 1)
    k = multiple(unit - 10 * s, 5, 1)
    b = unit - 10 * s - 5 * k
    kk = multiple(place, 5, 2)
    target = (((3 * k + kk) * 5 + place - 5 * kk) * 5 + b) * 2 + s
    target = jnp.where((place < 15) & (unit < 20), target, -1)
    blocks = [(target == column + i * LANES).astype(jnp.float32).astype(jnp.bfloat16) for i in range(FLAT_PAD // LANES)]
    return jnp.concatenate(blocks, axis=1)


def lit(flags):
    place = lax.shift_right_logical(lax.broadcasted_iota(jnp.int32, (8, FLAT_PAD), 1), 1)
    place = place - 25 * multiple(place, 25, 7)
    found = jnp.zeros((8, FLAT_PAD), jnp.float32)
    for a in range(5):
        for b in range(5):
            found = jnp.where(place == a * 5 + b, flags[1 + a * 5 + b].astype(jnp.float32), found)
    return found


def lane_index(shape):
    return lax.broadcasted_iota(jnp.int32, shape, len(shape) - 1)


def pack_kernel(low, core, high, meta, out):
    def window(ref, first, count, start):
        tile, shift = divmod(start, LANES)
        rows = slice(first, first + count)
        left = ref[rows, tile * LANES : (tile + 1) * LANES]
        if shift == 0:
            return left
        left = pltpu.roll(left, LANES - shift, 1)
        if (tile + 2) * LANES > KEPT:
            return left
        right = pltpu.roll(ref[rows, (tile + 1) * LANES : (tile + 2) * LANES], LANES - shift, 1)
        return jnp.where(lane_index(left.shape) < LANES - shift, left, right)

    sources = ((low, 0), (core, 40), (high, 80))

    def columns(first, start):
        ref, base = [source for source in sources if source[1] <= first][-1]
        return window(ref, first - base, PIX, start)

    lane = lane_index((PIX, LANES))
    for m in range(CHIPS):
        start = FIRST + m * CHIP_ROWS
        for ref, base in sources:
            out[m, base : base + 40, :] = window(ref, 0, 40, start)
        for r in range(REST // PIX):
            joined = None
            for q in range(4):
                first = q * REST + r * PIX
                if first >= WINDOW:
                    continue
                piece = columns(first, start + LANES - q * REST_LANES)
                joined = piece if joined is None else jnp.where(lane < q * REST_LANES, joined, piece)
            if WINDOW + r * PIX == META:
                joined = jnp.where(lane < META_LANE, joined, meta[...])
            out[m, WINDOW + r * PIX : WINDOW + (r + 1) * PIX, :] = joined


def hand_kernel(place, own, partner, own_target, *outs):
    *outs, leaving = outs
    outs = [outs[3], *outs[:3]]
    lane = lane_index((PIX, LANES))

    def window(ref, first, count, start):
        tile = lax.shift_right_logical(start, 7)
        cut = LANES - (start & (LANES - 1))
        turn = cut & (LANES - 1)
        rows = slice(first, first + count)
        after = jnp.minimum(tile + 1, HALF_LANES // LANES - 1)
        left = pltpu.roll(ref[rows, pl.ds(pl.multiple_of(tile * LANES, LANES), LANES)], turn, 1)
        right = pltpu.roll(ref[rows, pl.ds(pl.multiple_of(after * LANES, LANES), LANES)], turn, 1)
        return jnp.where(lane_index(left.shape) < cut, left, right)

    for d, out in enumerate(outs):
        start = FIRST + 64 * place[2] + CHIP_ROWS * ((place[1] + d) & 3)
        for w, ref in enumerate((own, partner)):
            base = w * NEW_PAYLOAD
            out[base : base + UPDATES, :] = window(ref, 0, UPDATES, start)
            for r in range(NEW_REST // PIX):
                joined = None
                for q in range(4):
                    first = q * NEW_REST + r * PIX
                    if first >= UPDATES:
                        continue
                    piece = window(ref, first, PIX, start + LANES - q * REST_LANES)
                    joined = piece if joined is None else jnp.where(lane < q * REST_LANES, joined, piece)
                out[base + UPDATES + r * PIX : base + UPDATES + (r + 1) * PIX, :] = joined
        if d == 0:
            copy = pltpu.make_async_copy(out, own_target, leaving)
            copy.start()
    copy.wait()


def sincos(x):
    n = jnp.floor(x * (2.0 / math.pi) + 0.5)
    r = x - n * 1.5703125
    r = r - n * 4.8351287841796875e-4
    r = r - n * 3.13855707645416259765625e-7
    r = r - n * 6.0771005065061922e-11
    q = n.astype(jnp.int32)
    z = r * r
    s = r + r * z * (-1.6666654611e-1 + z * (8.3321608736e-3 + z * -1.9515295891e-4))
    c = 1.0 - 0.5 * z + z * z * (4.166664568298827e-2 + z * (-1.388731625493765e-3 + z * 2.443315711809948e-5))
    swap = (q & 1) == 1
    sine = jnp.where(swap, c, s)
    cosine = jnp.where(swap, s, c)
    sine = jnp.where((q & 2) == 2, -sine, sine)
    cosine = jnp.where(((q + 1) & 2) == 2, -cosine, cosine)
    return sine, cosine


def sum_kernel(place, mine, new_0, new_1, new_2, new_3, keep, send, state, numbers, meta, arrived):
    lane = lane_index((40, LANES))
    side = place[0]
    for p in range(CHIPS):
        numbers[p] = mine[p, META : META + PIX, :].astype(jnp.int32)
    copy = pltpu.make_async_copy(numbers, meta, arrived)
    copy.start()

    def unpack(p, target, near, rest, q):
        count = near.shape[0]
        left = pltpu.roll(near, LANES - BEHIND, 1)
        right = pltpu.roll(rest, (LANES - BEHIND - REST_LANES * q) % LANES, 1)
        state[p, target : target + count, :] = near
        state[p, TILE + target : TILE + target + count, :] = jnp.where(
            lane_index(left.shape) < LANES - BEHIND, left, right
        )

    def begin(p, carry):
        for q in range(4):
            first = q * REST
            count = min(REST, WINDOW - first)
            unpack(p, first, mine[p, first : first + count, :], mine[p, WINDOW : WINDOW + count, :], q)
        return carry

    lax.fori_loop(0, CHIPS, begin, 0)
    for d, ref in enumerate((new_0, new_1, new_2, new_3)):
        for w in range(2):
            half = place[2] if w == 0 else 1 - place[2]
            p = half * 4 + ((place[1] + 4 - d) & 3)
            base = w * NEW_PAYLOAD
            for q in range(4):
                first = q * NEW_REST
                count = min(NEW_REST, UPDATES - first)
                near = ref[base + first : base + first + count, :]
                unpack(p, WINDOW + first, near, ref[base + UPDATES : base + UPDATES + count, :], q)
    copy.wait()

    def step(t, carry):
        for l in range(CHIPS):
            dst = pl.multiple_of(meta[l, 6, META_LANE + t], NEW_COLS)
            src = pl.multiple_of(WINDOW + t * NEW_COLS, NEW_COLS)
            for base in (0, TILE):
                state[l, pl.ds(base + dst, NEW_COLS), :] = state[l, pl.ds(base + src, NEW_COLS), :]
        acc = []
        for g in range(STARS):
            total = jnp.zeros((40, LANES), jnp.float32)
            for l in range(CHIPS):
                window = state[l, pl.ds(meta[l, g, META_LANE + t], 40), :]
                total = total + pltpu.roll(window, meta[l, g, TURN_LANE + t], 1)
            acc.append(total)
        for out, block in ((keep, side), (send, 1 - side)):
            for k in range(2):
                placed = [
                    pltpu.roll(acc[3 * k + j], lax.rem(LANES + 40 * j - 40 * block, LANES), 1) for j in range(3)
                ]
                joined = jnp.where(lane < 40, placed[0], jnp.where(lane < 80, placed[1], placed[2]))
                out[t, k * 40 : (k + 1) * 40, :] = joined
        return carry

    lax.fori_loop(0, STEPS, step, 0)


def spot_kernel(flags, here, there, recon, keep, send, flat_out, sums, lane_tab, lane_rest):
    side = flags[0]
    sums[...] = jnp.zeros_like(sums)
    weights = [ahead(d) for d in range(1, 5)]
    lane_tab[...], lane_rest[...] = lane_table()

    def spots(t):
        sine, cosine = sincos(here[t] + there[t])
        c1, c2 = parts(cosine, 2)
        s1, s2 = parts(sine, 2)
        head = jnp.concatenate([c1, s1], axis=1)
        tail = jnp.concatenate([c2, s2], axis=1)
        first = jnp.dot(jnp.concatenate([head, tail]), lane_tab[...], preferred_element_type=jnp.float32)
        second = jnp.dot(c1, lane_rest[...], preferred_element_type=jnp.float32)
        along = first[:80] + first[80:]
        z_y = sine * (along[:, :LANES] + second) + cosine * along[:, LANES:]

        c3 = cosine.reshape(10, PIX, LANES)
        s3 = sine.reshape(10, PIX, LANES)
        by_sine = -8.0 * s3
        by_cosine = -8.0 * c3
        for d in range(1, 5):
            weight = weights[d - 1][None]
            even = -8.0 if d == 4 else 16.0 * (-1.0) ** (d + 1)
            c_d = pltpu.roll(c3, d, 1)
            s_d = pltpu.roll(s3, d, 1)
            by_sine = by_sine + (weight * c_d + even * s_d)
            by_cosine = by_cosine + (even * c_d - weight * s_d)
        z_x = jnp.sum(s3 * by_sine + c3 * by_cosine, axis=1)
        z_y = jnp.sum(z_y.reshape(10, PIX, LANES), axis=1)
        for unit in range(10):
            sums[unit, pl.ds(t, 1), :] = z_x[unit : unit + 1]
            sums[10 + unit, pl.ds(t, 1), :] = z_y[unit : unit + 1]

    def step(t, carry):
        spots(t)
        return carry

    lax.fori_loop(0, STEPS, step, 0, unroll=2)

    units = 20
    stacked = jnp.concatenate(parts(sums[...].reshape(units * 16, LANES), 3))
    got = jnp.dot(stacked, group_table(), preferred_element_type=jnp.float32)
    size = units * 16
    got = (got[:size] + got[size : 2 * size]) + got[2 * size :]
    tiles = [jnp.zeros((16, LANES), jnp.float32) for _ in range(3)]
    for unit in range(units):
        tiles[unit // 8] = tiles[unit // 8] + pltpu.roll(got[unit * 16 : (unit + 1) * 16], (unit % 8) * 16, 1)
    flat = jnp.zeros((16, FLAT_PAD), jnp.float32)
    for i in range(3):
        moved = jnp.dot(
            jnp.concatenate(parts(tiles[i], 3)), order_table(i), preferred_element_type=jnp.float32
        )
        flat = flat + ((moved[:16] + moved[16:32]) + moved[32:])
    shown = lit(flags)
    flat = flat * jnp.concatenate([shown, shown])
    flat_out[...] = flat
    rounded = flat[:, :FLAT].astype(jnp.bfloat16)
    for out, half in ((keep, side), (send, 1 - side)):
        out[...] = jnp.zeros_like(out)
        for i in range(HALF_TILES):
            column = pl.multiple_of((half * HALF_TILES + i) * LANES, LANES)
            part = jnp.dot(rounded, recon[:, pl.ds(column, LANES)], preferred_element_type=jnp.float32)
            for slab, row, first, count in pieces(i):
                out[slab, row : row + count, :] = part[first : first + count]


def pieces(i):
    found = []
    first = 0
    while first < STEPS:
        slab, row = divmod(i * STEPS + first, SLAB_USED)
        count = min(STEPS - first, SLAB_USED - row)
        found.append((slab, row, first, count))
        first += count
    return found


def finish_kernel(core, mine, other, out):
    for ref, half in ((mine, core[0]), (other, 1 - core[0])):
        for i in range(HALF_TILES):
            column = pl.multiple_of((half * HALF_TILES + i) * LANES, LANES)
            for slab, row, first, count in pieces(i):
                out[first : first + count, pl.ds(column, LANES)] = ref[slab, row : row + count, :]


def vmem():
    return pl.BlockSpec(memory_space=pltpu.VMEM)


def smem():
    return pl.BlockSpec(memory_space=pltpu.SMEM)


def pack(low, core, high, meta):
    return pl.pallas_call(
        pack_kernel,
        out_shape=jax.ShapeDtypeStruct((CHIPS, PAYLOAD, LANES), jnp.float32),
        in_specs=[vmem()] * 4,
        out_specs=vmem(),
        compiler_params=pltpu.CompilerParams(vmem_limit_bytes=16 << 20),
    )(low, core, high, meta)


def hand(place, own, partner):
    return pl.pallas_call(
        hand_kernel,
        out_shape=(jax.ShapeDtypeStruct((2 * NEW_PAYLOAD, LANES), jnp.float32),) * 4,
        in_specs=[smem(), vmem(), vmem()],
        out_specs=(pl.BlockSpec(memory_space=pl.ANY),) + (vmem(),) * 3,
        scratch_shapes=[pltpu.VMEM((2 * NEW_PAYLOAD, LANES), jnp.float32), pltpu.SemaphoreType.DMA(())],
        compiler_params=pltpu.CompilerParams(vmem_limit_bytes=8 << 20),
    )(place, own, partner)


def partial_phases(place, mine, news):
    half = jax.ShapeDtypeStruct((STEPS, 10 * PIX, LANES), jnp.float32)
    return pl.pallas_call(
        sum_kernel,
        out_shape=(half, half),
        in_specs=[smem()] + [vmem()] * 5,
        out_specs=(vmem(), vmem()),
        scratch_shapes=[
            pltpu.VMEM((CHIPS, 2 * TILE, LANES), jnp.float32),
            pltpu.VMEM((CHIPS, PIX, LANES), jnp.int32),
            pltpu.SMEM((CHIPS, PIX, LANES), jnp.int32),
            pltpu.SemaphoreType.DMA(()),
        ],
        compiler_params=pltpu.CompilerParams(vmem_limit_bytes=16 << 20),
    )(place, mine, *news)


def slopes_and_products(flags, here, there, recon):
    slab = jax.ShapeDtypeStruct((SLABS, SLAB_ROWS, LANES), jnp.float32)
    return pl.pallas_call(
        spot_kernel,
        out_shape=(slab, slab, jax.ShapeDtypeStruct((16, FLAT_PAD), jnp.float32)),
        in_specs=[smem()] + [vmem()] * 3,
        out_specs=(vmem(),) * 3,
        scratch_shapes=[
            pltpu.VMEM((20, 16, LANES), jnp.float32),
            pltpu.VMEM((2 * LANES, 2 * LANES), jnp.bfloat16),
            pltpu.VMEM((LANES, LANES), jnp.bfloat16),
        ],
        compiler_params=pltpu.CompilerParams(vmem_limit_bytes=16 << 20),
    )(flags, here, there, recon)


def finish(core, mine, other):
    return pl.pallas_call(
        finish_kernel,
        out_shape=jax.ShapeDtypeStruct((STEPS, ACTS), jnp.float32),
        in_specs=[smem(), vmem(), vmem()],
        out_specs=vmem(),
        compiler_params=pltpu.CompilerParams(vmem_limit_bytes=8 << 20),
    )(core, mine, other)


def groups_by(key):
    found = {}
    for device in range(256):
        layer, sub = divmod(device, 16)
        found.setdefault(key(layer // 8, layer // 2 % 4, layer % 2, sub // 4, sub % 4), []).append(device)
    return [found[name] for name in sorted(found)]


def exchange(blocks, groups):
    return lax.all_to_all(blocks, ("layer", "sub"), 0, 0, tiled=True, axis_index_groups=groups)


def to_all(block, groups):
    return exchange(jnp.broadcast_to(block[None], (len(groups[0]),) + block.shape), groups)


def to_other_core(block):
    return lax.ppermute(block, "layer", [(i, i ^ 1) for i in range(16)])


def local(screens, new_columns, col_block, shift_x, shift_y, valid, recon):
    owner = lax.axis_index("sub")
    count = lax.axis_size("sub")
    strips = jnp.transpose(screens[0], (0, 2, 1))
    fresh = jnp.transpose(new_columns[:, 0], (0, 2, 1))
    layer = lax.axis_index("layer").astype(jnp.int32)
    half = layer // 8

    def new_rows(part):
        at = LANE0 + part * (KEPT - HALF_LANES)
        return lax.dynamic_slice(fresh, (0, 0, at), (STEPS, NEW_COLS, HALF_LANES)).reshape(UPDATES, HALF_LANES)

    def strip(turn):
        return lax.dynamic_slice(strips, (turn, 0, LANE0), (1, 40, KEPT))[0]

    core = strip(PUP_TURN)
    forward = [(i, (i + 1) % count) for i in range(count)]
    backward = [(target, source) for source, target in forward]
    low = lax.ppermute(strip(jnp.where(owner == count - 1, PUP_TURN - 1, PUP_TURN)), "sub", forward)
    high = lax.ppermute(strip(jnp.where(owner == 0, PUP_TURN + 1, PUP_TURN)), "sub", backward)

    partner = lax.ppermute(new_rows(1 - half), "layer", [(i, i ^ 8) for i in range(16)])

    offset = jnp.transpose(shift_y[:, 0]) + HALO
    behind = (offset > LANES - CHIP_ROWS).astype(jnp.int32)
    start = jnp.transpose(shift_x[:, 0]) + HALO + behind * TILE
    turn = (LANES - offset + behind * BEHIND) % LANES
    block = jnp.transpose(col_block) - (PUP_TURN * PUP // NEW_COLS) - (owner * 5 - 5)
    block = jnp.where((block >= 0) & (block < WINDOW // NEW_COLS), block, COLS // NEW_COLS) * NEW_COLS
    meta = (
        jnp.pad(start, ((0, 2), (META_LANE, LANES - META_LANE - STEPS)))
        + jnp.pad(turn, ((0, 2), (TURN_LANE, LANES - TURN_LANE - STEPS)))
        + jnp.pad(block, ((6, 1), (META_LANE, LANES - META_LANE - STEPS)))
    ).astype(jnp.float32)

    side = (layer % 2).reshape(1)
    place = jnp.stack([layer % 2, layer // 2 % 4, half])
    flags = jnp.concatenate([side, valid.reshape(-1)])
    payload, partner, flags = lax.optimization_barrier((pack(low, core, high, meta), partner, flags))
    mine = exchange(payload, groups_by(lambda zh, x, c, y, zl: (c, y, zl)))
    news = list(hand(place, new_rows(half), partner))
    *news[1:], recon = lax.optimization_barrier((*news[1:], recon))
    for d in range(1, 4):
        along = [(i, i // 8 * 8 + (i % 8 + 2 * d) % 8) for i in range(16)]
        news[d] = lax.ppermute(news[d], "layer", along)
    matrix = jnp.transpose(recon, (0, 2, 3, 1, 4)).reshape(FLAT, ACTS)
    mine, matrix = lax.optimization_barrier((mine, matrix))
    here, there = partial_phases(place, mine, news)
    keep, send, flat = slopes_and_products(flags, here, to_other_core(there), matrix)

    plane = groups_by(lambda zh, x, c, y, zl: (c, zh, zl))
    column = groups_by(lambda zh, x, c, y, zl: (c, x, y))
    part = jnp.sum(exchange(keep + to_other_core(send), plane), axis=0)
    total = to_all(jnp.sum(to_all(part, column), axis=0), plane)
    commands = finish(side, total, to_other_core(total))
    slopes = jnp.transpose(flat[:STEPS, :FLAT].reshape(STEPS, STARS, 5, 5, 2), (0, 1, 4, 2, 3))
    return (slopes, commands)


def solution(mesh):
    return jax.shard_map(
        local,
        mesh=mesh,
        in_specs=(
            P("layer", None, None, "sub"),
            P(None, "layer", None, None),
            P(None, "layer"),
            P(None, "layer", None),
            P(None, "layer", None),
            P("layer", "sub"),
            P(None, None, "layer", "sub", None),
        ),
        out_specs=(P(None, None, None, "layer", "sub"), P()),
        check_vma=False,
    )
```

```python
import math
import jax
import jax.numpy as jnp
import numpy as np
from jax import lax
from jax.experimental import pallas as pl
from jax.experimental.pallas import tpu as pltpu
from jax.sharding import PartitionSpec as P

ACTS = 5376
HALO = 40
NEW_COLS = 8
PUP = 640
PUP_TURN = 3
ROW0 = 704
STEPS = 10
STARS = 6
PIX = 8
LANES = 128
LANE0 = 640
KEPT = 768
FIRST = ROW0 - HALO - LANE0
WINDOW = 120
UPDATES = STEPS * NEW_COLS
COLS = WINDOW + UPDATES
REST = 32
META = WINDOW + 24
PAYLOAD = WINDOW + REST
NEW_REST = 24
NEW_PAYLOAD = UPDATES + NEW_REST
HALF_LANES = 512
TILE = COLS + NEW_COLS
META_LANE = 96
TURN_LANE = 106
BEHIND = 32
CHIPS = 8
CHIP_ROWS = 80
REST_LANES = 32
HALF_TILES = 21
SLABS = 16
SLAB_USED = 14
SLAB_ROWS = 16
FLAT = 300
FLAT_PAD = 384


def toeplitz():
    d = np.arange(PIX)[:, None] - np.arange(PIX)[None, :]
    safe = np.where(d == 0, 1, d)
    return np.where(d == 0, 0.0, -4.0 * (-1.0) ** d / np.tan(np.pi * safe / 16))


def parts(value, count):
    found = []
    rest = value
    for _ in range(count):
        found.append(rest.astype(jnp.bfloat16))
        rest = rest - found[-1].astype(jnp.float32)
    return found


def ahead(d):
    t = toeplitz()
    x = lax.broadcasted_iota(jnp.int32, (PIX, LANES), 0)
    weight = jnp.zeros((PIX, LANES), jnp.float32)
    for i in range(PIX):
        weight = jnp.where(x == i, jnp.float32((2.0 if d == 4 else 4.0) * t[i, (i - d) % PIX]), weight)
    return weight


def lane_table():
    t = toeplitz()
    row = lax.broadcasted_iota(jnp.int32, (LANES, LANES), 0)
    column = lax.broadcasted_iota(jnp.int32, (LANES, LANES), 1)
    same = (lax.shift_right_logical(row, 3) == lax.shift_right_logical(column, 3)) & (row < WINDOW)
    ahead_by = jnp.where(same, column - row, LANES)
    value = jnp.zeros((LANES, LANES), jnp.float32)
    for d in range(1, PIX):
        for step in (d, -d):
            value = jnp.where(ahead_by == step, jnp.float32(4.0 * t[max(step, 0), max(-step, 0)]), value)
    sign = jnp.where(same, jnp.where((ahead_by & 1) == 0, -8.0, 8.0), 0.0).astype(jnp.bfloat16)
    main, rest = parts(value, 2)
    left = jnp.concatenate([main, sign], axis=0)
    right = jnp.concatenate([sign, jnp.zeros_like(sign)], axis=0)
    return jnp.concatenate([left, right], axis=1), rest


def group_table():
    lane = lax.broadcasted_iota(jnp.int32, (LANES, LANES), 0)
    group = lax.broadcasted_iota(jnp.int32, (LANES, LANES), 1)
    first = group * PIX
    return jnp.where((lane >= first) & (lane < first + PIX) & (lane < WINDOW), 1.0 / 1024, 0.0).astype(jnp.bfloat16)


def multiple(value, step, count):
    found = jnp.zeros_like(value)
    for i in range(1, count + 1):
        found = found + (value >= step * i).astype(jnp.int32)
    return found


def order_table(tile):
    row = lax.broadcasted_iota(jnp.int32, (LANES, LANES), 0) + tile * LANES
    column = lax.broadcasted_iota(jnp.int32, (LANES, LANES), 1)
    unit = lax.shift_right_logical(row, 4)
    place = row & 15
    s = multiple(unit, 10, 1)
    k = multiple(unit - 10 * s, 5, 1)
    b = unit - 10 * s - 5 * k
    kk = multiple(place, 5, 2)
    target = (((3 * k + kk) * 5 + place - 5 * kk) * 5 + b) * 2 + s
    target = jnp.where((place < 15) & (unit < 20), target, -1)
    blocks = [(target == column + i * LANES).astype(jnp.float32).astype(jnp.bfloat16) for i in range(FLAT_PAD // LANES)]
    return jnp.concatenate(blocks, axis=1)


def lit(flags):
    place = lax.shift_right_logical(lax.broadcasted_iota(jnp.int32, (8, FLAT_PAD), 1), 1)
    place = place - 25 * multiple(place, 25, 7)
    found = jnp.zeros((8, FLAT_PAD), jnp.float32)
    for a in range(5):
        for b in range(5):
            found = jnp.where(place == a * 5 + b, flags[1 + a * 5 + b].astype(jnp.float32), found)
    return found


def lane_index(shape):
    return lax.broadcasted_iota(jnp.int32, shape, len(shape) - 1)


def pack_kernel(low, core, high, meta, out):
    def window(ref, first, count, start):
        tile, shift = divmod(start, LANES)
        rows = slice(first, first + count)
        left = ref[rows, tile * LANES : (tile + 1) * LANES]
        if shift == 0:
            return left
        left = pltpu.roll(left, LANES - shift, 1)
        if (tile + 2) * LANES > KEPT:
            return left
        right = pltpu.roll(ref[rows, (tile + 1) * LANES : (tile + 2) * LANES], LANES - shift, 1)
        return jnp.where(lane_index(left.shape) < LANES - shift, left, right)

    sources = ((low, 0), (core, 40), (high, 80))

    def columns(first, start):
        ref, base = [source for source in sources if source[1] <= first][-1]
        return window(ref, first - base, PIX, start)

    lane = lane_index((PIX, LANES))
    for m in range(CHIPS):
        start = FIRST + m * CHIP_ROWS
        for ref, base in sources:
            out[m, base : base + 40, :] = window(ref, 0, 40, start)
        for r in range(REST // PIX):
            joined = None
            for q in range(4):
                first = q * REST + r * PIX
                if first >= WINDOW:
                    continue
                piece = columns(first, start + LANES - q * REST_LANES)
                joined = piece if joined is None else jnp.where(lane < q * REST_LANES, joined, piece)
            if WINDOW + r * PIX == META:
                joined = jnp.where(lane < META_LANE, joined, meta[...])
            out[m, WINDOW + r * PIX : WINDOW + (r + 1) * PIX, :] = joined


def hand_kernel(place, own, partner, own_target, *outs):
    *outs, leaving = outs
    outs = [outs[3], *outs[:3]]
    lane = lane_index((PIX, LANES))

    def window(ref, first, count, start):
        tile = lax.shift_right_logical(start, 7)
        cut = LANES - (start & (LANES - 1))
        turn = cut & (LANES - 1)
        rows = slice(first, first + count)
        after = jnp.minimum(tile + 1, HALF_LANES // LANES - 1)
        left = pltpu.roll(ref[rows, pl.ds(pl.multiple_of(tile * LANES, LANES), LANES)], turn, 1)
        right = pltpu.roll(ref[rows, pl.ds(pl.multiple_of(after * LANES, LANES), LANES)], turn, 1)
        return jnp.where(lane_index(left.shape) < cut, left, right)

    for d, out in enumerate(outs):
        start = FIRST + 64 * place[2] + CHIP_ROWS * ((place[1] + d) & 3)
        for w, ref in enumerate((own, partner)):
            base = w * NEW_PAYLOAD
            out[base : base + UPDATES, :] = window(ref, 0, UPDATES, start)
            for r in range(NEW_REST // PIX):
                joined = None
                for q in range(4):
                    first = q * NEW_REST + r * PIX
                    if first >= UPDATES:
                        continue
                    piece = window(ref, first, PIX, start + LANES - q * REST_LANES)
                    joined = piece if joined is None else jnp.where(lane < q * REST_LANES, joined, piece)
                out[base + UPDATES + r * PIX : base + UPDATES + (r + 1) * PIX, :] = joined
        if d == 0:
            copy = pltpu.make_async_copy(out, own_target, leaving)
            copy.start()
    copy.wait()


def sincos(x):
    n = jnp.floor(x * (2.0 / math.pi) + 0.5)
    r = x - n * 1.5703125
    r = r - n * 4.8351287841796875e-4
    r = r - n * 3.13855707645416259765625e-7
    r = r - n * 6.0771005065061922e-11
    q = n.astype(jnp.int32)
    z = r * r
    s = r + r * z * (-1.6666654611e-1 + z * (8.3321608736e-3 + z * -1.9515295891e-4))
    c = 1.0 - 0.5 * z + z * z * (4.166664568298827e-2 + z * (-1.388731625493765e-3 + z * 2.443315711809948e-5))
    swap = (q & 1) == 1
    sine = jnp.where(swap, c, s)
    cosine = jnp.where(swap, s, c)
    sine = jnp.where((q & 2) == 2, -sine, sine)
    cosine = jnp.where(((q + 1) & 2) == 2, -cosine, cosine)
    return sine, cosine


def sum_kernel(place, mine, new_0, new_1, new_2, new_3, keep, send, state, numbers, meta, arrived):
    lane = lane_index((40, LANES))
    side = place[0]
    for p in range(CHIPS):
        numbers[p] = mine[p, META : META + PIX, :].astype(jnp.int32)
    copy = pltpu.make_async_copy(numbers, meta, arrived)
    copy.start()

    def unpack(p, target, near, rest, q):
        count = near.shape[0]
        left = pltpu.roll(near, LANES - BEHIND, 1)
        right = pltpu.roll(rest, (LANES - BEHIND - REST_LANES * q) % LANES, 1)
        state[p, target : target + count, :] = near
        state[p, TILE + target : TILE + target + count, :] = jnp.where(
            lane_index(left.shape) < LANES - BEHIND, left, right
        )

    def begin(p, carry):
        for q in range(4):
            first = q * REST
            count = min(REST, WINDOW - first)
            unpack(p, first, mine[p, first : first + count, :], mine[p, WINDOW : WINDOW + count, :], q)
        return carry

    lax.fori_loop(0, CHIPS, begin, 0)
    for d, ref in enumerate((new_0, new_1, new_2, new_3)):
        for w in range(2):
            half = place[2] if w == 0 else 1 - place[2]
            p = half * 4 + ((place[1] + 4 - d) & 3)
            base = w * NEW_PAYLOAD
            for q in range(4):
                first = q * NEW_REST
                count = min(NEW_REST, UPDATES - first)
                near = ref[base + first : base + first + count, :]
                unpack(p, WINDOW + first, near, ref[base + UPDATES : base + UPDATES + count, :], q)
    copy.wait()

    def step(t, carry):
        for l in range(CHIPS):
            dst = pl.multiple_of(meta[l, 6, META_LANE + t], NEW_COLS)
            src = pl.multiple_of(WINDOW + t * NEW_COLS, NEW_COLS)
            for base in (0, TILE):
                state[l, pl.ds(base + dst, NEW_COLS), :] = state[l, pl.ds(base + src, NEW_COLS), :]
        acc = []
        for g in range(STARS):
            total = jnp.zeros((40, LANES), jnp.float32)
            for l in range(CHIPS):
                window = state[l, pl.ds(meta[l, g, META_LANE + t], 40), :]
                total = total + pltpu.roll(window, meta[l, g, TURN_LANE + t], 1)
            acc.append(total)
        for k in range(2):
            one, two, three = acc[3 * k : 3 * k + 3]
            near = jnp.where(lane < 40, one, jnp.where(lane < 80, pltpu.roll(two, 40, 1), pltpu.roll(three, 80, 1)))
            far = jnp.where(lane < 40, pltpu.roll(one, LANES - 40, 1), jnp.where(lane < 80, two, pltpu.roll(three, 40, 1)))
            keep[t, k * 40 : (k + 1) * 40, :] = jnp.where(side == 0, near, far)
            send[t, k * 40 : (k + 1) * 40, :] = jnp.where(side == 0, far, near)
        return carry

    lax.fori_loop(0, STEPS, step, 0, unroll=2)


def spot_kernel(flags, here, there, recon, keep, send, flat_out, sums, lane_tab, lane_rest):
    side = flags[0]
    sums[...] = jnp.zeros_like(sums)
    weights = [ahead(d) for d in range(1, 5)]
    lane_tab[...], lane_rest[...] = lane_table()

    def spots(t):
        sine, cosine = sincos(here[t] + there[t])
        c1, c2 = parts(cosine, 2)
        s1, s2 = parts(sine, 2)
        head = jnp.concatenate([c1, s1], axis=1)
        tail = jnp.concatenate([c2, s2], axis=1)
        first = jnp.dot(jnp.concatenate([head, tail]), lane_tab[...], preferred_element_type=jnp.float32)
        second = jnp.dot(c1, lane_rest[...], preferred_element_type=jnp.float32)
        along = first[:80] + first[80:]
        z_y = sine * (along[:, :LANES] + second) + cosine * along[:, LANES:]

        c3 = cosine.reshape(10, PIX, LANES)
        s3 = sine.reshape(10, PIX, LANES)
        by_sine = -8.0 * s3
        by_cosine = -8.0 * c3
        for d in range(1, 5):
            weight = weights[d - 1][None]
            even = -8.0 if d == 4 else 16.0 * (-1.0) ** (d + 1)
            c_d = pltpu.roll(c3, d, 1)
            s_d = pltpu.roll(s3, d, 1)
            by_sine = by_sine + (weight * c_d + even * s_d)
            by_cosine = by_cosine + (even * c_d - weight * s_d)
        z_x = jnp.sum(s3 * by_sine + c3 * by_cosine, axis=1)
        z_y = jnp.sum(z_y.reshape(10, PIX, LANES), axis=1)
        for unit in range(10):
            sums[unit, pl.ds(t, 1), :] = z_x[unit : unit + 1]
            sums[10 + unit, pl.ds(t, 1), :] = z_y[unit : unit + 1]

    def step(t, carry):
        spots(t)
        return carry

    lax.fori_loop(0, STEPS, step, 0, unroll=2)

    units = 20
    stacked = jnp.concatenate(parts(sums[...].reshape(units * 16, LANES), 3))
    got = jnp.dot(stacked, group_table(), preferred_element_type=jnp.float32)
    size = units * 16
    got = (got[:size] + got[size : 2 * size]) + got[2 * size :]
    tiles = [jnp.zeros((16, LANES), jnp.float32) for _ in range(3)]
    for unit in range(units):
        tiles[unit // 8] = tiles[unit // 8] + pltpu.roll(got[unit * 16 : (unit + 1) * 16], (unit % 8) * 16, 1)
    flat = jnp.zeros((16, FLAT_PAD), jnp.float32)
    for i in range(3):
        moved = jnp.dot(
            jnp.concatenate(parts(tiles[i], 3)), order_table(i), preferred_element_type=jnp.float32
        )
        flat = flat + ((moved[:16] + moved[16:32]) + moved[32:])
    shown = lit(flags)
    flat = flat * jnp.concatenate([shown, shown])
    flat_out[...] = flat
    rounded = flat[:, :FLAT].astype(jnp.bfloat16)
    for out, half in ((keep, side), (send, 1 - side)):
        out[...] = jnp.zeros_like(out)
        for i in range(HALF_TILES):
            column = pl.multiple_of((half * HALF_TILES + i) * LANES, LANES)
            part = jnp.dot(rounded, recon[:, pl.ds(column, LANES)], preferred_element_type=jnp.float32)
            for slab, row, first, count in pieces(i):
                out[slab, row : row + count, :] = part[first : first + count]


def pieces(i):
    found = []
    first = 0
    while first < STEPS:
        slab, row = divmod(i * STEPS + first, SLAB_USED)
        count = min(STEPS - first, SLAB_USED - row)
        found.append((slab, row, first, count))
        first += count
    return found


def finish_kernel(core, mine, other, out):
    for ref, half in ((mine, core[0]), (other, 1 - core[0])):
        for i in range(HALF_TILES):
            column = pl.multiple_of((half * HALF_TILES + i) * LANES, LANES)
            for slab, row, first, count in pieces(i):
                out[first : first + count, pl.ds(column, LANES)] = ref[slab, row : row + count, :]


def vmem():
    return pl.BlockSpec(memory_space=pltpu.VMEM)


def smem():
    return pl.BlockSpec(memory_space=pltpu.SMEM)


def pack(low, core, high, meta):
    return pl.pallas_call(
        pack_kernel,
        out_shape=jax.ShapeDtypeStruct((CHIPS, PAYLOAD, LANES), jnp.float32),
        in_specs=[vmem()] * 4,
        out_specs=vmem(),
        compiler_params=pltpu.CompilerParams(vmem_limit_bytes=16 << 20),
    )(low, core, high, meta)


def hand(place, own, partner):
    return pl.pallas_call(
        hand_kernel,
        out_shape=(jax.ShapeDtypeStruct((2 * NEW_PAYLOAD, LANES), jnp.float32),) * 4,
        in_specs=[smem(), vmem(), vmem()],
        out_specs=(pl.BlockSpec(memory_space=pl.ANY),) + (vmem(),) * 3,
        scratch_shapes=[pltpu.VMEM((2 * NEW_PAYLOAD, LANES), jnp.float32), pltpu.SemaphoreType.DMA(())],
        compiler_params=pltpu.CompilerParams(vmem_limit_bytes=8 << 20),
    )(place, own, partner)


def partial_phases(place, mine, news):
    half = jax.ShapeDtypeStruct((STEPS, 10 * PIX, LANES), jnp.float32)
    return pl.pallas_call(
        sum_kernel,
        out_shape=(half, half),
        in_specs=[smem()] + [vmem()] * 5,
        out_specs=(vmem(), vmem()),
        scratch_shapes=[
            pltpu.VMEM((CHIPS, 2 * TILE, LANES), jnp.float32),
            pltpu.VMEM((CHIPS, PIX, LANES), jnp.int32),
            pltpu.SMEM((CHIPS, PIX, LANES), jnp.int32),
            pltpu.SemaphoreType.DMA(()),
        ],
        compiler_params=pltpu.CompilerParams(vmem_limit_bytes=16 << 20),
    )(place, mine, *news)


def slopes_and_products(flags, here, there, recon):
    slab = jax.ShapeDtypeStruct((SLABS, SLAB_ROWS, LANES), jnp.float32)
    return pl.pallas_call(
        spot_kernel,
        out_shape=(slab, slab, jax.ShapeDtypeStruct((16, FLAT_PAD), jnp.float32)),
        in_specs=[smem()] + [vmem()] * 3,
        out_specs=(vmem(),) * 3,
        scratch_shapes=[
            pltpu.VMEM((20, 16, LANES), jnp.float32),
            pltpu.VMEM((2 * LANES, 2 * LANES), jnp.bfloat16),
            pltpu.VMEM((LANES, LANES), jnp.bfloat16),
        ],
        compiler_params=pltpu.CompilerParams(vmem_limit_bytes=16 << 20),
    )(flags, here, there, recon)


def finish(core, mine, other):
    return pl.pallas_call(
        finish_kernel,
        out_shape=jax.ShapeDtypeStruct((STEPS, ACTS), jnp.float32),
        in_specs=[smem(), vmem(), vmem()],
        out_specs=vmem(),
        compiler_params=pltpu.CompilerParams(vmem_limit_bytes=8 << 20),
    )(core, mine, other)


def groups_by(key):
    found = {}
    for device in range(256):
        layer, sub = divmod(device, 16)
        found.setdefault(key(layer // 8, layer // 2 % 4, layer % 2, sub // 4, sub % 4), []).append(device)
    return [found[name] for name in sorted(found)]


def exchange(blocks, groups):
    return lax.all_to_all(blocks, ("layer", "sub"), 0, 0, tiled=True, axis_index_groups=groups)


def to_all(block, groups):
    return exchange(jnp.broadcast_to(block[None], (len(groups[0]),) + block.shape), groups)


def to_other_core(block):
    return lax.ppermute(block, "layer", [(i, i ^ 1) for i in range(16)])


def local(screens, new_columns, col_block, shift_x, shift_y, valid, recon):
    owner = lax.axis_index("sub")
    count = lax.axis_size("sub")
    strips = jnp.transpose(screens[0], (0, 2, 1))
    fresh = jnp.transpose(new_columns[:, 0], (0, 2, 1))
    layer = lax.axis_index("layer").astype(jnp.int32)
    half = layer // 8

    def new_rows(part):
        at = LANE0 + part * (KEPT - HALF_LANES)
        return lax.dynamic_slice(fresh, (0, 0, at), (STEPS, NEW_COLS, HALF_LANES)).reshape(UPDATES, HALF_LANES)

    def strip(turn):
        return lax.dynamic_slice(strips, (turn, 0, LANE0), (1, 40, KEPT))[0]

    core = strip(PUP_TURN)
    forward = [(i, (i + 1) % count) for i in range(count)]
    backward = [(target, source) for source, target in forward]
    low = lax.ppermute(strip(jnp.where(owner == count - 1, PUP_TURN - 1, PUP_TURN)), "sub", forward)
    high = lax.ppermute(strip(jnp.where(owner == 0, PUP_TURN + 1, PUP_TURN)), "sub", backward)

    partner = lax.ppermute(new_rows(1 - half), "layer", [(i, i ^ 8) for i in range(16)])

    offset = jnp.transpose(shift_y[:, 0]) + HALO
    behind = (offset > LANES - CHIP_ROWS).astype(jnp.int32)
    start = jnp.transpose(shift_x[:, 0]) + HALO + behind * TILE
    turn = (LANES - offset + behind * BEHIND) % LANES
    block = jnp.transpose(col_block) - (PUP_TURN * PUP // NEW_COLS) - (owner * 5 - 5)
    block = jnp.where((block >= 0) & (block < WINDOW // NEW_COLS), block, COLS // NEW_COLS) * NEW_COLS
    meta = (
        jnp.pad(start, ((0, 2), (META_LANE, LANES - META_LANE - STEPS)))
        + jnp.pad(turn, ((0, 2), (TURN_LANE, LANES - TURN_LANE - STEPS)))
        + jnp.pad(block, ((6, 1), (META_LANE, LANES - META_LANE - STEPS)))
    ).astype(jnp.float32)

    side = (layer % 2).reshape(1)
    place = jnp.stack([layer % 2, layer // 2 % 4, half])
    flags = jnp.concatenate([side, valid.reshape(-1)])
    payload, partner, flags = lax.optimization_barrier((pack(low, core, high, meta), partner, flags))
    mine = exchange(payload, groups_by(lambda zh, x, c, y, zl: (c, y, zl)))
    news = list(hand(place, new_rows(half), partner))
    *news[1:], recon = lax.optimization_barrier((*news[1:], recon))
    for d in range(1, 4):
        along = [(i, i // 8 * 8 + (i % 8 + 2 * d) % 8) for i in range(16)]
        news[d] = lax.ppermute(news[d], "layer", along)
    matrix = jnp.transpose(recon, (0, 2, 3, 1, 4)).reshape(FLAT, ACTS)
    mine, matrix = lax.optimization_barrier((mine, matrix))
    here, there = partial_phases(place, mine, news)
    keep, send, flat = slopes_and_products(flags, here, to_other_core(there), matrix)

    plane = groups_by(lambda zh, x, c, y, zl: (c, zh, zl))
    column = groups_by(lambda zh, x, c, y, zl: (c, x, y))
    part = jnp.sum(exchange(keep + to_other_core(send), plane), axis=0)
    total = to_all(jnp.sum(to_all(part, column), axis=0), plane)
    commands = finish(side, total, to_other_core(total))
    slopes = jnp.transpose(flat[:STEPS, :FLAT].reshape(STEPS, STARS, 5, 5, 2), (0, 1, 4, 2, 3))
    return (slopes, commands)


def solution(mesh):
    return jax.shard_map(
        local,
        mesh=mesh,
        in_specs=(
            P("layer", None, None, "sub"),
            P(None, "layer", None, None),
            P(None, "layer"),
            P(None, "layer", None),
            P(None, "layer", None),
            P("layer", "sub"),
            P(None, None, "layer", "sub", None),
        ),
        out_specs=(P(None, None, None, "layer", "sub"), P()),
        check_vma=False,
    )
```

```python
import math
import jax
import jax.numpy as jnp
import numpy as np
from jax import lax
from jax.experimental import pallas as pl
from jax.experimental.pallas import tpu as pltpu
from jax.sharding import PartitionSpec as P

ACTS = 5376
HALO = 40
NEW_COLS = 8
PUP = 640
PUP_TURN = 3
ROW0 = 704
STEPS = 10
STARS = 6
PIX = 8
LANES = 128
LANE0 = 640
KEPT = 768
FIRST = ROW0 - HALO - LANE0
WINDOW = 120
UPDATES = STEPS * NEW_COLS
COLS = WINDOW + UPDATES
REST = 32
META = WINDOW + 24
PAYLOAD = WINDOW + REST
NEW_REST = 24
NEW_PAYLOAD = UPDATES + NEW_REST
HALF_LANES = 512
TILE = COLS + NEW_COLS
META_LANE = 96
TURN_LANE = 106
BEHIND = 32
CHIPS = 8
CHIP_ROWS = 80
REST_LANES = 32
HALF_TILES = 21
SLABS = 16
SLAB_USED = 14
SLAB_ROWS = 16
FLAT = 300
FLAT_PAD = 384


def toeplitz():
    d = np.arange(PIX)[:, None] - np.arange(PIX)[None, :]
    safe = np.where(d == 0, 1, d)
    return np.where(d == 0, 0.0, -4.0 * (-1.0) ** d / np.tan(np.pi * safe / 16))


def parts(value, count):
    found = []
    rest = value
    for _ in range(count):
        found.append(rest.astype(jnp.bfloat16))
        rest = rest - found[-1].astype(jnp.float32)
    return found


def ahead(d):
    t = toeplitz()
    x = lax.broadcasted_iota(jnp.int32, (PIX, LANES), 0)
    weight = jnp.zeros((PIX, LANES), jnp.float32)
    for i in range(PIX):
        weight = jnp.where(x == i, jnp.float32((2.0 if d == 4 else 4.0) * t[i, (i - d) % PIX]), weight)
    return weight


def lane_table():
    t = toeplitz()
    row = lax.broadcasted_iota(jnp.int32, (LANES, LANES), 0)
    column = lax.broadcasted_iota(jnp.int32, (LANES, LANES), 1)
    same = (lax.shift_right_logical(row, 3) == lax.shift_right_logical(column, 3)) & (row < WINDOW)
    ahead_by = jnp.where(same, column - row, LANES)
    value = jnp.zeros((LANES, LANES), jnp.float32)
    for d in range(1, PIX):
        for step in (d, -d):
            value = jnp.where(ahead_by == step, jnp.float32(4.0 * t[max(step, 0), max(-step, 0)]), value)
    sign = jnp.where(same, jnp.where((ahead_by & 1) == 0, -8.0, 8.0), 0.0).astype(jnp.bfloat16)
    main, rest = parts(value, 2)
    left = jnp.concatenate([main, sign], axis=0)
    right = jnp.concatenate([sign, jnp.zeros_like(sign)], axis=0)
    return jnp.concatenate([left, right], axis=1), rest


def group_table():
    lane = lax.broadcasted_iota(jnp.int32, (LANES, LANES), 0)
    group = lax.broadcasted_iota(jnp.int32, (LANES, LANES), 1)
    first = group * PIX
    return jnp.where((lane >= first) & (lane < first + PIX) & (lane < WINDOW), 1.0 / 1024, 0.0).astype(jnp.bfloat16)


def multiple(value, step, count):
    found = jnp.zeros_like(value)
    for i in range(1, count + 1):
        found = found + (value >= step * i).astype(jnp.int32)
    return found


def order_table(tile):
    row = lax.broadcasted_iota(jnp.int32, (LANES, LANES), 0) + tile * LANES
    column = lax.broadcasted_iota(jnp.int32, (LANES, LANES), 1)
    unit = lax.shift_right_logical(row, 4)
    place = row & 15
    s = multiple(unit, 10, 1)
    k = multiple(unit - 10 * s, 5, 1)
    b = unit - 10 * s - 5 * k
    kk = multiple(place, 5, 2)
    target = (((3 * k + kk) * 5 + place - 5 * kk) * 5 + b) * 2 + s
    target = jnp.where((place < 15) & (unit < 20), target, -1)
    blocks = [(target == column + i * LANES).astype(jnp.float32).astype(jnp.bfloat16) for i in range(FLAT_PAD // LANES)]
    return jnp.concatenate(blocks, axis=1)


def lit(flags):
    place = lax.shift_right_logical(lax.broadcasted_iota(jnp.int32, (8, FLAT_PAD), 1), 1)
    place = place - 25 * multiple(place, 25, 7)
    found = jnp.zeros((8, FLAT_PAD), jnp.float32)
    for a in range(5):
        for b in range(5):
            found = jnp.where(place == a * 5 + b, flags[1 + a * 5 + b].astype(jnp.float32), found)
    return found


def lane_index(shape):
    return lax.broadcasted_iota(jnp.int32, shape, len(shape) - 1)


def pack_kernel(low, core, high, meta, out):
    def window(ref, first, count, start):
        tile, shift = divmod(start, LANES)
        rows = slice(first, first + count)
        left = ref[rows, tile * LANES : (tile + 1) * LANES]
        if shift == 0:
            return left
        left = pltpu.roll(left, LANES - shift, 1)
        if (tile + 2) * LANES > KEPT:
            return left
        right = pltpu.roll(ref[rows, (tile + 1) * LANES : (tile + 2) * LANES], LANES - shift, 1)
        return jnp.where(lane_index(left.shape) < LANES - shift, left, right)

    sources = ((low, 0), (core, 40), (high, 80))

    def columns(first, start):
        ref, base = [source for source in sources if source[1] <= first][-1]
        return window(ref, first - base, PIX, start)

    lane = lane_index((PIX, LANES))
    for m in range(CHIPS):
        start = FIRST + m * CHIP_ROWS
        for ref, base in sources:
            out[m, base : base + 40, :] = window(ref, 0, 40, start)
        for r in range(REST // PIX):
            joined = None
            for q in range(4):
                first = q * REST + r * PIX
                if first >= WINDOW:
                    continue
                piece = columns(first, start + LANES - q * REST_LANES)
                joined = piece if joined is None else jnp.where(lane < q * REST_LANES, joined, piece)
            if WINDOW + r * PIX == META:
                joined = jnp.where(lane < META_LANE, joined, meta[...])
            out[m, WINDOW + r * PIX : WINDOW + (r + 1) * PIX, :] = joined


def hand_kernel(place, own, partner, own_target, *outs):
    *outs, leaving = outs
    outs = [outs[3], *outs[:3]]
    lane = lane_index((PIX, LANES))

    def window(ref, first, count, start):
        tile = lax.shift_right_logical(start, 7)
        cut = LANES - (start & (LANES - 1))
        turn = cut & (LANES - 1)
        rows = slice(first, first + count)
        after = jnp.minimum(tile + 1, HALF_LANES // LANES - 1)
        left = pltpu.roll(ref[rows, pl.ds(pl.multiple_of(tile * LANES, LANES), LANES)], turn, 1)
        right = pltpu.roll(ref[rows, pl.ds(pl.multiple_of(after * LANES, LANES), LANES)], turn, 1)
        return jnp.where(lane_index(left.shape) < cut, left, right)

    for d, out in enumerate(outs):
        start = FIRST + 64 * place[2] + CHIP_ROWS * ((place[1] + d) & 3)
        for w, ref in enumerate((own, partner)):
            base = w * NEW_PAYLOAD
            out[base : base + UPDATES, :] = window(ref, 0, UPDATES, start)
            for r in range(NEW_REST // PIX):
                joined = None
                for q in range(4):
                    first = q * NEW_REST + r * PIX
                    if first >= UPDATES:
                        continue
                    piece = window(ref, first, PIX, start + LANES - q * REST_LANES)
                    joined = piece if joined is None else jnp.where(lane < q * REST_LANES, joined, piece)
                out[base + UPDATES + r * PIX : base + UPDATES + (r + 1) * PIX, :] = joined
        if d == 0:
            copy = pltpu.make_async_copy(out, own_target, leaving)
            copy.start()
    copy.wait()


def sincos(x):
    n = jnp.floor(x * (2.0 / math.pi) + 0.5)
    r = x - n * 1.5703125
    r = r - n * 4.8351287841796875e-4
    r = r - n * 3.13855707645416259765625e-7
    r = r - n * 6.0771005065061922e-11
    q = n.astype(jnp.int32)
    z = r * r
    s = r + r * z * (-1.6666654611e-1 + z * (8.3321608736e-3 + z * -1.9515295891e-4))
    c = 1.0 - 0.5 * z + z * z * (4.166664568298827e-2 + z * (-1.388731625493765e-3 + z * 2.443315711809948e-5))
    swap = (q & 1) == 1
    sine = jnp.where(swap, c, s)
    cosine = jnp.where(swap, s, c)
    sine = jnp.where((q & 2) == 2, -sine, sine)
    cosine = jnp.where(((q + 1) & 2) == 2, -cosine, cosine)
    return sine, cosine


def sum_kernel(place, mine, new_0, new_1, new_2, new_3, keep, send, state, numbers, meta, arrived):
    lane = lane_index((40, LANES))
    side = place[0]
    for p in range(CHIPS):
        numbers[p] = mine[p, META : META + PIX, :].astype(jnp.int32)
    copy = pltpu.make_async_copy(numbers, meta, arrived)
    copy.start()

    def unpack(p, target, near, rest, q):
        count = near.shape[0]
        left = pltpu.roll(near, LANES - BEHIND, 1)
        right = pltpu.roll(rest, (LANES - BEHIND - REST_LANES * q) % LANES, 1)
        state[p, target : target + count, :] = near
        state[p, TILE + target : TILE + target + count, :] = jnp.where(
            lane_index(left.shape) < LANES - BEHIND, left, right
        )

    def begin(p, carry):
        for q in range(4):
            first = q * REST
            count = min(REST, WINDOW - first)
            unpack(p, first, mine[p, first : first + count, :], mine[p, WINDOW : WINDOW + count, :], q)
        return carry

    lax.fori_loop(0, CHIPS, begin, 0)
    for d, ref in enumerate((new_0, new_1, new_2, new_3)):
        for w in range(2):
            half = place[2] if w == 0 else 1 - place[2]
            p = half * 4 + ((place[1] + 4 - d) & 3)
            base = w * NEW_PAYLOAD
            for q in range(4):
                first = q * NEW_REST
                count = min(NEW_REST, UPDATES - first)
                near = ref[base + first : base + first + count, :]
                unpack(p, WINDOW + first, near, ref[base + UPDATES : base + UPDATES + count, :], q)
    copy.wait()

    def step(t, carry):
        for l in range(CHIPS):
            dst = pl.multiple_of(meta[l, 6, META_LANE + t], NEW_COLS)
            src = pl.multiple_of(WINDOW + t * NEW_COLS, NEW_COLS)
            for base in (0, TILE):
                state[l, pl.ds(base + dst, NEW_COLS), :] = state[l, pl.ds(base + src, NEW_COLS), :]
        acc = []
        for g in range(STARS):
            total = jnp.zeros((40, LANES), jnp.float32)
            for l in range(CHIPS):
                window = state[l, pl.ds(meta[l, g, META_LANE + t], 40), :]
                total = total + pltpu.roll(window, meta[l, g, TURN_LANE + t], 1)
            acc.append(total)
        for k in range(2):
            one, two, three = acc[3 * k : 3 * k + 3]
            near = jnp.where(lane < 40, one, jnp.where(lane < 80, pltpu.roll(two, 40, 1), pltpu.roll(three, 80, 1)))
            far = jnp.where(lane < 40, pltpu.roll(one, LANES - 40, 1), jnp.where(lane < 80, two, pltpu.roll(three, 40, 1)))
            keep[t, k * 40 : (k + 1) * 40, :] = jnp.where(side == 0, near, far)
            send[t, k * 40 : (k + 1) * 40, :] = jnp.where(side == 0, far, near)
        return carry

    lax.fori_loop(0, STEPS, step, 0, unroll=5)


def spot_kernel(flags, here, there, recon, keep, send, flat_out, sums, lane_tab, lane_rest):
    side = flags[0]
    sums[...] = jnp.zeros_like(sums)
    weights = [ahead(d) for d in range(1, 5)]
    lane_tab[...], lane_rest[...] = lane_table()

    def spots(t):
        sine, cosine = sincos(here[t] + there[t])
        c1, c2 = parts(cosine, 2)
        s1, s2 = parts(sine, 2)
        head = jnp.concatenate([c1, s1], axis=1)
        tail = jnp.concatenate([c2, s2], axis=1)
        first = jnp.dot(jnp.concatenate([head, tail]), lane_tab[...], preferred_element_type=jnp.float32)
        second = jnp.dot(c1, lane_rest[...], preferred_element_type=jnp.float32)
        along = first[:80] + first[80:]
        z_y = sine * (along[:, :LANES] + second) + cosine * along[:, LANES:]

        c3 = cosine.reshape(10, PIX, LANES)
        s3 = sine.reshape(10, PIX, LANES)
        by_sine = -8.0 * s3
        by_cosine = -8.0 * c3
        for d in range(1, 5):
            weight = weights[d - 1][None]
            even = -8.0 if d == 4 else 16.0 * (-1.0) ** (d + 1)
            c_d = pltpu.roll(c3, d, 1)
            s_d = pltpu.roll(s3, d, 1)
            by_sine = by_sine + (weight * c_d + even * s_d)
            by_cosine = by_cosine + (even * c_d - weight * s_d)
        z_x = jnp.sum(s3 * by_sine + c3 * by_cosine, axis=1)
        z_y = jnp.sum(z_y.reshape(10, PIX, LANES), axis=1)
        for unit in range(10):
            sums[unit, pl.ds(t, 1), :] = z_x[unit : unit + 1]
            sums[10 + unit, pl.ds(t, 1), :] = z_y[unit : unit + 1]

    def step(t, carry):
        spots(t)
        return carry

    lax.fori_loop(0, STEPS, step, 0, unroll=5)

    units = 20
    stacked = jnp.concatenate(parts(sums[...].reshape(units * 16, LANES), 3))
    got = jnp.dot(stacked, group_table(), preferred_element_type=jnp.float32)
    size = units * 16
    got = (got[:size] + got[size : 2 * size]) + got[2 * size :]
    tiles = [jnp.zeros((16, LANES), jnp.float32) for _ in range(3)]
    for unit in range(units):
        tiles[unit // 8] = tiles[unit // 8] + pltpu.roll(got[unit * 16 : (unit + 1) * 16], (unit % 8) * 16, 1)
    flat = jnp.zeros((16, FLAT_PAD), jnp.float32)
    for i in range(3):
        moved = jnp.dot(
            jnp.concatenate(parts(tiles[i], 3)), order_table(i), preferred_element_type=jnp.float32
        )
        flat = flat + ((moved[:16] + moved[16:32]) + moved[32:])
    shown = lit(flags)
    flat = flat * jnp.concatenate([shown, shown])
    flat_out[...] = flat
    rounded = flat[:, :FLAT].astype(jnp.bfloat16)
    for out, half in ((keep, side), (send, 1 - side)):
        out[...] = jnp.zeros_like(out)
        for i in range(HALF_TILES):
            column = pl.multiple_of((half * HALF_TILES + i) * LANES, LANES)
            part = jnp.dot(rounded, recon[:, pl.ds(column, LANES)], preferred_element_type=jnp.float32)
            for slab, row, first, count in pieces(i):
                out[slab, row : row + count, :] = part[first : first + count]


def pieces(i):
    found = []
    first = 0
    while first < STEPS:
        slab, row = divmod(i * STEPS + first, SLAB_USED)
        count = min(STEPS - first, SLAB_USED - row)
        found.append((slab, row, first, count))
        first += count
    return found


def finish_kernel(core, mine, other, out):
    for ref, half in ((mine, core[0]), (other, 1 - core[0])):
        for i in range(HALF_TILES):
            column = pl.multiple_of((half * HALF_TILES + i) * LANES, LANES)
            for slab, row, first, count in pieces(i):
                out[first : first + count, pl.ds(column, LANES)] = ref[slab, row : row + count, :]


def vmem():
    return pl.BlockSpec(memory_space=pltpu.VMEM)


def smem():
    return pl.BlockSpec(memory_space=pltpu.SMEM)


def pack(low, core, high, meta):
    return pl.pallas_call(
        pack_kernel,
        out_shape=jax.ShapeDtypeStruct((CHIPS, PAYLOAD, LANES), jnp.float32),
        in_specs=[vmem()] * 4,
        out_specs=vmem(),
        compiler_params=pltpu.CompilerParams(vmem_limit_bytes=16 << 20),
    )(low, core, high, meta)


def hand(place, own, partner):
    return pl.pallas_call(
        hand_kernel,
        out_shape=(jax.ShapeDtypeStruct((2 * NEW_PAYLOAD, LANES), jnp.float32),) * 4,
        in_specs=[smem(), vmem(), vmem()],
        out_specs=(pl.BlockSpec(memory_space=pl.ANY),) + (vmem(),) * 3,
        scratch_shapes=[pltpu.VMEM((2 * NEW_PAYLOAD, LANES), jnp.float32), pltpu.SemaphoreType.DMA(())],
        compiler_params=pltpu.CompilerParams(vmem_limit_bytes=8 << 20),
    )(place, own, partner)


def partial_phases(place, mine, news):
    half = jax.ShapeDtypeStruct((STEPS, 10 * PIX, LANES), jnp.float32)
    return pl.pallas_call(
        sum_kernel,
        out_shape=(half, half),
        in_specs=[smem()] + [vmem()] * 5,
        out_specs=(vmem(), vmem()),
        scratch_shapes=[
            pltpu.VMEM((CHIPS, 2 * TILE, LANES), jnp.float32),
            pltpu.VMEM((CHIPS, PIX, LANES), jnp.int32),
            pltpu.SMEM((CHIPS, PIX, LANES), jnp.int32),
            pltpu.SemaphoreType.DMA(()),
        ],
        compiler_params=pltpu.CompilerParams(vmem_limit_bytes=16 << 20),
    )(place, mine, *news)


def slopes_and_products(flags, here, there, recon):
    slab = jax.ShapeDtypeStruct((SLABS, SLAB_ROWS, LANES), jnp.float32)
    return pl.pallas_call(
        spot_kernel,
        out_shape=(slab, slab, jax.ShapeDtypeStruct((16, FLAT_PAD), jnp.float32)),
        in_specs=[smem()] + [vmem()] * 3,
        out_specs=(vmem(),) * 3,
        scratch_shapes=[
            pltpu.VMEM((20, 16, LANES), jnp.float32),
            pltpu.VMEM((2 * LANES, 2 * LANES), jnp.bfloat16),
            pltpu.VMEM((LANES, LANES), jnp.bfloat16),
        ],
        compiler_params=pltpu.CompilerParams(vmem_limit_bytes=16 << 20),
    )(flags, here, there, recon)


def finish(core, mine, other):
    return pl.pallas_call(
        finish_kernel,
        out_shape=jax.ShapeDtypeStruct((STEPS, ACTS), jnp.float32),
        in_specs=[smem(), vmem(), vmem()],
        out_specs=vmem(),
        compiler_params=pltpu.CompilerParams(vmem_limit_bytes=8 << 20),
    )(core, mine, other)


def groups_by(key):
    found = {}
    for device in range(256):
        layer, sub = divmod(device, 16)
        found.setdefault(key(layer // 8, layer // 2 % 4, layer % 2, sub // 4, sub % 4), []).append(device)
    return [found[name] for name in sorted(found)]


def exchange(blocks, groups):
    return lax.all_to_all(blocks, ("layer", "sub"), 0, 0, tiled=True, axis_index_groups=groups)


def to_all(block, groups):
    return exchange(jnp.broadcast_to(block[None], (len(groups[0]),) + block.shape), groups)


def to_other_core(block):
    return lax.ppermute(block, "layer", [(i, i ^ 1) for i in range(16)])


def local(screens, new_columns, col_block, shift_x, shift_y, valid, recon):
    owner = lax.axis_index("sub")
    count = lax.axis_size("sub")
    strips = jnp.transpose(screens[0], (0, 2, 1))
    fresh = jnp.transpose(new_columns[:, 0], (0, 2, 1))
    layer = lax.axis_index("layer").astype(jnp.int32)
    half = layer // 8

    def new_rows(part):
        at = LANE0 + part * (KEPT - HALF_LANES)
        return lax.dynamic_slice(fresh, (0, 0, at), (STEPS, NEW_COLS, HALF_LANES)).reshape(UPDATES, HALF_LANES)

    def strip(turn):
        return lax.dynamic_slice(strips, (turn, 0, LANE0), (1, 40, KEPT))[0]

    core = strip(PUP_TURN)
    forward = [(i, (i + 1) % count) for i in range(count)]
    backward = [(target, source) for source, target in forward]
    low = lax.ppermute(strip(jnp.where(owner == count - 1, PUP_TURN - 1, PUP_TURN)), "sub", forward)
    high = lax.ppermute(strip(jnp.where(owner == 0, PUP_TURN + 1, PUP_TURN)), "sub", backward)

    partner = lax.ppermute(new_rows(1 - half), "layer", [(i, i ^ 8) for i in range(16)])

    offset = jnp.transpose(shift_y[:, 0]) + HALO
    behind = (offset > LANES - CHIP_ROWS).astype(jnp.int32)
    start = jnp.transpose(shift_x[:, 0]) + HALO + behind * TILE
    turn = (LANES - offset + behind * BEHIND) % LANES
    block = jnp.transpose(col_block) - (PUP_TURN * PUP // NEW_COLS) - (owner * 5 - 5)
    block = jnp.where((block >= 0) & (block < WINDOW // NEW_COLS), block, COLS // NEW_COLS) * NEW_COLS
    meta = (
        jnp.pad(start, ((0, 2), (META_LANE, LANES - META_LANE - STEPS)))
        + jnp.pad(turn, ((0, 2), (TURN_LANE, LANES - TURN_LANE - STEPS)))
        + jnp.pad(block, ((6, 1), (META_LANE, LANES - META_LANE - STEPS)))
    ).astype(jnp.float32)

    side = (layer % 2).reshape(1)
    place = jnp.stack([layer % 2, layer // 2 % 4, half])
    flags = jnp.concatenate([side, valid.reshape(-1)])
    payload, partner, flags = lax.optimization_barrier((pack(low, core, high, meta), partner, flags))
    mine = exchange(payload, groups_by(lambda zh, x, c, y, zl: (c, y, zl)))
    news = list(hand(place, new_rows(half), partner))
    *news[1:], recon = lax.optimization_barrier((*news[1:], recon))
    for d in range(1, 4):
        along = [(i, i // 8 * 8 + (i % 8 + 2 * d) % 8) for i in range(16)]
        news[d] = lax.ppermute(news[d], "layer", along)
    matrix = jnp.transpose(recon, (0, 2, 3, 1, 4)).reshape(FLAT, ACTS)
    mine, matrix = lax.optimization_barrier((mine, matrix))
    here, there = partial_phases(place, mine, news)
    keep, send, flat = slopes_and_products(flags, here, to_other_core(there), matrix)

    plane = groups_by(lambda zh, x, c, y, zl: (c, zh, zl))
    column = groups_by(lambda zh, x, c, y, zl: (c, x, y))
    part = jnp.sum(exchange(keep + to_other_core(send), plane), axis=0)
    total = to_all(jnp.sum(to_all(part, column), axis=0), plane)
    commands = finish(side, total, to_other_core(total))
    slopes = jnp.transpose(flat[:STEPS, :FLAT].reshape(STEPS, STARS, 5, 5, 2), (0, 1, 4, 2, 3))
    return (slopes, commands)


def solution(mesh):
    return jax.shard_map(
        local,
        mesh=mesh,
        in_specs=(
            P("layer", None, None, "sub"),
            P(None, "layer", None, None),
            P(None, "layer"),
            P(None, "layer", None),
            P(None, "layer", None),
            P("layer", "sub"),
            P(None, None, "layer", "sub", None),
        ),
        out_specs=(P(None, None, None, "layer", "sub"), P()),
        check_vma=False,
    )
```
